32 devices in a mesh: fsdp: 8 (over z, x), ctx: 2 (over y), tp: 2 (over core).
Axes of the slice: x: 2, y: 2, z: 4, core: 2. Of those that a mesh axis runs over, the one named last changes fastest.
Arguments:
- prompt: bfloat16 [8, 1024, 768], P('fsdp', 'ctx'), may hold values from -6 to 6
- continuations: bfloat16 [8, 2, 256, 768], P('fsdp', 'ctx'), may hold values from -6 to 6
- prev_logits: bfloat16 [8, 2, 12, 256, 1280], P('fsdp', 'ctx', 'tp'), may hold values from -6 to 6
- cont_len: int32 [8, 2], P('fsdp', 'ctx'), may hold values from 1 to 256, 384 in all within a row
- query_weight: bfloat16 [768, 768], P('fsdp', 'tp'), may hold values from -0.21875 to 0.21875
- query_bias: bfloat16 [12, 64], P('tp', 'fsdp'), may hold values from -3 to 3
- key_weight: bfloat16 [768, 768], P('fsdp', 'tp'), may hold values from -0.21875 to 0.21875
- value_weight: bfloat16 [768, 768], P('fsdp', 'tp'), may hold values from -0.21875 to 0.21875
- value_bias: bfloat16 [12, 64], P('tp', 'fsdp'), may hold values from -3 to 3
- output_weight: bfloat16 [768, 768], P('tp', 'fsdp'), may hold values from -3.5 to 3.5
- output_bias: bfloat16 [768], P('fsdp'), may hold values from -3 to 3
- first_gain: bfloat16 [768], P('fsdp'), may hold values from 0.5 to 1.5
- first_shift: bfloat16 [768], P('fsdp'), may hold values from -3 to 3
- up_weight: bfloat16 [768, 3072], P('fsdp', 'tp'), may hold values from -0.21875 to 0.21875
- up_bias: bfloat16 [24, 128], P('tp', 'fsdp'), may hold values from -3 to 3
- down_weight: bfloat16 [3072, 768], P('tp', 'fsdp'), may hold values from -0.109375 to 0.109375
- down_bias: bfloat16 [768], P('fsdp'), may hold values from -3 to 3
- second_gain: bfloat16 [768], P('fsdp'), may hold values from 0.5 to 1.5
- second_shift: bfloat16 [768], P('fsdp'), may hold values from -3 to 3
- cot_prompt: bfloat16 [8, 1024, 768], P('fsdp', 'ctx'), may hold values from -6 to 6
- cot_conts: bfloat16 [8, 2, 256, 768], P('fsdp', 'ctx'), may hold values from -6 to 6
- cot_logits: bfloat16 [8, 2, 12, 256, 1280], P('fsdp', 'ctx', 'tp'), may hold values from -0.29882812 to 0.29882812
Outputs:
- prompt_out: bfloat16 [8, 1024, 768], P('fsdp', 'ctx')
- conts_out: bfloat16 [8, 2, 256, 768], P('fsdp', 'ctx')
- new_logits: bfloat16 [8, 2, 12, 256, 1280], P('fsdp', 'ctx', 'tp')
- grad_prompt: float32 [8, 1024, 768], P('fsdp', 'ctx')
- grad_conts: float32 [8, 2, 256, 768], P('fsdp', 'ctx')
- grad_prev: bfloat16 [8, 2, 12, 256, 1280], P('fsdp', 'ctx', 'tp')
- query_weight_grad: float32 [768, 768], P('fsdp', 'tp')
- query_bias_grad: float32 [12, 64], P('tp', 'fsdp')
- key_weight_grad: float32 [768, 768], P('fsdp', 'tp')
- value_weight_grad: float32 [768, 768], P('fsdp', 'tp')
- value_bias_grad: float32 [12, 64], P('tp', 'fsdp')
- output_weight_grad: float32 [768, 768], P('tp', 'fsdp')
- output_bias_grad: float32 [768], P('fsdp')
- first_gain_grad: float32 [768], P('fsdp')
- first_shift_grad: float32 [768], P('fsdp')
- up_weight_grad: float32 [768, 3072], P('fsdp', 'tp')
- up_bias_grad: float32 [24, 128], P('tp', 'fsdp')
- down_weight_grad: float32 [3072, 768], P('tp', 'fsdp')
- down_bias_grad: float32 [768], P('fsdp')
- second_gain_grad: float32 [768], P('fsdp')
- second_shift_grad: float32 [768], P('fsdp')
The draws below stay inside these ranges and needn't reach their ends.
Inputs may be any that keep to these rules, and one draw needn't show every extreme that they name: `cont_len`: A group's lengths sum to 384.
All inputs are finite; a program needn't handle non-finite values.
Results may differ from the reference program's by a relative error of at most 0.02.
Values may be sent and summed in bfloat16 or wider, within the bound.
No kernel may reach another device: no remote copies, remote signals or barrier semaphores. Data moves between devices by JAX's collectives and lax.ppermute only.
A program may use at most 192 MiB of HBM per device.

```python
import math
import jax
import jax.numpy as jnp
import numpy as np
from jax import lax

D = 768
HEADS = 12
HEAD_DIM = 64
FF = 3072
CLEN = 256
PROMPT = 1024
CONTS = 2
GROUPS = 8


def strengthened(values, own_key, source, target, shards_of, factor):
    def block_of(axis_at):
        return (jnp.arange(values.shape[axis_at]) // (values.shape[axis_at] // shards_of)).reshape((-1,) + (1,) * (values.ndim - 1 - axis_at))

    first = jax.random.permutation(own_key, shards_of)[block_of(target)]
    far = (block_of(target) + shards_of // 2) % shards_of
    return jnp.where((block_of(source) == first) | (block_of(source) == far), factor * values, values)


def levels(stream_key, shape, pieces, least, largest):
    level, own = 1.0, jax.random.fold_in(stream_key, 6)
    for axis_at, blocks in pieces:
        steps = jnp.exp(jax.random.uniform(jax.random.fold_in(own, axis_at), (blocks,), jnp.float32, least / len(pieces), largest / len(pieces)))
        level = level * jnp.repeat(steps, shape[axis_at] // blocks).reshape([-1 if axis == axis_at else 1 for axis in range(len(shape))])
    return level


def length_profile(count, total, limit, lean):
    weights = [(1 << 20) // math.isqrt(grade ** lean) + 1 for grade in range(2, count + 1)]
    rest, holding = total - limit - (count - 1), [1] * (count - 1)
    while rest > 0:
        free = [i for i in range(count - 1) if holding[i] < limit]
        pool, budget = sum([weights[i] for i in free]), rest
        for i in free:
            addition = min(limit - holding[i], max(1, budget * weights[i] // pool), rest)
            holding[i] = holding[i] + addition
            rest = rest - addition
    return np.array([limit] + holding)


def ragged_sizes(stream_key, amount, total, bound, slope):
    if amount == 2:
        one = jax.random.randint(stream_key, (), max(1, total - bound), min(bound, total - 1) + 1)
        return jnp.stack([one, total - one])
    sizes = jnp.asarray(length_profile(amount, total, bound, slope), jnp.int32)
    pairs = (amount - 1) // 2
    giver, sink = sizes[1:1 + 2 * pairs:2], sizes[2:2 + 2 * pairs:2]
    margin = jnp.minimum(giver - 1, bound - sink)
    passed = jax.random.randint(jax.random.fold_in(stream_key, 1), (pairs,), 0, 1 << 20) % (margin + 1)
    sizes = sizes.at[1:1 + 2 * pairs:2].set(giver - passed).at[2:2 + 2 * pairs:2].set(sink + passed)
    return sizes[jax.random.permutation(jax.random.fold_in(stream_key, 2), amount)]


def normal_values(key, extent, scale, bound, cuts=(), held_as=jnp.bfloat16):
    drawn = scale * jax.random.normal(key, extent, jnp.float32)
    if cuts:
        drawn = drawn * levels(key, extent, cuts, -0.22, 0.18)
    return jnp.clip(drawn, -bound, bound).astype(held_as)


def heavy_noise(rng, extent, scale, limit, pieces, heavy, held_as=jnp.bfloat16):
    entries = scale * jax.random.normal(rng, extent, jnp.float32)
    if pieces:
        entries = entries * levels(rng, extent, pieces, -0.22, 0.18)
    return jnp.clip(strengthened(entries, jax.random.fold_in(rng, 3), *heavy), -limit, limit).astype(held_as)


def setup_inputs(seed: int = 0) -> dict:
    key_of = jax.random.split(jax.random.key(seed), 23)
    return {
        "prompt": normal_values(key_of[0], (GROUPS, PROMPT, D), 1.0, 6.0, ((0, 8), (1, 2))),
        "continuations": normal_values(key_of[1], (GROUPS, CONTS, CLEN, D), 1.0, 6.0, ((0, 8), (1, 2))),
        "prev_logits": normal_values(key_of[2], (GROUPS, CONTS, HEADS, CLEN, PROMPT + CLEN), 1.0, 6.0, ((0, 8), (1, 2), (2, 2))),
        "cont_len": jax.vmap(lambda own: ragged_sizes(own, CONTS, CONTS * CLEN * 3 // 4, CLEN, 0))(jax.random.split(key_of[3], GROUPS)).reshape((GROUPS, CONTS)).astype(jnp.int32),
        "query_weight": normal_values(key_of[4], (D, D), D ** -0.5, 0.21875, ((0, 8), (1, 2))),
        "query_bias": normal_values(key_of[5], (HEADS, HEAD_DIM), 0.5, 3.0, ((0, 2), (1, 8))),
        "key_weight": normal_values(key_of[6], (D, D), D ** -0.5, 0.21875, ((0, 8), (1, 2))),
        "value_weight": normal_values(key_of[7], (D, D), D ** -0.5, 0.21875, ((0, 8), (1, 2))),
        "value_bias": normal_values(key_of[8], (HEADS, HEAD_DIM), 0.5, 3.0, ((0, 2), (1, 8))),
        "output_weight": normal_values(key_of[9], (D, D), (max(1, D // 256)) ** -0.5, 3.5, ((0, 2), (1, 8))),
        "output_bias": normal_values(key_of[10], (D,), 0.5, 3.0, ((0, 8),)),
        "first_gain": jnp.clip(1.0 + 0.1 * jax.random.normal(key_of[11], (D,), jnp.float32), 0.5, 1.5).astype(jnp.bfloat16),
        "first_shift": normal_values(key_of[12], (D,), 0.5, 3.0, ((0, 8),)),
        "up_weight": normal_values(key_of[13], (D, FF), D ** -0.5, 0.21875, ((0, 8), (1, 2))),
        "up_bias": normal_values(key_of[14], (FF // 128, 128), 0.5, 3.0, ((0, 2), (1, 8))),
        "down_weight": normal_values(key_of[15], (FF, D), FF ** -0.5, 0.109375, ((0, 2), (1, 8))),
        "down_bias": normal_values(key_of[16], (D,), 0.5, 3.0, ((0, 8),)),
        "second_gain": jnp.clip(1.0 + 0.1 * jax.random.normal(key_of[17], (D,), jnp.float32), 0.5, 1.5).astype(jnp.bfloat16),
        "second_shift": normal_values(key_of[18], (D,), 0.5, 3.0, ((0, 8),)),
        "cot_prompt": heavy_noise(key_of[19], (GROUPS, PROMPT, D), 1.0, 6.0, ((0, 8), (1, 2)), (0, 2, 8, 2.0)),
        "cot_conts": normal_values(key_of[20], (GROUPS, CONTS, CLEN, D), 1.0, 6.0, ((0, 8), (1, 2))),
        "cot_logits": normal_values(key_of[21], (GROUPS, CONTS, HEADS, CLEN, PROMPT + CLEN), 0.05, 0.29882812, ((0, 8), (1, 2), (2, 2))),
    }


@jax.custom_vjp
def low(v):
    return lax.optimization_barrier(v.astype(jnp.bfloat16)).astype(jnp.float32)

@jax.custom_vjp
def low_back(v):
    return v

def low_keep(v):
    return (low(v), None)

def low_pass(kept, grad):
    return (grad,)

def back_keep(v):
    return (v, None)

def back_low(kept, grad):
    return (low(grad),)
low.defvjp(low_keep, low_pass)
low_back.defvjp(back_keep, back_low)
highest = lax.Precision.HIGHEST
epsilon = 1e-06

def both_ways(tensor):
    return low_back(low(tensor))

def matmul(left_mat, right_mat):
    return jnp.dot(left_mat, right_mat, precision=highest, preferred_element_type=jnp.float32)

def norm_rows(hidden_in, gain_full, shift_full):
    centre = lax.optimization_barrier(jnp.mean(hidden_in, axis=-1, keepdims=True))
    shifted = hidden_in - centre
    spread = lax.optimization_barrier(jnp.mean(shifted * shifted, axis=-1, keepdims=True))
    return shifted * lax.rsqrt(spread + epsilon) * gain_full + shift_full

def block_forward(param_set, prompt_rows, cont_rows, prev_rows, lengths):
    query_weight, query_bias, key_weight, value_weight, value_bias, output_weight, output_bias, first_gain, first_shift, up_weight, up_bias, down_weight, down_bias, second_gain, second_shift = param_set
    cont_count, cont_size, model_width = cont_rows.shape
    prompt_len = prompt_rows.shape[0]
    head_count = query_bias.shape[0]
    head_size = query_bias.shape[1]
    scale = 1.0 / math.sqrt(head_size)
    stacked = jnp.concatenate([prompt_rows, cont_rows.reshape(cont_count * cont_size, model_width)], 0)
    total_rows = stacked.shape[0]
    queries = both_ways(matmul(stacked, query_weight) + query_bias.reshape(-1)).reshape(total_rows, head_count, head_size)
    key_rows = both_ways(matmul(stacked, key_weight)).reshape(total_rows, head_count, head_size)
    value_rows = both_ways(matmul(stacked, value_weight) + value_bias.reshape(-1)).reshape(total_rows, head_count, head_size)
    query_prompt = queries[:prompt_len]
    key_prompt = key_rows[:prompt_len]
    value_prompt = value_rows[:prompt_len]
    scores_prompt = low_back(jnp.einsum('qhd,khd->hqk', query_prompt, key_prompt, precision=highest) * scale)
    probs_prompt = low(jax.nn.softmax(scores_prompt, axis=-1))
    out_prompt = jnp.einsum('hqk,khd->qhd', probs_prompt, value_prompt, precision=highest)
    query_cont = queries[prompt_len:].reshape(cont_count, cont_size, head_count, head_size)
    key_cont = key_rows[prompt_len:].reshape(cont_count, cont_size, head_count, head_size)
    value_cont = value_rows[prompt_len:].reshape(cont_count, cont_size, head_count, head_size)
    key_all = jnp.concatenate([jnp.broadcast_to(key_prompt[None], (cont_count,) + key_prompt.shape), key_cont], 1)
    value_all = jnp.concatenate([jnp.broadcast_to(value_prompt[None], (cont_count,) + value_prompt.shape), value_cont], 1)
    raw_scores = low_back(prev_rows + jnp.einsum('cqhd,ckhd->chqk', query_cont, key_all, precision=highest) * scale)
    column = jnp.arange(prompt_len + cont_size, dtype=jnp.int32)
    live_cols = (column[None, :] < prompt_len) | (column[None, :] - prompt_len < lengths.astype(jnp.int32)[:, None])
    masked = jnp.where(live_cols[:, None, None, :], raw_scores, -1e+30)
    probs_cont = low(jax.nn.softmax(masked, axis=-1))
    out_cont = jnp.einsum('chqk,ckhd->cqhd', probs_cont, value_all, precision=highest)
    attended = both_ways(jnp.concatenate([out_prompt.reshape(prompt_len, model_width), out_cont.reshape(cont_count * cont_size, model_width)], 0))
    branch = low_back(matmul(attended, output_weight) + output_bias)
    first_out = norm_rows(stacked + branch, first_gain, first_shift)
    inner_act = low_back(matmul(low(first_out), up_weight) + up_bias.reshape(-1))
    hidden = low(jax.nn.gelu(inner_act, approximate=False))
    second = low_back(matmul(hidden, down_weight) + down_bias)
    result = norm_rows(first_out + second, second_gain, second_shift)
    return (result, raw_scores)

def reference(prompt, continuations, prev_logits, cont_len, query_weight, query_bias, key_weight, value_weight, value_bias, output_weight, output_bias, first_gain, first_shift, up_weight, up_bias, down_weight, down_bias, second_gain, second_shift, cot_prompt, cot_conts, cot_logits):
    params = tuple((weight_in.astype(jnp.float32) for weight_in in (query_weight, query_bias, key_weight, value_weight, value_bias, output_weight, output_bias, first_gain, first_shift, up_weight, up_bias, down_weight, down_bias, second_gain, second_shift)))

    def one_group(grad_sums, group_items):
        prompt_rows, cont_rows, prev_rows, lengths, cot_rows_p, cot_rows_c, cot_rows_l = group_items
        prompt_len = prompt_rows.shape[0]

        def forward(param_set, prompt_in, cont_in, prev_in):
            return block_forward(param_set, prompt_in, cont_in, prev_in, lengths)
        (result, raw_scores), pullback = jax.vjp(forward, params, prompt_rows.astype(jnp.float32), cont_rows.astype(jnp.float32), prev_rows.astype(jnp.float32))
        upstream = jnp.concatenate([cot_rows_p, cot_rows_c.reshape(-1, cot_rows_c.shape[-1])], 0).astype(jnp.float32)
        group_grads, grad_prompt, grad_conts, grad_prev = pullback((upstream, cot_rows_l.astype(jnp.float32)))
        grad_sums = jax.tree.map(lambda sum_now, addend: sum_now + addend, grad_sums, group_grads)
        outputs = (result[:prompt_len].astype(jnp.bfloat16), result[prompt_len:].reshape(cont_rows.shape).astype(jnp.bfloat16), raw_scores.astype(jnp.bfloat16), grad_prompt, grad_conts, grad_prev.astype(jnp.bfloat16))
        return (grad_sums, outputs)
    zero_grads = tuple((jnp.zeros(param.shape, jnp.float32) for param in params))
    grad_sums, group_outs = lax.scan(one_group, zero_grads, (prompt, continuations, prev_logits, cont_len, cot_prompt, cot_conts, cot_logits))
    return (group_outs[0], group_outs[1], group_outs[2], group_outs[3], group_outs[4], group_outs[5], grad_sums[0], grad_sums[1], grad_sums[2], grad_sums[3], grad_sums[4], grad_sums[5], grad_sums[6], grad_sums[7], grad_sums[8], grad_sums[9], grad_sums[10], grad_sums[11], grad_sums[12], grad_sums[13], grad_sums[14])
```

```python
import math

import jax
import jax.numpy as jnp
from jax import lax
from jax.experimental import pallas as pl
from jax.experimental.pallas import tpu as pltpu
from jax.sharding import PartitionSpec as P

epsilon = 1e-06
f32 = jnp.float32
bf16 = jnp.bfloat16
LANES = 128


def product(left_mat, right_mat):
    return jnp.dot(left_mat, right_mat, preferred_element_type=f32)


def contract_rows(left_mat, right_mat):
    return lax.dot_general(
        left_mat, right_mat, (((0,), (0,)), ((), ())), preferred_element_type=f32
    )


def contract_cols(left_mat, right_mat):
    return lax.dot_general(
        left_mat, right_mat, (((1,), (1,)), ((), ())), preferred_element_type=f32
    )


class Grid:
    def __init__(self, sizes):
        self.fsdp, self.ctx, self.tp = sizes
        self.staged = sizes == (8, 2, 2)
        place = lax.axis_index("fsdp")
        self.outer, self.inner = place // 2, place % 2
        self.row = lax.axis_index("ctx")
        self.core = lax.axis_index("tp")
        self.place = jnp.stack([self.outer, self.inner, self.row]).astype(jnp.int32)

    def over_inner(self, array):
        return lax.ppermute(array, "fsdp", [(i, i ^ 1) for i in range(8)])

    def over_outer(self, array, step):
        return lax.ppermute(array, "fsdp", [(i, i ^ (2 * step)) for i in range(8)])

    def over_ctx(self, array):
        return lax.ppermute(array, "ctx", [(0, 1), (1, 0)])

    def over_tp(self, array):
        return lax.ppermute(array, "tp", [(0, 1), (1, 0)])

    def tp_sum(self, partial):
        low = partial.astype(bf16)
        return low.astype(f32) + self.over_tp(low).astype(f32)


def assemble(place, cuts, own, across, along, far_one, far_two):
    half = own.shape[1]
    edges = [sum(cuts[:i]) for i in range(len(cuts) + 1)]

    def body(place_ref, own_ref, across_ref, along_ref, one_ref, two_ref, *outs):
        outer, inner, row = place_ref[0], place_ref[1], place_ref[2]

        def put(piece, at_piece, step, swap_inner, swap_row):
            at = ((outer ^ step) * 2 + (inner ^ swap_inner)) * 2 + (row ^ swap_row)
            here = pl.ds(pl.multiple_of(at * half, 16), half)
            for out, low, high in zip(outs, edges, edges[1:]):
                out[here, :] = piece[at_piece, :, low:high]

        for step in range(4):
            put(own_ref, step, step, 0, 0)
            put(across_ref, step, step, 1, 0)
            put(along_ref, step, step, 0, 1)
            put(one_ref if step < 2 else two_ref, step % 2, step, 1, 1)

    vmem = pl.BlockSpec(memory_space=pltpu.VMEM)
    outs = [like((16 * half, cols), own.dtype) for cols in cuts]
    return pl.pallas_call(
        body,
        out_shape=outs,
        in_specs=[pl.BlockSpec(memory_space=pltpu.SMEM)] + [vmem] * 5,
        out_specs=[vmem] * len(outs),
        compiler_params=pltpu.CompilerParams(vmem_limit_bytes=VMEM_LIMIT),
        cost_estimate=cost(0, *outs, *outs),
        name="assemble",
    )(place, own, across, along, far_one, far_two)


def gather_rows(grid, early, late):
    cuts = [[a.shape[1] for a in arrays] for arrays in (early, late)]
    if not grid.staged:
        return [[lax.all_gather(a, "fsdp", axis=0, tiled=True) for a in arrays] for arrays in (early, late)]
    early, late = [jnp.concatenate(arrays, 1) for arrays in (early, late)]
    half = early.shape[0] // 2

    def lines(mine):
        return [grid.over_outer(mine, step) for step in (1, 2, 3)]

    def pairs(own):
        return grid.over_inner(own), grid.over_ctx(own)

    def corners(across, along):
        return grid.over_ctx(across[:2]), grid.over_inner(along[2:])

    mine, late_mine = [
        lax.dynamic_slice_in_dim(a, grid.row * half, half, 0) for a in (early, late)
    ]
    came = lines(mine)
    came, late_mine = lax.optimization_barrier((came, late_mine))
    own = jnp.stack([mine] + came)
    across, along = pairs(own)
    far = corners(across, along)
    late_came = lines(late_mine)
    far, late_came = lax.optimization_barrier((far, late_came))
    late_own = jnp.stack([late_mine] + late_came)
    late_pairs = pairs(late_own)
    late_far = corners(*late_pairs)
    return (
        assemble(grid.place, cuts[0], own, across, along, *far),
        assemble(grid.place, cuts[1], late_own, *late_pairs, *late_far),
    )


def pick(array, at, axis):
    return lax.dynamic_index_in_dim(array, at, axis, keepdims=False)


def add_low(left, right):
    return (left.astype(f32) + right.astype(f32)).astype(bf16)


VMEM_LIMIT = 60 * 1024 * 1024


def whole_block(array):
    rank = array.ndim
    return pl.BlockSpec(array.shape, lambda *_: (0,) * rank)


def cost(flops, *arrays, transcendentals=0):
    moved = sum(math.prod(a.shape) * jnp.dtype(a.dtype).itemsize for a in arrays)
    return pl.CostEstimate(
        flops=int(flops), transcendentals=int(transcendentals), bytes_accessed=int(moved)
    )


def like(shape, dtype):
    return jax.ShapeDtypeStruct(shape, dtype)


def norm_rows(hidden_in):
    centre = jnp.mean(hidden_in, axis=-1, keepdims=True)
    shifted = hidden_in - centre
    spread = jnp.mean(shifted * shifted, axis=-1, keepdims=True)
    inverse = lax.rsqrt(spread + epsilon)
    return shifted * inverse, inverse


def norm_pull(upstream, normed, inverse, gain):
    scaled = upstream * gain
    mean_one = jnp.mean(scaled, axis=-1, keepdims=True)
    mean_two = jnp.mean(scaled * normed, axis=-1, keepdims=True)
    return inverse * (scaled - mean_one - normed * mean_two)


def column_sums(values):
    return jnp.sum(values, axis=0, keepdims=True)


def row_tile(rows):
    return 256 if rows % 256 == 0 else rows


def ffn_forward(inputs, part, other, output_add, gain, shift, up_mat, up_add, down_turned):
    rows, width = inputs.shape
    hidden = up_mat.shape[1]
    tile = row_tile(rows)

    def body(x, p, o, b, g, s, up, ub, dn, norm_out, inv_out, act_out, slope_out, part_out):
        hidden_in = x[...].astype(f32) + (p[...].astype(f32) + o[...].astype(f32)) + b[...]
        normed, inverse = norm_rows(hidden_in)
        norm_out[...] = normed
        inv_out[...] = jnp.broadcast_to(inverse, inv_out.shape)
        low = (normed * g[...] + s[...]).astype(bf16)
        inner = product(low, up[...]) + ub[...]
        normal_cdf = 0.5 * (1.0 + lax.erf(inner * math.sqrt(0.5)))
        act = (inner * normal_cdf).astype(bf16)
        act_out[...] = act
        density = jnp.exp(-0.5 * inner * inner) * (1.0 / math.sqrt(2.0 * math.pi))
        slope_out[...] = (normal_cdf + inner * density).astype(bf16)
        part_out[...] = contract_cols(act, dn[...]).astype(bf16)

    outs = [
        like((rows, width), f32),
        like((rows, LANES), f32),
        like((rows, hidden), bf16),
        like((rows, hidden), bf16),
        like((rows, width), bf16),
    ]

    def tiled(array):
        return pl.BlockSpec((tile, array.shape[1]), lambda i: (i, 0))

    args = [inputs, part, other, output_add, gain, shift, up_mat, up_add, down_turned]
    return pl.pallas_call(
        body,
        grid=(rows // tile,),
        out_shape=outs,
        in_specs=[tiled(a) for a in args[:3]] + [whole_block(a) for a in args[3:]],
        out_specs=[tiled(a) for a in outs],
        compiler_params=pltpu.CompilerParams(vmem_limit_bytes=VMEM_LIMIT),
        cost_estimate=cost(4 * rows * width * hidden, *args, *outs, transcendentals=2 * rows * hidden),
        name="ffn_forward",
    )(*args)


def split_out(grid, length, cols):
    if grid.staged:
        return [like((length // 2, cols), bf16), like((length // 2, cols), bf16)]
    return [like((length, cols), bf16)]


def store_split(grid, place, full_ref, outs, over_inner):
    if not grid.staged:
        outs[0][...] = full_ref[...]
        return
    half = full_ref.shape[0] // 16
    for out, flip in zip(outs, (0, 1)):
        if over_inner:
            for outer in range(4):
                at = pl.multiple_of((2 * outer + (place[1] ^ flip)) * (2 * half), 32)
                out[2 * half * outer : 2 * half * (outer + 1), :] = full_ref[pl.ds(at, 2 * half), :]
        else:
            for block in range(8):
                at = pl.multiple_of((2 * block + (place[2] ^ flip)) * half, 16)
                out[half * block : half * (block + 1), :] = full_ref[pl.ds(at, half), :]


def ffn_backward(grid, norm1, gain1, shift1, part, other, down_add, gain2, shift2, cots, act, slope, up_mat, down_turned):
    rows, width = norm1.shape
    hidden = up_mat.shape[1]
    tile = 256
    chunk = row_tile(rows)
    prompt_len = cots[0].shape[0]
    count = 2 if grid.staged else 1

    def body(place, n1, g1, s1, p, o, db, g2, s2, cp, cc, u, sl, up, dn, *rest):
        outs, scratch = rest[:-6], rest[-6:]
        y_p, y_c, dh2, dx1, sums, up_sum = outs[:6]
        up_outs, down_outs = outs[6 : 6 + count], outs[6 + count :]
        df, x1_t, df_t, acc, full_up, full_down = scratch
        step = pl.program_id(0)

        @pl.when(step == 0)
        def _():
            total = [jnp.zeros((1, width), f32) for _ in range(3)]
            for at in range(0, rows, chunk):
                here = slice(at, at + chunk)
                first = n1[here, :] * g1[...] + s1[...]
                second = first + (p[here, :].astype(f32) + o[here, :].astype(f32)) + db[...]
                normed, inverse = norm_rows(second)
                result = (normed * g2[...] + s2[...]).astype(bf16)
                if at < prompt_len:
                    y_p[here, :] = result
                    cot = cp[here, :].astype(f32)
                else:
                    there = slice(at - prompt_len, at - prompt_len + chunk)
                    y_c[there, :] = result
                    cot = cc[there, :].astype(f32)
                grad = norm_pull(cot, normed, inverse, g2[...])
                dh2[here, :] = grad
                low = grad.astype(bf16)
                df[here, :] = low
                wide = low.astype(f32)
                df_t[:, here] = wide.T.astype(bf16)
                x1_t[:, here] = first.T.astype(bf16)
                total[0] += column_sums(cot * normed)
                total[1] += column_sums(cot)
                total[2] += column_sums(wide)
            sums[...] = jnp.zeros(sums.shape, f32)
            for i in range(3):
                sums[i : i + 1, :] = total[i]
            acc[...] = jnp.zeros_like(acc)

        inner = (product(df[...], dn[...]) * sl[...].astype(f32)).astype(bf16)
        up_sum[...] = jnp.broadcast_to(column_sums(inner.astype(f32)), up_sum.shape)
        full_up[...] = product(x1_t[...], inner).astype(bf16)
        full_down[...] = product(df_t[...], u[...]).astype(bf16)
        acc[...] += contract_cols(inner, up[...])
        store_split(grid, place, full_up, up_outs, True)
        store_split(grid, place, full_down, down_outs, False)

        @pl.when(step == hidden // tile - 1)
        def _():
            dx1[...] = acc[...].astype(bf16)

    def tiled(array):
        return pl.BlockSpec((array.shape[0], tile), lambda j: (0, j))

    fixed = [norm1, gain1, shift1, part, other, down_add, gain2, shift2, *cots]
    moving = [act, slope, up_mat, down_turned]
    outs = [
        like((prompt_len, width), bf16),
        like((rows - prompt_len, width), bf16),
        like((rows, width), f32),
        like((rows, width), bf16),
        like((8, width), f32),
        like((8, hidden), f32),
    ]
    grads = split_out(grid, width, hidden) * 2
    return pl.pallas_call(
        body,
        grid=(hidden // tile,),
        out_shape=outs + grads,
        in_specs=[pl.BlockSpec(memory_space=pltpu.SMEM)]
        + [whole_block(a) for a in fixed]
        + [tiled(a) for a in moving],
        out_specs=[whole_block(a) for a in outs[:5]] + [tiled(a) for a in outs[5:] + grads],
        scratch_shapes=[
            pltpu.VMEM((rows, width), bf16),
            pltpu.VMEM((width, rows), bf16),
            pltpu.VMEM((width, rows), bf16),
            pltpu.VMEM((rows, width), f32),
            pltpu.VMEM((width, tile), bf16),
            pltpu.VMEM((width, tile), bf16),
        ],
        compiler_params=pltpu.CompilerParams(vmem_limit_bytes=VMEM_LIMIT),
        cost_estimate=cost(8 * rows * width * hidden, *fixed, *moving, *outs, *grads),
        name="ffn_backward",
    )(grid.place, *fixed, *moving)


def fold_pair(grid, first, second):
    half = first[0].shape[0] // 8
    outs = []
    for kept, _ in (first, second):
        outs += [like((4 * half, kept.shape[1]), bf16)] * 2

    def body(place, fk, fa, sk, sa, f_keep, f_send, s_keep, s_send):
        for kept, came, keep, send, mine in (
            (fk, fa, f_keep, f_send, place[2]),
            (sk, sa, s_keep, s_send, place[1]),
        ):
            for out, flip in ((send, 1), (keep, 0)):
                at = pl.multiple_of((mine ^ flip) * half, 16)
                here = pl.ds(at, half)
                out[...] = (kept[here, :].astype(f32) + came[here, :].astype(f32)).astype(bf16)

    args = [*first, *second]
    return pl.pallas_call(
        body,
        grid=(4,),
        out_shape=outs,
        in_specs=[pl.BlockSpec(memory_space=pltpu.SMEM)]
        + [pl.BlockSpec((2 * half, a.shape[1]), lambda i: (i, 0)) for a in args],
        out_specs=[pl.BlockSpec((half, a.shape[1]), lambda i: (i, 0)) for a in outs],
        cost_estimate=cost(0, *args, *outs),
        name="fold_pair",
    )(grid.place, *args)


def fold_line(grid, first, second):
    half = first[0].shape[0] // 4
    left, right = first[0].shape[1], second[0].shape[1]
    outs = [like((half, left + right), f32)] + [like((half, left + right), bf16)] * 3

    def body(place, fk, fa, sk, sa, *out_refs):
        for step, out in enumerate(out_refs):
            here = pl.ds(pl.multiple_of((place[0] ^ step) * half, 16), half)
            out[:, :left] = (fk[here, :].astype(f32) + fa[here, :].astype(f32)).astype(out.dtype)
            out[:, left:] = (sk[here, :].astype(f32) + sa[here, :].astype(f32)).astype(out.dtype)

    vmem = pl.BlockSpec(memory_space=pltpu.VMEM)
    args = [*first, *second]
    return pl.pallas_call(
        body,
        out_shape=outs,
        in_specs=[pl.BlockSpec(memory_space=pltpu.SMEM)] + [vmem] * 4,
        out_specs=[vmem] * 4,
        cost_estimate=cost(0, *args, *outs),
        name="fold_line",
    )(grid.place, *args)


def scatter_split(grid, first, second):
    if not grid.staged:
        both = jnp.concatenate([first[0], second[0]], 1)
        both = lax.psum_scatter(both, "fsdp", scatter_dimension=0, tiled=True)
        return lax.psum(both, "ctx")
    came_first = grid.over_inner(first[1])
    came_second = grid.over_ctx(second[1])
    f_keep, f_send, s_keep, s_send = fold_pair(grid, (first[0], came_first), (second[0], came_second))
    came_first = grid.over_ctx(f_send)
    came_second = grid.over_inner(s_send)
    total, *sent = fold_line(grid, (f_keep, came_first), (s_keep, came_second))
    for step in (1, 2, 3):
        total = total + grid.over_outer(sent[step - 1], step).astype(f32)
    total = total.astype(bf16)
    other = grid.over_ctx(total)
    low = jnp.where(grid.row == 0, total, other)
    high = jnp.where(grid.row == 0, other, total)
    return jnp.concatenate([low, high], 0)


def head_lanes(shape, index):
    lane = lax.broadcasted_iota(jnp.int32, shape, 1)
    return (lane < LANES // 2) if index == 0 else (lane >= LANES // 2)


def attention_forward(queries, keys, values, prev_logits, cont_len, prompt_len):
    rows, width = queries.shape
    total = keys.shape[0]
    cont_size = rows - prompt_len
    full_len = total - cont_size
    heads = prev_logits.shape[0]
    chunk = row_tile(prompt_len)

    def body(length, q, k, v, prev, logits, probs_p, probs_c, out):
        def soft(scores):
            weights = jnp.exp(scores - jnp.max(scores, axis=-1, keepdims=True))
            return (weights * (1.0 / jnp.sum(weights, axis=-1, keepdims=True))).astype(bf16)

        column = lax.broadcasted_iota(jnp.int32, (1, total), 1)
        live = column < full_len + length[0, 0]
        for at in range(0, rows, chunk):
            here = slice(at, at + chunk)
            halves = []
            for head in range(2):
                one = jnp.where(head_lanes((chunk, LANES), head), q[here, :], 0)
                if at < prompt_len:
                    probs = soft(contract_cols(one, k[:full_len, :]))
                    probs_p[head, here, :] = probs
                    halves.append(product(probs, v[:full_len, :]))
                else:
                    there = slice(at - prompt_len, at - prompt_len + chunk)
                    raw = prev[head, there, :].astype(f32) + contract_cols(one, k[...])
                    logits[head, there, :] = raw.astype(bf16)
                    probs = soft(jnp.where(live, raw, -1e30))
                    probs_c[head, there, :] = probs
                    halves.append(product(probs, v[...]))
            first = head_lanes((chunk, LANES), 0)
            out[here, :] = jnp.where(first, halves[0], halves[1]).astype(bf16)

    outs = [
        like((heads, cont_size, total), bf16),
        like((heads, prompt_len, full_len), bf16),
        like((heads, cont_size, total), bf16),
        like((rows, width), bf16),
    ]

    def columns(array):
        return pl.BlockSpec((array.shape[0], LANES), lambda i: (0, i))

    def pairs(array):
        return pl.BlockSpec((2,) + array.shape[1:], lambda i: (i, 0, 0))

    args = [queries, keys, values, prev_logits]
    scores = heads * (prompt_len * full_len + cont_size * total)
    return pl.pallas_call(
        body,
        grid=(heads // 2,),
        out_shape=outs,
        in_specs=[pl.BlockSpec(memory_space=pltpu.SMEM)]
        + [columns(a) for a in args[:3]]
        + [pairs(prev_logits)],
        out_specs=[pairs(a) for a in outs[:3]] + [columns(outs[3])],
        compiler_params=pltpu.CompilerParams(vmem_limit_bytes=VMEM_LIMIT),
        cost_estimate=cost(512 * scores, *args, *outs, transcendentals=scores),
        name="attention_forward",
    )(cont_len, *args)


def attention_backward(queries, keys, values, dout, attended, probs_p, probs_c, cots, scale):
    rows, width = queries.shape
    total = keys.shape[0]
    heads, prompt_len, full_len = probs_p.shape
    cont_size = rows - prompt_len
    chunk = row_tile(prompt_len)

    def body(q, k, v, do, o, pp, pc, cot, prev_out, dq, dk, dv, acc_k, acc_v):
        acc_k[...] = jnp.zeros_like(acc_k)
        acc_v[...] = jnp.zeros_like(acc_v)
        for at in range(0, rows, chunk):
            here = slice(at, at + chunk)
            grads = []
            for head in range(2):
                mine = head_lanes((chunk, LANES), head)
                one_q = jnp.where(mine, q[here, :], 0)
                one_do = jnp.where(mine, do[here, :], 0)
                delta = jnp.sum(
                    one_do.astype(f32) * o[here, :].astype(f32), axis=-1, keepdims=True
                )
                if at < prompt_len:
                    span = full_len
                    probs = pp[head, here, :]
                    dprob = contract_cols(one_do, v[:span, :])
                    dscore = (probs.astype(f32) * (dprob - delta)).astype(bf16)
                else:
                    span = total
                    there = slice(at - prompt_len, at - prompt_len + chunk)
                    probs = pc[head, there, :]
                    dprob = contract_cols(one_do, v[...])
                    dscore = (
                        probs.astype(f32) * (dprob - delta) + cot[head, there, :].astype(f32)
                    ).astype(bf16)
                    prev_out[head, there, :] = dscore
                grads.append(product(dscore, k[:span, :]))
                acc_k[:span, :] += contract_rows(dscore, one_q)
                acc_v[:span, :] += contract_rows(probs, one_do)
            first = head_lanes((chunk, LANES), 0)
            dq[here, :] = (jnp.where(first, grads[0], grads[1]) * scale).astype(bf16)
        dk[...] = acc_k[...].astype(bf16)
        dv[...] = acc_v[...].astype(bf16)

    outs = [
        like((heads, cont_size, total), bf16),
        like((rows, width), bf16),
        like((total, width), bf16),
        like((total, width), bf16),
    ]

    def columns(array):
        return pl.BlockSpec((array.shape[0], LANES), lambda i: (0, i))

    def pairs(array):
        return pl.BlockSpec((2,) + array.shape[1:], lambda i: (i, 0, 0))

    args = [queries, keys, values, dout, attended, probs_p, probs_c, cots]
    scores = heads * (prompt_len * full_len + cont_size * total)
    return pl.pallas_call(
        body,
        grid=(heads // 2,),
        out_shape=outs,
        in_specs=[columns(a) for a in args[:5]] + [pairs(a) for a in args[5:]],
        out_specs=[pairs(outs[0])] + [columns(a) for a in outs[1:]],
        scratch_shapes=[pltpu.VMEM((total, LANES), f32), pltpu.VMEM((total, LANES), f32)],
        compiler_params=pltpu.CompilerParams(vmem_limit_bytes=VMEM_LIMIT),
        cost_estimate=cost(1024 * scores, *args, *outs),
        name="attention_backward",
    )(*args)


def first_norm_backward(grad_second, part, other, norm1, inv1, gain1, output_turned):
    rows, width = grad_second.shape
    tile = row_tile(rows)

    def body(d2, p, o, n1, r1, g1, ot, dh1, dout, sums):
        @pl.when(pl.program_id(0) == 0)
        def _():
            sums[...] = jnp.zeros_like(sums)

        upstream = d2[...] + (p[...].astype(f32) + o[...].astype(f32))
        normed = n1[...]
        grad = norm_pull(upstream, normed, r1[:, :1], g1[...])
        dh1[...] = grad
        low = grad.astype(bf16)
        dout[...] = product(low, ot[...]).astype(bf16)
        sums[0:1, :] += column_sums(upstream * normed)
        sums[1:2, :] += column_sums(upstream)
        sums[2:3, :] += column_sums(low.astype(f32))

    def tiled(array):
        return pl.BlockSpec((tile, array.shape[1]), lambda i: (i, 0))

    args = [grad_second, part, other, norm1, inv1, gain1, output_turned]
    outs = [
        like((rows, width), f32),
        like((rows, output_turned.shape[1]), bf16),
        like((8, width), f32),
    ]
    return pl.pallas_call(
        body,
        grid=(rows // tile,),
        out_shape=outs,
        in_specs=[tiled(a) for a in args[:5]] + [whole_block(a) for a in args[5:]],
        out_specs=[tiled(a) for a in outs[:2]] + [whole_block(outs[2])],
        compiler_params=pltpu.CompilerParams(vmem_limit_bytes=VMEM_LIMIT),
        cost_estimate=cost(2 * rows * width * output_turned.shape[1], *args, *outs),
        name="first_norm_backward",
    )(*args)


def weight_grads(grid, shards, grad_first, attended, inputs_t, whole_t, dq, dk, dv, sums1, sums2, up_sum):
    rows, width = grad_first.shape
    part = dq.shape[1]
    hidden = up_sum.shape[1]
    count = 2 if grid.staged else 1
    block = width // shards
    sides = pl.cdiv((6 * width + 2 * part + hidden) // LANES, block)
    extra = sides * LANES

    def body(place, d1, o, xt, wt, q, k, v, s1, s2, us, *rest):
        firsts, seconds = rest[:count], rest[count : 2 * count]
        full_a, full_b = rest[2 * count :]
        turned = d1[...].T.astype(bf16)
        full_a[:, :part] = product(turned, o[...]).astype(bf16)
        full_a[:, part:] = product(xt[...], q[...]).astype(bf16)
        full_b[:, :part] = product(wt[...], k[...]).astype(bf16)
        full_b[:, part : 2 * part] = product(wt[...], v[...]).astype(bf16)
        wide = 2 * part
        lines = [(s1, i) for i in range(3)] + [(s2, i) for i in range(3)]
        pieces = []
        for ref, i in lines:
            pieces += [ref[i : i + 1, at : at + LANES] for at in range(0, width, LANES)]
        for sums in (column_sums(q[...].astype(f32)), column_sums(v[...].astype(f32))):
            pieces += [sums[:, at : at + LANES] for at in range(0, part, LANES)]
        pieces += [us[0:1, at : at + LANES] for at in range(0, hidden, LANES)]
        pieces.append(jnp.zeros((sides * block - len(pieces), LANES), f32))
        table = jnp.concatenate(pieces, 0).astype(bf16)
        for shard in range(shards):
            for side in range(sides):
                low = wide + side * LANES
                full_b[shard * block : (shard + 1) * block, low : low + LANES] = table[
                    side * block : (side + 1) * block
                ]
        store_split(grid, place, full_a, firsts, True)
        store_split(grid, place, full_b, seconds, False)

    args = [grad_first, attended, inputs_t, whole_t, dq, dk, dv, sums1, sums2, up_sum]
    outs = split_out(grid, width, 2 * part) + split_out(grid, width, 2 * part + extra)
    vmem = pl.BlockSpec(memory_space=pltpu.VMEM)
    return pl.pallas_call(
        body,
        out_shape=outs,
        in_specs=[pl.BlockSpec(memory_space=pltpu.SMEM)] + [vmem] * len(args),
        out_specs=[vmem] * len(outs),
        scratch_shapes=[
            pltpu.VMEM((width, 2 * part), bf16),
            pltpu.VMEM((width, 2 * part + extra), bf16),
        ],
        compiler_params=pltpu.CompilerParams(vmem_limit_bytes=VMEM_LIMIT),
        cost_estimate=cost(4 * width * part * (rows + whole_t.shape[1]), *args, *outs),
        name="weight_grads",
    )(grid.place, *args)


def unpack_small(grid, packed, heads, head_size, up_rows):
    width = packed.shape[0]
    shards = grid.fsdp
    block, per_head, per_up = width // shards, head_size // shards, LANES // shards

    def body(packed_ref, lines, query_out, value_out, up_out):
        source = lax.broadcasted_iota(jnp.int32, (LANES, width), 0)
        target = lax.broadcasted_iota(jnp.int32, (LANES, width), 1)
        whole = jnp.zeros((32, width), f32)
        by_head = jnp.zeros((32, LANES), f32)
        by_up = jnp.zeros((32, LANES), f32)
        near, far = source[:, :LANES], target[:, :LANES]
        for shard in range(shards):
            piece = packed_ref[shard * block : shard * block + 32, :]
            put = (target - source == shard * block) & (source < block)
            whole += product(piece, put.astype(bf16))
            place = shard * per_head
            shift = far - near
            put = ((shift == place) | (shift == place + head_size)) & (near < per_head)
            by_head += product(piece, put.astype(bf16))
            put = (shift == shard * per_up) & (near < per_up)
            by_up += product(piece, put.astype(bf16))
        lines[...] = whole[:8, :]
        low = lax.broadcasted_iota(jnp.int32, (1, LANES), 1) < head_size
        for pair in range(heads // 2):
            at = slice(pair * LANES, (pair + 1) * LANES)
            for out, base in ((query_out, 6), (value_out, 6 + heads)):
                row = base + 2 * pair
                out[:, at] = jnp.where(low, by_head[row : row + 1, :], by_head[row + 1 : row + 2, :])
        for i in range(up_rows):
            row = 6 + 2 * heads + i
            up_out[:, i * LANES : (i + 1) * LANES] = by_up[row : row + 1, :]

    outs = [
        like((8, width), f32),
        like((1, heads * head_size), f32),
        like((1, heads * head_size), f32),
        like((1, up_rows * LANES), f32),
    ]
    vmem = pl.BlockSpec(memory_space=pltpu.VMEM)
    return pl.pallas_call(
        body,
        out_shape=outs,
        in_specs=[vmem],
        out_specs=[vmem] * 4,
        cost_estimate=cost(0, packed, *outs),
        name="unpack_small",
    )(packed)


def per_device(
    sizes,
    prompt,
    continuations,
    prev_logits,
    cont_len,
    query_weight,
    query_bias,
    key_weight,
    value_weight,
    value_bias,
    output_weight,
    output_bias,
    first_gain,
    first_shift,
    up_weight,
    up_bias,
    down_weight,
    down_bias,
    second_gain,
    second_shift,
    cot_prompt,
    cot_conts,
    cot_logits,
):
    grid = Grid(sizes)
    rows = query_weight.shape[0]
    width = query_weight.shape[1]
    hidden = up_weight.shape[1]
    prompt_len = prompt.shape[1]
    cont_size = continuations.shape[2]
    head_count = query_bias.shape[0]
    head_size = width // head_count
    scale = 1.0 / math.sqrt(head_size)

    lines = [v[None] for v in (output_bias, first_gain, first_shift, down_bias, second_gain, second_shift)]
    lines += [query_bias, value_bias, up_bias]
    small = jnp.concatenate([jnp.pad(v, ((0, 0), (0, LANES - v.shape[1]))) for v in lines], 0)
    small = jnp.pad(small, ((0, rows - small.shape[0]), (0, 0)))
    early, late = gather_rows(
        grid,
        [query_weight, key_weight, value_weight, small],
        [output_weight.T, up_weight, down_weight.T],
    )
    query_mat, key_mat, value_mat, small = early
    output_turned, up_mat, down_turned = late
    vectors, query_add, value_add, up_line = unpack_small(
        grid, small, head_count, head_size, up_bias.shape[0]
    )
    output_line, gain1, shift1, down_line, gain2, shift2 = [vectors[i : i + 1] for i in range(6)]

    mine = prompt[0]
    inputs = jnp.concatenate([mine, continuations[0, 0]], 0)
    if sizes[1] == 2:
        theirs = grid.over_ctx(mine)
        whole = jnp.concatenate(
            [
                jnp.where(grid.row == 0, mine, theirs),
                jnp.where(grid.row == 0, theirs, mine),
                continuations[0, 0],
            ],
            0,
        )
    else:
        whole = jnp.concatenate(
            [lax.all_gather(mine, "ctx", axis=0, tiled=True), continuations[0, 0]], 0
        )
    full_len = whole.shape[0] - cont_size
    whole_t, inputs_t = whole.T, inputs.T

    queries = ((product(inputs, query_mat) + query_add) * scale).astype(bf16)
    keys = product(whole, key_mat).astype(bf16)
    values = (product(whole, value_mat) + value_add).astype(bf16)
    new_logits, probs_p, probs_c, attended = attention_forward(
        queries, keys, values, prev_logits[0, 0], cont_len, prompt_len
    )
    part = contract_cols(attended, output_turned).astype(bf16)
    first_norm, first_inv, activated, slope, part2 = ffn_forward(
        inputs, part, grid.over_tp(part), output_line, gain1, shift1, up_mat, up_line, down_turned
    )
    results = ffn_backward(
        grid,
        first_norm,
        gain1,
        shift1,
        part2,
        grid.over_tp(part2),
        down_line,
        gain2,
        shift2,
        (cot_prompt[0], cot_conts[0, 0]),
        activated,
        slope,
        up_mat,
        down_turned,
    )
    result_prompt, result_cont, grad_second, part3, sums2, up_sum = results[:6]
    splits = results[6:]
    half = len(splits) // 2
    ffn_shard = scatter_split(grid, splits[:half], splits[half:]).astype(f32)
    grad_first, dout, sums1 = first_norm_backward(
        grad_second, part3, grid.over_tp(part3), first_norm, first_inv, gain1, output_turned
    )
    grad_prev, dq, dk, dv = attention_backward(
        queries, keys, values, dout, attended, probs_p, probs_c, cot_logits[0, 0], scale
    )
    splits = weight_grads(
        grid, sizes[0], grad_first, attended, inputs_t, whole_t, dq, dk, dv, sums1, sums2, up_sum
    )
    half = len(splits) // 2
    late_shard = scatter_split(grid, splits[:half], splits[half:]).astype(f32)

    from_query = contract_cols(dq, query_mat)
    from_keyvalue = contract_cols(dk, key_mat) + contract_cols(dv, value_mat)
    shared, own_cont = from_keyvalue[:full_len], from_keyvalue[full_len:]
    if sizes[1] == 2 and sizes[2] == 2:
        shared = shared.reshape(2, prompt_len, -1)
        abroad = pick(shared, 1 - grid.row, 0).astype(bf16).reshape(2, prompt_len // 2, -1)
        abroad_sum = add_low(
            pick(abroad, grid.core, 0), grid.over_tp(pick(abroad, 1 - grid.core, 0))
        )
        arrived = grid.over_ctx(abroad_sum).astype(f32)
        own = (pick(shared, grid.row, 0) + from_query[:prompt_len]).reshape(2, prompt_len // 2, -1)
        at = lax.broadcasted_iota(jnp.int32, (2, 1, 1), 0)
        own = own + jnp.where(at == grid.core, arrived[None], 0.0)
        own = own.reshape(prompt_len, -1)
    else:
        own = lax.psum_scatter(
            shared.astype(bf16), "ctx", scatter_dimension=0, tiled=True
        ).astype(f32)
        own = own + from_query[:prompt_len]
    partial = jnp.concatenate([own, own_cont + from_query[prompt_len:]], 0)
    input_grad = grad_first + grid.tp_sum(partial)

    table = late_shard[:, 4 * width :]
    table = jnp.concatenate([table[:, at : at + LANES] for at in range(0, table.shape[1], LANES)], 0)
    model = whole.shape[1]
    place = lax.axis_index("fsdp")
    at = 6 * (model // LANES)
    long_lines = table[:at].reshape(6, model)
    long_lines = lax.dynamic_slice_in_dim(long_lines, place * rows, rows, 1)
    shorts = []
    for bias in (query_bias, value_bias, up_bias):
        height, cols = bias.shape
        span = height * cols * sizes[0] // LANES
        block = table[at : at + span].reshape(height, -1)
        shorts.append(lax.dynamic_slice_in_dim(block, place * cols, cols, 1))
        at += span
    gain_one_grad, shift_one_grad, output_add_grad = long_lines[0], long_lines[1], long_lines[2]
    gain_two_grad, shift_two_grad, down_add_grad = long_lines[3], long_lines[4], long_lines[5]
    return (
        result_prompt[None],
        result_cont[None, None],
        new_logits[None, None],
        input_grad[:prompt_len][None],
        input_grad[prompt_len:][None, None],
        grad_prev[None, None],
        late_shard[:, width : 2 * width],
        shorts[0],
        late_shard[:, 2 * width : 3 * width],
        late_shard[:, 3 * width : 4 * width],
        shorts[1],
        late_shard[:, :width].T,
        output_add_grad,
        gain_one_grad,
        shift_one_grad,
        ffn_shard[:, :hidden],
        shorts[2],
        ffn_shard[:, hidden:].T,
        down_add_grad,
        gain_two_grad,
        shift_two_grad,
    )


def solution(mesh):
    sizes = tuple(mesh.shape[name] for name in ("fsdp", "ctx", "tp"))

    def step(*arrays):
        return per_device(sizes, *arrays)

    return jax.shard_map(
        step,
        mesh=mesh,
        in_specs=(
            P("fsdp", "ctx", None),
            P("fsdp", "ctx", None, None),
            P("fsdp", "ctx", "tp", None, None),
            P("fsdp", "ctx"),
            P("fsdp", "tp"),
            P("tp", "fsdp"),
            P("fsdp", "tp"),
            P("fsdp", "tp"),
            P("tp", "fsdp"),
            P("tp", "fsdp"),
            P("fsdp"),
            P("fsdp"),
            P("fsdp"),
            P("fsdp", "tp"),
            P("tp", "fsdp"),
            P("tp", "fsdp"),
            P("fsdp"),
            P("fsdp"),
            P("fsdp"),
            P("fsdp", "ctx", None),
            P("fsdp", "ctx", None, None),
            P("fsdp", "ctx", "tp", None, None),
        ),
        out_specs=(
            P("fsdp", "ctx", None),
            P("fsdp", "ctx", None, None),
            P("fsdp", "ctx", "tp", None, None),
            P("fsdp", "ctx", None),
            P("fsdp", "ctx", None, None),
            P("fsdp", "ctx", "tp", None, None),
            P("fsdp", "tp"),
            P("tp", "fsdp"),
            P("fsdp", "tp"),
            P("fsdp", "tp"),
            P("tp", "fsdp"),
            P("tp", "fsdp"),
            P("fsdp"),
            P("fsdp"),
            P("fsdp"),
            P("fsdp", "tp"),
            P("tp", "fsdp"),
            P("tp", "fsdp"),
            P("fsdp"),
            P("fsdp"),
            P("fsdp"),
        ),
        check_vma=False,
    )
```

```python
import math

import jax
import jax.numpy as jnp
from jax import lax
from jax.experimental import pallas as pl
from jax.experimental.pallas import tpu as pltpu
from jax.sharding import PartitionSpec as P

epsilon = 1e-06
f32 = jnp.float32
bf16 = jnp.bfloat16
LANES = 128


def product(left_mat, right_mat):
    return jnp.dot(left_mat, right_mat, preferred_element_type=f32)


def contract_rows(left_mat, right_mat):
    return lax.dot_general(
        left_mat, right_mat, (((0,), (0,)), ((), ())), preferred_element_type=f32
    )


def contract_cols(left_mat, right_mat):
    return lax.dot_general(
        left_mat, right_mat, (((1,), (1,)), ((), ())), preferred_element_type=f32
    )


class Grid:
    def __init__(self, sizes):
        self.fsdp, self.ctx, self.tp = sizes
        self.staged = sizes == (8, 2, 2)
        place = lax.axis_index("fsdp")
        self.outer, self.inner = place // 2, place % 2
        self.row = lax.axis_index("ctx")
        self.core = lax.axis_index("tp")
        self.place = jnp.stack([self.outer, self.inner, self.row]).astype(jnp.int32)

    def over_inner(self, array):
        return lax.ppermute(array, "fsdp", [(i, i ^ 1) for i in range(8)])

    def over_outer(self, array, step):
        return lax.ppermute(array, "fsdp", [(i, i ^ (2 * step)) for i in range(8)])

    def over_ctx(self, array):
        return lax.ppermute(array, "ctx", [(0, 1), (1, 0)])

    def over_tp(self, array):
        return lax.ppermute(array, "tp", [(0, 1), (1, 0)])

    def tp_sum(self, partial):
        low = partial.astype(bf16)
        return low.astype(f32) + self.over_tp(low).astype(f32)


def pack_early(grid, weights, vectors, tables):
    rows = weights[0].shape[0]
    edges = [sum(w.shape[1] for w in weights[:i]) for i in range(len(weights) + 1)]
    cols = edges[-1] + LANES
    count = len(weights)

    def body(place, *refs):
        out, half_out, lines = refs[-3:]
        for ref, low, high in zip(refs, edges, edges[1:]):
            out[:, low:high] = ref[...]
        lines[...] = jnp.zeros_like(lines)
        at = 0
        for ref in refs[count:-3]:
            height, width = ref.shape
            lines[at : at + height, :width] = ref[...].astype(f32)
            at += height
        out[:, edges[-1] :] = lines[...].astype(bf16)
        half_out[...] = out[pl.ds(pl.multiple_of(place[2] * (rows // 2), 16), rows // 2), :]

    vmem = pl.BlockSpec(memory_space=pltpu.VMEM)
    args = [*weights, *vectors, *tables]
    outs = [like((rows, cols), bf16), like((rows // 2, cols), bf16)]
    return pl.pallas_call(
        body,
        out_shape=outs,
        in_specs=[pl.BlockSpec(memory_space=pltpu.SMEM)] + [vmem] * len(args),
        out_specs=[vmem] * 2,
        scratch_shapes=[pltpu.VMEM((rows, LANES), f32)],
        cost_estimate=cost(0, *args, *outs),
        name="pack_early",
    )(grid.place, *args)


def pack_late(grid, shard, late):
    rows, head = shard.shape
    cols = sum(w.shape[1] for w in late)

    def body(place, early_ref, *refs):
        out, half_out = refs[-2:]
        out[:, :head] = early_ref[...]
        here = pl.ds(pl.multiple_of(place[2] * (rows // 2), 16), rows // 2)
        low = 0
        for ref in refs[:-2]:
            high = low + ref.shape[1]
            out[:, head + low : head + high] = ref[...]
            half_out[:, low:high] = ref[here, :]
            low = high

    vmem = pl.BlockSpec(memory_space=pltpu.VMEM)
    outs = [like((rows, head + cols), bf16), like((rows // 2, cols), bf16)]
    return pl.pallas_call(
        body,
        out_shape=outs,
        in_specs=[pl.BlockSpec(memory_space=pltpu.SMEM)] + [vmem] * (1 + len(late)),
        out_specs=[vmem] * 2,
        cost_estimate=cost(0, shard, *late, *outs),
        name="pack_late",
    )(grid.place, shard, *late)


def join(pieces):
    height, cols = pieces[0].shape

    def body(*refs):
        for i, ref in enumerate(refs[:-1]):
            refs[-1][i * height : (i + 1) * height, :] = ref[...]

    vmem = pl.BlockSpec(memory_space=pltpu.VMEM)
    out = like((len(pieces) * height, cols), pieces[0].dtype)
    return pl.pallas_call(
        body,
        out_shape=out,
        in_specs=[vmem] * len(pieces),
        out_specs=vmem,
        cost_estimate=cost(0, out, out),
        name="join",
    )(*pieces)


def assemble(grid, cuts, base, own, side, came, across, along):
    full = own.shape[0]
    half = full // 2
    edges = [sum(cuts[:i]) for i in range(len(cuts) + 1)]

    def body(place, own_ref, side_ref, came_ref, across_ref, along_ref, *outs):
        outer, inner, row = place[0], place[1], place[2]

        def put(ref, start, length, step, swap_inner, swap_row, skip=0):
            at = (outer ^ step) * 2 + (inner ^ swap_inner)
            if length == half:
                at = at * 2 + (row ^ swap_row)
            here = pl.ds(pl.multiple_of(at * length, 16), length)
            for out, low, high in zip(outs, edges, edges[1:]):
                out[here, :] = ref[start : start + length, skip + low : skip + high]

        put(own_ref, 0, full, 0, 0, 0, base)
        put(side_ref, 0, full, 0, 1, 0, base)
        for step in (1, 2, 3):
            start = (step - 1) * half
            put(came_ref, start, half, step, 0, 0)
            put(across_ref, start, half, step, 1, 0)
            put(along_ref, start, half, step, 0, 1)
            for out in outs:
                at = (((outer ^ step) * 2 + (inner ^ 1)) * 2 + (row ^ 1)) * half
                out[pl.ds(pl.multiple_of(at, 16), half), :] = jnp.zeros((half, out.shape[1]), bf16)

    vmem = pl.BlockSpec(memory_space=pltpu.VMEM)
    outs = [like((8 * full, cols), own.dtype) for cols in cuts]
    return pl.pallas_call(
        body,
        out_shape=outs,
        in_specs=[pl.BlockSpec(memory_space=pltpu.SMEM)] + [vmem] * 5,
        out_specs=[vmem] * len(outs),
        compiler_params=pltpu.CompilerParams(vmem_limit_bytes=VMEM_LIMIT),
        cost_estimate=cost(0, *outs, *outs),
        name="assemble",
    )(grid.place, own, side, came, across, along)


def complete(grid, arrays, far_one, far_two):
    half = far_one.shape[0] // 3
    first = 0
    while sum(a.shape[1] for a in arrays[: first + 1]) <= far_one.shape[1]:
        first += 1
    count = len(arrays)
    copies = 3 * count

    def body(place, one_ref, two_ref, *refs):
        outs, sems = refs[count : 2 * count], refs[2 * count]
        outer, inner, row = place[0], place[1], place[2]
        started = []
        low = 0
        for i, out in enumerate(outs):
            ref = one_ref if i < first else two_ref
            if i == first:
                low = 0
            cols = out.shape[1]
            for step in (1, 2, 3):
                at = (((outer ^ step) * 2 + (inner ^ 1)) * 2 + (row ^ 1)) * half
                copy = pltpu.make_async_copy(
                    ref.at[(step - 1) * half : step * half, low : low + cols],
                    out.at[pl.ds(pl.multiple_of(at, 16), half), :],
                    sems.at[len(started)],
                )
                copy.start()
                started.append(copy)
            low += cols
        for copy in started:
            copy.wait()

    vmem = pl.BlockSpec(memory_space=pltpu.VMEM)
    anywhere = pl.BlockSpec(memory_space=pl.ANY)
    return pl.pallas_call(
        body,
        out_shape=[like(a.shape, a.dtype) for a in arrays],
        in_specs=[pl.BlockSpec(memory_space=pltpu.SMEM), vmem, vmem] + [anywhere] * count,
        out_specs=[anywhere] * count,
        scratch_shapes=[pltpu.SemaphoreType.DMA((copies,))],
        input_output_aliases={3 + i: i for i in range(count)},
        cost_estimate=cost(0, far_one, far_two, far_one, far_two),
        name="complete",
    )(grid.place, far_one, far_two, *arrays)


def lines_of(grid, mine):
    return [grid.over_outer(mine, step) for step in (1, 2, 3)]


def pairs_of(grid, came):
    return grid.over_inner(came), grid.over_ctx(came)


def corners_of(grid, across, along, cut):
    return grid.over_ctx(across[:, :cut]), grid.over_inner(along[:, cut:])


def pick(array, at, axis):
    return lax.dynamic_index_in_dim(array, at, axis, keepdims=False)


def add_low(left, right):
    return (left.astype(f32) + right.astype(f32)).astype(bf16)


VMEM_LIMIT = 60 * 1024 * 1024


def whole_block(array):
    rank = array.ndim
    return pl.BlockSpec(array.shape, lambda *_: (0,) * rank)


def cost(flops, *arrays, transcendentals=0):
    moved = sum(math.prod(a.shape) * jnp.dtype(a.dtype).itemsize for a in arrays)
    return pl.CostEstimate(
        flops=int(flops), transcendentals=int(transcendentals), bytes_accessed=int(moved)
    )


def like(shape, dtype):
    return jax.ShapeDtypeStruct(shape, dtype)


def norm_rows(hidden_in):
    centre = jnp.mean(hidden_in, axis=-1, keepdims=True)
    shifted = hidden_in - centre
    spread = jnp.mean(shifted * shifted, axis=-1, keepdims=True)
    inverse = lax.rsqrt(spread + epsilon)
    return shifted * inverse, inverse


def norm_pull(upstream, normed, inverse, gain):
    scaled = upstream * gain
    mean_one = jnp.mean(scaled, axis=-1, keepdims=True)
    mean_two = jnp.mean(scaled * normed, axis=-1, keepdims=True)
    return inverse * (scaled - mean_one - normed * mean_two)


def column_sums(values):
    return jnp.sum(values, axis=0, keepdims=True)


def row_tile(rows):
    return 256 if rows % 256 == 0 else rows


def first_norm(prompt, conts, part, other, output_add, gain, shift):
    prompt_len, width = prompt.shape
    rows = prompt_len + conts.shape[0]
    tile = row_tile(prompt_len)
    ahead = prompt_len // tile

    def body(x, c, p, o, b, g, s, norm_out, inv_out, low_out, turned_out):
        rows_in = jnp.where(pl.program_id(0) < ahead, x[...].astype(f32), c[...].astype(f32))
        normed, inverse = norm_rows(rows_in + (p[...].astype(f32) + o[...].astype(f32)) + b[...])
        norm_out[...] = normed
        inv_out[...] = jnp.broadcast_to(inverse, inv_out.shape)
        value = normed * g[...] + s[...]
        low_out[...] = value.astype(bf16)
        turned_out[...] = value.T.astype(bf16)

    def tiled(array):
        return pl.BlockSpec((tile, array.shape[1]), lambda i: (i, 0))

    args = [prompt, conts, part, other, output_add, gain, shift]
    outs = [
        like((rows, width), f32),
        like((rows, LANES), f32),
        like((rows, width), bf16),
        like((width, rows), bf16),
    ]
    return pl.pallas_call(
        body,
        grid=(rows // tile,),
        out_shape=outs,
        in_specs=[
            pl.BlockSpec((tile, width), lambda i: (jnp.minimum(i, ahead - 1), 0)),
            pl.BlockSpec((tile, width), lambda i: (jnp.maximum(i - ahead, 0), 0)),
        ]
        + [tiled(a) for a in args[2:4]]
        + [whole_block(a) for a in args[4:]],
        out_specs=[tiled(a) for a in outs[:3]] + [pl.BlockSpec((width, tile), lambda i: (0, i))],
        compiler_params=pltpu.CompilerParams(vmem_limit_bytes=VMEM_LIMIT),
        cost_estimate=cost(0, *args, *outs),
        name="first_norm",
    )(*args)


def ffn_forward(low, up_mat, up_add, down_turned):
    rows, width = low.shape
    hidden = up_mat.shape[1]
    tile = row_tile(rows)

    def body(x, up, ub, dn, act_out, slope_out, part_out):
        inner = product(x[...], up[...]) + ub[...]
        normal_cdf = 0.5 * (1.0 + lax.erf(inner * math.sqrt(0.5)))
        act = (inner * normal_cdf).astype(bf16)
        act_out[...] = act
        density = jnp.exp(-0.5 * inner * inner) * (1.0 / math.sqrt(2.0 * math.pi))
        slope_out[...] = (normal_cdf + inner * density).astype(bf16)
        part_out[...] = contract_cols(act, dn[...]).astype(bf16)

    outs = [
        like((rows, hidden), bf16),
        like((rows, hidden), bf16),
        like((rows, width), bf16),
    ]

    def tiled(array):
        return pl.BlockSpec((tile, array.shape[1]), lambda i: (i, 0))

    args = [low, up_mat, up_add, down_turned]
    return pl.pallas_call(
        body,
        grid=(rows // tile,),
        out_shape=outs,
        in_specs=[tiled(low)] + [whole_block(a) for a in args[1:]],
        out_specs=[tiled(a) for a in outs],
        compiler_params=pltpu.CompilerParams(vmem_limit_bytes=VMEM_LIMIT),
        cost_estimate=cost(4 * rows * width * hidden, *args, *outs, transcendentals=2 * rows * hidden),
        name="ffn_forward",
    )(*args)


def split_out(grid, length, cols):
    if grid.staged:
        return [like((length // 2, cols), bf16), like((length // 2, cols), bf16)]
    return [like((length, cols), bf16)]


def store_split(grid, place, full_ref, outs, over_inner):
    if not grid.staged:
        outs[0][...] = full_ref[...]
        return
    half = full_ref.shape[0] // 16
    for out, flip in zip(outs, (0, 1)):
        if over_inner:
            for outer in range(4):
                at = pl.multiple_of((2 * outer + (place[1] ^ flip)) * (2 * half), 32)
                out[2 * half * outer : 2 * half * (outer + 1), :] = full_ref[pl.ds(at, 2 * half), :]
        else:
            for block in range(8):
                at = pl.multiple_of((2 * block + (place[2] ^ flip)) * half, 16)
                out[half * block : half * (block + 1), :] = full_ref[pl.ds(at, half), :]


def ffn_backward(grid, norm1, turned1, gain1, shift1, part, other, down_add, gain2, shift2, cots, act, slope, up_mat, down_turned):
    rows, width = norm1.shape
    hidden = up_mat.shape[1]
    tile = 256
    chunk = row_tile(rows)
    prompt_len = cots[0].shape[0]
    count = 2 if grid.staged else 1

    def body(place, n1, x1_t, g1, s1, p, o, db, g2, s2, cp, cc, u, sl, up, dn, *rest):
        outs, scratch = rest[:-5], rest[-5:]
        y_p, y_c, dh2, dx1, sums, up_sum = outs[:6]
        up_outs, down_outs = outs[6 : 6 + count], outs[6 + count :]
        df, df_t, acc, full_up, full_down = scratch
        step = pl.program_id(0)

        @pl.when(step == 0)
        def _():
            total = [jnp.zeros((1, width), f32) for _ in range(3)]
            for at in range(0, rows, chunk):
                here = slice(at, at + chunk)
                first = n1[here, :] * g1[...] + s1[...]
                second = first + (p[here, :].astype(f32) + o[here, :].astype(f32)) + db[...]
                normed, inverse = norm_rows(second)
                result = (normed * g2[...] + s2[...]).astype(bf16)
                if at < prompt_len:
                    y_p[here, :] = result
                    cot = cp[here, :].astype(f32)
                else:
                    there = slice(at - prompt_len, at - prompt_len + chunk)
                    y_c[there, :] = result
                    cot = cc[there, :].astype(f32)
                grad = norm_pull(cot, normed, inverse, g2[...])
                dh2[here, :] = grad
                low = grad.astype(bf16)
                df[here, :] = low
                wide = low.astype(f32)
                df_t[:, here] = wide.T.astype(bf16)
                total[0] += column_sums(cot * normed)
                total[1] += column_sums(cot)
                total[2] += column_sums(wide)
            sums[...] = jnp.zeros(sums.shape, f32)
            for i in range(3):
                sums[i : i + 1, :] = total[i]
            acc[...] = jnp.zeros_like(acc)

        inner = (product(df[...], dn[...]) * sl[...].astype(f32)).astype(bf16)
        up_sum[...] = jnp.broadcast_to(column_sums(inner.astype(f32)), up_sum.shape)
        full_up[...] = product(x1_t[...], inner).astype(bf16)
        full_down[...] = product(df_t[...], u[...]).astype(bf16)
        acc[...] += contract_cols(inner, up[...])
        store_split(grid, place, full_up, up_outs, True)
        store_split(grid, place, full_down, down_outs, False)

        @pl.when(step == hidden // tile - 1)
        def _():
            dx1[...] = acc[...].astype(bf16)

    def tiled(array):
        return pl.BlockSpec((array.shape[0], tile), lambda j: (0, j))

    fixed = [norm1, turned1, gain1, shift1, part, other, down_add, gain2, shift2, *cots]
    moving = [act, slope, up_mat, down_turned]
    outs = [
        like((prompt_len, width), bf16),
        like((rows - prompt_len, width), bf16),
        like((rows, width), f32),
        like((rows, width), bf16),
        like((8, width), f32),
        like((8, hidden), f32),
    ]
    grads = split_out(grid, width, hidden) * 2
    return pl.pallas_call(
        body,
        grid=(hidden // tile,),
        out_shape=outs + grads,
        in_specs=[pl.BlockSpec(memory_space=pltpu.SMEM)]
        + [whole_block(a) for a in fixed]
        + [tiled(a) for a in moving],
        out_specs=[whole_block(a) for a in outs[:5]] + [tiled(a) for a in outs[5:] + grads],
        scratch_shapes=[
            pltpu.VMEM((rows, width), bf16),
            pltpu.VMEM((width, rows), bf16),
            pltpu.VMEM((rows, width), f32),
            pltpu.VMEM((width, tile), bf16),
            pltpu.VMEM((width, tile), bf16),
        ],
        compiler_params=pltpu.CompilerParams(vmem_limit_bytes=VMEM_LIMIT),
        cost_estimate=cost(8 * rows * width * hidden, *fixed, *moving, *outs, *grads),
        name="ffn_backward",
    )(grid.place, *fixed, *moving)


def fold_pair(grid, first, second):
    half = first[0].shape[0] // 8
    outs = []
    for kept, _ in (first, second):
        outs += [like((4 * half, kept.shape[1]), bf16)] * 2

    def body(place, fk, fa, sk, sa, f_keep, f_send, s_keep, s_send):
        for kept, came, keep, send, mine in (
            (fk, fa, f_keep, f_send, place[2]),
            (sk, sa, s_keep, s_send, place[1]),
        ):
            for out, flip in ((send, 1), (keep, 0)):
                at = pl.multiple_of((mine ^ flip) * half, 16)
                here = pl.ds(at, half)
                out[...] = (kept[here, :].astype(f32) + came[here, :].astype(f32)).astype(bf16)

    args = [*first, *second]
    return pl.pallas_call(
        body,
        grid=(4,),
        out_shape=outs,
        in_specs=[pl.BlockSpec(memory_space=pltpu.SMEM)]
        + [pl.BlockSpec((2 * half, a.shape[1]), lambda i: (i, 0)) for a in args],
        out_specs=[pl.BlockSpec((half, a.shape[1]), lambda i: (i, 0)) for a in outs],
        cost_estimate=cost(0, *args, *outs),
        name="fold_pair",
    )(grid.place, *args)


def fold_line(grid, first, second):
    half = first[0].shape[0] // 4
    left, right = first[0].shape[1], second[0].shape[1]
    outs = [like((half, left + right), f32)] + [like((half, left + right), bf16)] * 3

    def body(place, fk, fa, sk, sa, *out_refs):
        for step, out in enumerate(out_refs):
            here = pl.ds(pl.multiple_of((place[0] ^ step) * half, 16), half)
            out[:, :left] = (fk[here, :].astype(f32) + fa[here, :].astype(f32)).astype(out.dtype)
            out[:, left:] = (sk[here, :].astype(f32) + sa[here, :].astype(f32)).astype(out.dtype)

    vmem = pl.BlockSpec(memory_space=pltpu.VMEM)
    args = [*first, *second]
    return pl.pallas_call(
        body,
        out_shape=outs,
        in_specs=[pl.BlockSpec(memory_space=pltpu.SMEM)] + [vmem] * 4,
        out_specs=[vmem] * 4,
        cost_estimate=cost(0, *args, *outs),
        name="fold_line",
    )(grid.place, *args)


def scatter_split(grid, first, second, after=None):
    if not grid.staged:
        both = jnp.concatenate([first[0], second[0]], 1)
        both = lax.psum_scatter(both, "fsdp", scatter_dimension=0, tiled=True)
        return lax.psum(both, "ctx")
    came_first = grid.over_inner(first[1])
    came_second = grid.over_ctx(second[1])
    if after is not None:
        came_first, came_second, _ = lax.optimization_barrier((came_first, came_second, after))
    f_keep, f_send, s_keep, s_send = fold_pair(grid, (first[0], came_first), (second[0], came_second))
    came_first = grid.over_ctx(f_send)
    came_second = grid.over_inner(s_send)
    total, *sent = fold_line(grid, (f_keep, came_first), (s_keep, came_second))
    for step in (1, 2, 3):
        total = total + grid.over_outer(sent[step - 1], step).astype(f32)
    total = total.astype(bf16)
    other = grid.over_ctx(total)
    low = jnp.where(grid.row == 0, total, other)
    high = jnp.where(grid.row == 0, other, total)
    return jnp.concatenate([low, high], 0)


def head_lanes(shape, index):
    lane = lax.broadcasted_iota(jnp.int32, shape, 1)
    return (lane < LANES // 2) if index == 0 else (lane >= LANES // 2)


def attention_forward(queries, keys, values, prev_logits, cont_len, prompt_len, pairs, held=()):
    begin, end = pairs
    kept = len(held)
    rows, width = queries.shape
    total = keys.shape[0]
    cont_size = rows - prompt_len
    full_len = total - cont_size
    heads = prev_logits.shape[0]
    chunk = row_tile(prompt_len)

    def body(length, q, k, v, prev, *refs):
        logits, probs_p, probs_c, out = refs[kept:]

        def soft(scores):
            weights = jnp.exp(scores - jnp.max(scores, axis=-1, keepdims=True))
            return (weights * (1.0 / jnp.sum(weights, axis=-1, keepdims=True))).astype(bf16)

        column = lax.broadcasted_iota(jnp.int32, (1, total), 1)
        live = column < full_len + length[0, 0]
        for at in range(0, rows, chunk):
            here = slice(at, at + chunk)
            halves = []
            for head in range(2):
                one = jnp.where(head_lanes((chunk, LANES), head), q[here, :], 0)
                if at < prompt_len:
                    probs = soft(contract_cols(one, k[:full_len, :]))
                    probs_p[head, here, :] = probs
                    halves.append(product(probs, v[:full_len, :]))
                else:
                    there = slice(at - prompt_len, at - prompt_len + chunk)
                    raw = prev[head, there, :].astype(f32) + contract_cols(one, k[...])
                    logits[head, there, :] = raw.astype(bf16)
                    probs = soft(jnp.where(live, raw, -1e30))
                    probs_c[head, there, :] = probs
                    halves.append(product(probs, v[...]))
            first = head_lanes((chunk, LANES), 0)
            out[here, :] = jnp.where(first, halves[0], halves[1]).astype(bf16)

    outs = [
        like((heads, cont_size, total), bf16),
        like((heads, prompt_len, full_len), bf16),
        like((heads, cont_size, total), bf16),
        like((rows, width), bf16),
    ]

    def columns(array):
        return pl.BlockSpec((array.shape[0], LANES), lambda i: (0, begin + i))

    def pair_of(array):
        return pl.BlockSpec((2,) + array.shape[1:], lambda i: (begin + i, 0, 0))

    args = [queries, keys, values, prev_logits]
    scores = heads * (prompt_len * full_len + cont_size * total)
    return pl.pallas_call(
        body,
        grid=(end - begin,),
        out_shape=outs,
        in_specs=[pl.BlockSpec(memory_space=pltpu.SMEM)]
        + [columns(a) for a in args[:3]]
        + [pair_of(prev_logits)]
        + [pl.BlockSpec(memory_space=pl.ANY)] * kept,
        out_specs=[pair_of(a) for a in outs[:3]] + [columns(outs[3])],
        compiler_params=pltpu.CompilerParams(vmem_limit_bytes=VMEM_LIMIT),
        input_output_aliases={5 + i: i for i in range(kept)},
        cost_estimate=cost((end - begin) * 256 * scores, *args, transcendentals=scores),
        name="attention_forward",
    )(cont_len, *args, *held)


def attention_backward(queries, keys, values, dout, attended, probs_p, probs_c, cots, scale):
    rows, width = queries.shape
    total = keys.shape[0]
    heads, prompt_len, full_len = probs_p.shape
    cont_size = rows - prompt_len
    chunk = row_tile(prompt_len)

    def body(q, k, v, do, o, pp, pc, cot, prev_out, dq, dk, dv, acc_k, acc_v):
        acc_k[...] = jnp.zeros_like(acc_k)
        acc_v[...] = jnp.zeros_like(acc_v)
        for at in range(0, rows, chunk):
            here = slice(at, at + chunk)
            grads = []
            for head in range(2):
                mine = head_lanes((chunk, LANES), head)
                one_q = jnp.where(mine, q[here, :], 0)
                one_do = jnp.where(mine, do[here, :], 0)
                delta = jnp.sum(
                    one_do.astype(f32) * o[here, :].astype(f32), axis=-1, keepdims=True
                )
                if at < prompt_len:
                    span = full_len
                    probs = pp[head, here, :]
                    dprob = contract_cols(one_do, v[:span, :])
                    dscore = (probs.astype(f32) * (dprob - delta)).astype(bf16)
                else:
                    span = total
                    there = slice(at - prompt_len, at - prompt_len + chunk)
                    probs = pc[head, there, :]
                    dprob = contract_cols(one_do, v[...])
                    dscore = (
                        probs.astype(f32) * (dprob - delta) + cot[head, there, :].astype(f32)
                    ).astype(bf16)
                    prev_out[head, there, :] = dscore
                grads.append(product(dscore, k[:span, :]))
                acc_k[:span, :] += contract_rows(dscore, one_q)
                acc_v[:span, :] += contract_rows(probs, one_do)
            first = head_lanes((chunk, LANES), 0)
            dq[here, :] = (jnp.where(first, grads[0], grads[1]) * scale).astype(bf16)
        dk[...] = acc_k[...].astype(bf16)
        dv[...] = acc_v[...].astype(bf16)

    outs = [
        like((heads, cont_size, total), bf16),
        like((rows, width), bf16),
        like((total, width), bf16),
        like((total, width), bf16),
    ]

    def columns(array):
        return pl.BlockSpec((array.shape[0], LANES), lambda i: (0, i))

    def pairs(array):
        return pl.BlockSpec((2,) + array.shape[1:], lambda i: (i, 0, 0))

    args = [queries, keys, values, dout, attended, probs_p, probs_c, cots]
    scores = heads * (prompt_len * full_len + cont_size * total)
    return pl.pallas_call(
        body,
        grid=(heads // 2,),
        out_shape=outs,
        in_specs=[columns(a) for a in args[:5]] + [pairs(a) for a in args[5:]],
        out_specs=[pairs(outs[0])] + [columns(a) for a in outs[1:]],
        scratch_shapes=[pltpu.VMEM((total, LANES), f32), pltpu.VMEM((total, LANES), f32)],
        compiler_params=pltpu.CompilerParams(vmem_limit_bytes=VMEM_LIMIT),
        cost_estimate=cost(1024 * scores, *args, *outs),
        name="attention_backward",
    )(*args)


def first_norm_backward(grad_second, part, other, norm1, inv1, gain1, output_turned):
    rows, width = grad_second.shape
    tile = row_tile(rows)

    def body(d2, p, o, n1, r1, g1, ot, dh1, dout, sums):
        @pl.when(pl.program_id(0) == 0)
        def _():
            sums[...] = jnp.zeros_like(sums)

        upstream = d2[...] + (p[...].astype(f32) + o[...].astype(f32))
        normed = n1[...]
        grad = norm_pull(upstream, normed, r1[:, :1], g1[...])
        dh1[...] = grad
        low = grad.astype(bf16)
        dout[...] = product(low, ot[...]).astype(bf16)
        sums[0:1, :] += column_sums(upstream * normed)
        sums[1:2, :] += column_sums(upstream)
        sums[2:3, :] += column_sums(low.astype(f32))

    def tiled(array):
        return pl.BlockSpec((tile, array.shape[1]), lambda i: (i, 0))

    args = [grad_second, part, other, norm1, inv1, gain1, output_turned]
    outs = [
        like((rows, width), f32),
        like((rows, output_turned.shape[1]), bf16),
        like((8, width), f32),
    ]
    return pl.pallas_call(
        body,
        grid=(rows // tile,),
        out_shape=outs,
        in_specs=[tiled(a) for a in args[:5]] + [whole_block(a) for a in args[5:]],
        out_specs=[tiled(a) for a in outs[:2]] + [whole_block(outs[2])],
        compiler_params=pltpu.CompilerParams(vmem_limit_bytes=VMEM_LIMIT),
        cost_estimate=cost(2 * rows * width * output_turned.shape[1], *args, *outs),
        name="first_norm_backward",
    )(*args)


def weight_grads(grid, shards, grad_first, attended, inputs_t, whole_t, dq, dk, dv, sums1, sums2, up_sum):
    rows, width = grad_first.shape
    part = dq.shape[1]
    hidden = up_sum.shape[1]
    count = 2 if grid.staged else 1
    block = width // shards
    sides = pl.cdiv((6 * width + 2 * part + hidden) // LANES, block)
    extra = sides * LANES

    def body(place, d1, o, xt, wt, q, k, v, s1, s2, us, *rest):
        firsts, seconds = rest[:count], rest[count : 2 * count]
        full_a, full_b = rest[2 * count :]
        turned = d1[...].T.astype(bf16)
        full_a[:, :part] = product(turned, o[...]).astype(bf16)
        full_a[:, part:] = product(xt[...], q[...]).astype(bf16)
        full_b[:, :part] = product(wt[...], k[...]).astype(bf16)
        full_b[:, part : 2 * part] = product(wt[...], v[...]).astype(bf16)
        wide = 2 * part
        lines = [(s1, i) for i in range(3)] + [(s2, i) for i in range(3)]
        pieces = []
        for ref, i in lines:
            pieces += [ref[i : i + 1, at : at + LANES] for at in range(0, width, LANES)]
        for sums in (column_sums(q[...].astype(f32)), column_sums(v[...].astype(f32))):
            pieces += [sums[:, at : at + LANES] for at in range(0, part, LANES)]
        pieces += [us[0:1, at : at + LANES] for at in range(0, hidden, LANES)]
        pieces.append(jnp.zeros((sides * block - len(pieces), LANES), f32))
        table = jnp.concatenate(pieces, 0).astype(bf16)
        for shard in range(shards):
            for side in range(sides):
                low = wide + side * LANES
                full_b[shard * block : (shard + 1) * block, low : low + LANES] = table[
                    side * block : (side + 1) * block
                ]
        store_split(grid, place, full_a, firsts, True)
        store_split(grid, place, full_b, seconds, False)

    args = [grad_first, attended, inputs_t, whole_t, dq, dk, dv, sums1, sums2, up_sum]
    outs = split_out(grid, width, 2 * part) + split_out(grid, width, 2 * part + extra)
    vmem = pl.BlockSpec(memory_space=pltpu.VMEM)
    return pl.pallas_call(
        body,
        out_shape=outs,
        in_specs=[pl.BlockSpec(memory_space=pltpu.SMEM)] + [vmem] * len(args),
        out_specs=[vmem] * len(outs),
        scratch_shapes=[
            pltpu.VMEM((width, 2 * part), bf16),
            pltpu.VMEM((width, 2 * part + extra), bf16),
        ],
        compiler_params=pltpu.CompilerParams(vmem_limit_bytes=VMEM_LIMIT),
        cost_estimate=cost(4 * width * part * (rows + whole_t.shape[1]), *args, *outs),
        name="weight_grads",
    )(grid.place, *args)


def unpack_small(grid, packed, heads, head_size, up_rows):
    width = packed.shape[0]
    shards = grid.fsdp
    block, per_head, per_up = width // shards, head_size // shards, LANES // shards

    def body(packed_ref, lines, query_out, value_out, up_out):
        source = lax.broadcasted_iota(jnp.int32, (LANES, width), 0)
        target = lax.broadcasted_iota(jnp.int32, (LANES, width), 1)
        whole = jnp.zeros((32, width), f32)
        by_head = jnp.zeros((32, LANES), f32)
        by_up = jnp.zeros((32, LANES), f32)
        near, far = source[:, :LANES], target[:, :LANES]
        for shard in range(shards):
            piece = packed_ref[shard * block : shard * block + 32, :]
            put = (target - source == shard * block) & (source < block)
            whole += product(piece, put.astype(bf16))
            place = shard * per_head
            shift = far - near
            put = ((shift == place) | (shift == place + head_size)) & (near < per_head)
            by_head += product(piece, put.astype(bf16))
            put = (shift == shard * per_up) & (near < per_up)
            by_up += product(piece, put.astype(bf16))
        lines[...] = whole[:8, :]
        low = lax.broadcasted_iota(jnp.int32, (1, LANES), 1) < head_size
        for pair in range(heads // 2):
            at = slice(pair * LANES, (pair + 1) * LANES)
            for out, base in ((query_out, 6), (value_out, 6 + heads)):
                row = base + 2 * pair
                out[:, at] = jnp.where(low, by_head[row : row + 1, :], by_head[row + 1 : row + 2, :])
        for i in range(up_rows):
            row = 6 + 2 * heads + i
            up_out[:, i * LANES : (i + 1) * LANES] = by_up[row : row + 1, :]

    outs = [
        like((8, width), f32),
        like((1, heads * head_size), f32),
        like((1, heads * head_size), f32),
        like((1, up_rows * LANES), f32),
    ]
    vmem = pl.BlockSpec(memory_space=pltpu.VMEM)
    return pl.pallas_call(
        body,
        out_shape=outs,
        in_specs=[vmem],
        out_specs=[vmem] * 4,
        cost_estimate=cost(0, packed, *outs),
        name="unpack_small",
    )(packed)


def per_device(
    sizes,
    prompt,
    continuations,
    prev_logits,
    cont_len,
    query_weight,
    query_bias,
    key_weight,
    value_weight,
    value_bias,
    output_weight,
    output_bias,
    first_gain,
    first_shift,
    up_weight,
    up_bias,
    down_weight,
    down_bias,
    second_gain,
    second_shift,
    cot_prompt,
    cot_conts,
    cot_logits,
):
    grid = Grid(sizes)
    rows = query_weight.shape[0]
    width = query_weight.shape[1]
    hidden = up_weight.shape[1]
    prompt_len = prompt.shape[1]
    cont_size = continuations.shape[2]
    head_count = query_bias.shape[0]
    head_size = width // head_count
    scale = 1.0 / math.sqrt(head_size)

    mine, conts = prompt[0], continuations[0, 0]
    lines = [v[None] for v in (output_bias, first_gain, first_shift, down_bias, second_gain, second_shift)]
    tables = [query_bias, value_bias, up_bias]
    early = [query_weight, key_weight, value_weight, output_weight.T]
    late = [up_weight, down_weight.T]
    shard, half_shard = pack_early(grid, early, lines, tables)
    cuts = [width, width, width, width, LANES]
    cut = 2 * width
    if grid.staged:
        came = lines_of(grid, half_shard)
        sent, shard = lax.optimization_barrier((mine, shard))
        theirs = grid.over_ctx(sent)
        shards, late_half = pack_late(grid, shard, late)
        side = grid.over_inner(shards)
        came, late_half, theirs = lax.optimization_barrier((came, late_half, theirs))
        came = join(came)
        across, along = pairs_of(grid, came)
        far = corners_of(grid, across, along, cut)
        late_came = lines_of(grid, late_half)
        far, late_came = lax.optimization_barrier((far, late_came))
        early = complete(
            grid, assemble(grid, cuts, 0, shards, side, came, across, along), *far
        )
        late_came = join(late_came)
        late_across, late_along = pairs_of(grid, late_came)
    else:
        shards = [shard] + late
        shards = [lax.all_gather(a, "fsdp", axis=0, tiled=True) for a in shards]
        edges = [sum(cuts[:i]) for i in range(len(cuts) + 1)]
        early = [shards[0][:, low:high] for low, high in zip(edges, edges[1:])]
        late = shards[1:]
    query_mat, key_mat, value_mat, output_turned, small = early
    vectors, query_add, value_add, up_line = unpack_small(
        grid, small, head_count, head_size, up_bias.shape[0]
    )
    output_line, gain1, shift1, down_line, gain2, shift2 = [vectors[i : i + 1] for i in range(6)]

    inputs = jnp.concatenate([mine, conts], 0)
    if sizes[1] == 2:
        if not grid.staged:
            theirs = grid.over_ctx(mine)
        whole = jnp.concatenate(
            [jnp.where(grid.row == 0, mine, theirs), jnp.where(grid.row == 0, theirs, mine), conts], 0
        )
    else:
        whole = jnp.concatenate([lax.all_gather(mine, "ctx", axis=0, tiled=True), conts], 0)
    full_len = whole.shape[0] - cont_size
    whole_t, inputs_t = whole.T, inputs.T

    queries = ((product(inputs, query_mat) + query_add) * scale).astype(bf16)
    keys = product(whole, key_mat).astype(bf16)
    values = (product(whole, value_mat) + value_add).astype(bf16)
    queries, whole_t, inputs_t = lax.optimization_barrier((queries, whole_t, inputs_t))
    attention = (queries, keys, values, prev_logits[0, 0], cont_len, prompt_len)
    pair_count = head_count // 2
    held = attention_forward(*attention, (0, pair_count - 1))
    if grid.staged:
        late_across, late_along, held = lax.optimization_barrier((late_across, late_along, held))
        far = corners_of(grid, late_across, late_along, hidden)
    new_logits, probs_p, probs_c, attended = attention_forward(
        *attention, (pair_count - 1, pair_count), held
    )
    if grid.staged:
        late = assemble(
            grid, [hidden, hidden], sum(cuts), shards, side, late_came, late_across, late_along
        )
    part = contract_cols(attended, output_turned).astype(bf16)
    norm1, inv1, low1, turned1 = first_norm(
        mine, conts, part, grid.over_tp(part), output_line, gain1, shift1
    )
    if grid.staged:
        late = complete(grid, late, *far)
    up_mat, down_turned = late
    activated, slope, part2 = ffn_forward(low1, up_mat, up_line, down_turned)
    results = ffn_backward(
        grid,
        norm1,
        turned1,
        gain1,
        shift1,
        part2,
        grid.over_tp(part2),
        down_line,
        gain2,
        shift2,
        (cot_prompt[0], cot_conts[0, 0]),
        activated,
        slope,
        up_mat,
        down_turned,
    )
    result_prompt, result_cont, grad_second, part3, sums2, up_sum = results[:6]
    splits = results[6:]
    half = len(splits) // 2
    ffn_splits = splits[:half], splits[half:]
    grad_first, dout, sums1 = first_norm_backward(
        grad_second, part3, grid.over_tp(part3), norm1, inv1, gain1, output_turned
    )
    grad_prev, dq, dk, dv = attention_backward(
        queries, keys, values, dout, attended, probs_p, probs_c, cot_logits[0, 0], scale
    )
    ffn_shard = scatter_split(grid, *ffn_splits, after=dq).astype(f32)
    splits = weight_grads(
        grid, sizes[0], grad_first, attended, inputs_t, whole_t, dq, dk, dv, sums1, sums2, up_sum
    )
    splits, dq, dk, dv = lax.optimization_barrier((splits, dq, dk, dv))
    half = len(splits) // 2
    late_shard = scatter_split(grid, splits[:half], splits[half:]).astype(f32)

    from_query = contract_cols(dq, query_mat)
    from_keyvalue = contract_cols(dk, key_mat) + contract_cols(dv, value_mat)
    shared, own_cont = from_keyvalue[:full_len], from_keyvalue[full_len:]
    if sizes[1] == 2 and sizes[2] == 2:
        shared = shared.reshape(2, prompt_len, -1)
        abroad = pick(shared, 1 - grid.row, 0).astype(bf16).reshape(2, prompt_len // 2, -1)
        abroad_sum = add_low(
            pick(abroad, grid.core, 0), grid.over_tp(pick(abroad, 1 - grid.core, 0))
        )
        arrived = grid.over_ctx(abroad_sum).astype(f32)
        own = (pick(shared, grid.row, 0) + from_query[:prompt_len]).reshape(2, prompt_len // 2, -1)
        at = lax.broadcasted_iota(jnp.int32, (2, 1, 1), 0)
        own = own + jnp.where(at == grid.core, arrived[None], 0.0)
        own = own.reshape(prompt_len, -1)
    else:
        own = lax.psum_scatter(
            shared.astype(bf16), "ctx", scatter_dimension=0, tiled=True
        ).astype(f32)
        own = own + from_query[:prompt_len]
    partial = jnp.concatenate([own, own_cont + from_query[prompt_len:]], 0)
    input_grad = grad_first + grid.tp_sum(partial)

    table = late_shard[:, 4 * width :]
    table = jnp.concatenate([table[:, at : at + LANES] for at in range(0, table.shape[1], LANES)], 0)
    model = whole.shape[1]
    place = lax.axis_index("fsdp")
    at = 6 * (model // LANES)
    long_lines = table[:at].reshape(6, model)
    long_lines = lax.dynamic_slice_in_dim(long_lines, place * rows, rows, 1)
    shorts = []
    for bias in (query_bias, value_bias, up_bias):
        height, cols = bias.shape
        span = height * cols * sizes[0] // LANES
        block = table[at : at + span].reshape(height, -1)
        shorts.append(lax.dynamic_slice_in_dim(block, place * cols, cols, 1))
        at += span
    gain_one_grad, shift_one_grad, output_add_grad = long_lines[0], long_lines[1], long_lines[2]
    gain_two_grad, shift_two_grad, down_add_grad = long_lines[3], long_lines[4], long_lines[5]
    return (
        result_prompt[None],
        result_cont[None, None],
        new_logits[None, None],
        input_grad[:prompt_len][None],
        input_grad[prompt_len:][None, None],
        grad_prev[None, None],
        late_shard[:, width : 2 * width],
        shorts[0],
        late_shard[:, 2 * width : 3 * width],
        late_shard[:, 3 * width : 4 * width],
        shorts[1],
        late_shard[:, :width].T,
        output_add_grad,
        gain_one_grad,
        shift_one_grad,
        ffn_shard[:, :hidden],
        shorts[2],
        ffn_shard[:, hidden:].T,
        down_add_grad,
        gain_two_grad,
        shift_two_grad,
    )


def solution(mesh):
    sizes = tuple(mesh.shape[name] for name in ("fsdp", "ctx", "tp"))

    def step(*arrays):
        return per_device(sizes, *arrays)

    return jax.shard_map(
        step,
        mesh=mesh,
        in_specs=(
            P("fsdp", "ctx", None),
            P("fsdp", "ctx", None, None),
            P("fsdp", "ctx", "tp", None, None),
            P("fsdp", "ctx"),
            P("fsdp", "tp"),
            P("tp", "fsdp"),
            P("fsdp", "tp"),
            P("fsdp", "tp"),
            P("tp", "fsdp"),
            P("tp", "fsdp"),
            P("fsdp"),
            P("fsdp"),
            P("fsdp"),
            P("fsdp", "tp"),
            P("tp", "fsdp"),
            P("tp", "fsdp"),
            P("fsdp"),
            P("fsdp"),
            P("fsdp"),
            P("fsdp", "ctx", None),
            P("fsdp", "ctx", None, None),
            P("fsdp", "ctx", "tp", None, None),
        ),
        out_specs=(
            P("fsdp", "ctx", None),
            P("fsdp", "ctx", None, None),
            P("fsdp", "ctx", "tp", None, None),
            P("fsdp", "ctx", None),
            P("fsdp", "ctx", None, None),
            P("fsdp", "ctx", "tp", None, None),
            P("fsdp", "tp"),
            P("tp", "fsdp"),
            P("fsdp", "tp"),
            P("fsdp", "tp"),
            P("tp", "fsdp"),
            P("tp", "fsdp"),
            P("fsdp"),
            P("fsdp"),
            P("fsdp"),
            P("fsdp", "tp"),
            P("tp", "fsdp"),
            P("tp", "fsdp"),
            P("fsdp"),
            P("fsdp"),
            P("fsdp"),
        ),
        check_vma=False,
    )
```

```python
import math

import jax
import jax.numpy as jnp
from jax import lax
from jax.experimental import pallas as pl
from jax.experimental.pallas import tpu as pltpu
from jax.sharding import PartitionSpec as P

epsilon = 1e-06
f32 = jnp.float32
bf16 = jnp.bfloat16
LANES = 128


def product(left_mat, right_mat):
    return jnp.dot(left_mat, right_mat, preferred_element_type=f32)


def contract_rows(left_mat, right_mat):
    return lax.dot_general(
        left_mat, right_mat, (((0,), (0,)), ((), ())), preferred_element_type=f32
    )


def contract_cols(left_mat, right_mat):
    return lax.dot_general(
        left_mat, right_mat, (((1,), (1,)), ((), ())), preferred_element_type=f32
    )


class Grid:
    def __init__(self, sizes):
        self.fsdp, self.ctx, self.tp = sizes
        self.staged = sizes == (8, 2, 2)
        place = lax.axis_index("fsdp")
        self.outer, self.inner = place // 2, place % 2
        self.row = lax.axis_index("ctx")
        self.core = lax.axis_index("tp")
        self.place = jnp.stack([self.outer, self.inner, self.row, self.core]).astype(jnp.int32)

    def over_inner(self, array):
        return lax.ppermute(array, "fsdp", [(i, i ^ 1) for i in range(8)])

    def over_outer(self, array, step):
        return lax.ppermute(array, "fsdp", [(i, i ^ (2 * step)) for i in range(8)])

    def over_ctx(self, array):
        return lax.ppermute(array, "ctx", [(0, 1), (1, 0)])

    def over_tp(self, array):
        return lax.ppermute(array, "tp", [(0, 1), (1, 0)])

    def tp_sum(self, partial):
        low = partial.astype(bf16)
        return low.astype(f32) + self.over_tp(low).astype(f32)


def pack_early(grid, weights, vectors, tables):
    rows = weights[0].shape[0]
    edges = [sum(w.shape[1] for w in weights[:i]) for i in range(len(weights) + 1)]
    cols = edges[-1] + LANES
    count = len(weights)

    def body(place, *refs):
        out, half_out, lines = refs[-3:]
        for ref, low, high in zip(refs, edges, edges[1:]):
            out[:, low:high] = ref[...]
        lines[...] = jnp.zeros_like(lines)
        at = 0
        for ref in refs[count:-3]:
            height, width = ref.shape
            lines[at : at + height, :width] = ref[...].astype(f32)
            at += height
        out[:, edges[-1] :] = lines[...].astype(bf16)
        half_out[...] = out[pl.ds(pl.multiple_of(place[2] * (rows // 2), 16), rows // 2), :]

    vmem = pl.BlockSpec(memory_space=pltpu.VMEM)
    args = [*weights, *vectors, *tables]
    outs = [like((rows, cols), bf16), like((rows // 2, cols), bf16)]
    return pl.pallas_call(
        body,
        out_shape=outs,
        in_specs=[pl.BlockSpec(memory_space=pltpu.SMEM)] + [vmem] * len(args),
        out_specs=[vmem] * 2,
        scratch_shapes=[pltpu.VMEM((rows, LANES), f32)],
        cost_estimate=cost(0, *args, *outs),
        name="pack_early",
    )(grid.place, *args)


def pack_late(grid, shard, late):
    rows, head = shard.shape
    cols = sum(w.shape[1] for w in late)

    def body(place, early_ref, *refs):
        out, half_out = refs[-2:]
        out[:, :head] = early_ref[...]
        here = pl.ds(pl.multiple_of(place[2] * (rows // 2), 16), rows // 2)
        low = 0
        for ref in refs[:-2]:
            high = low + ref.shape[1]
            out[:, head + low : head + high] = ref[...]
            half_out[:, low:high] = ref[here, :]
            low = high

    vmem = pl.BlockSpec(memory_space=pltpu.VMEM)
    outs = [like((rows, head + cols), bf16), like((rows // 2, cols), bf16)]
    return pl.pallas_call(
        body,
        out_shape=outs,
        in_specs=[pl.BlockSpec(memory_space=pltpu.SMEM)] + [vmem] * (1 + len(late)),
        out_specs=[vmem] * 2,
        cost_estimate=cost(0, shard, *late, *outs),
        name="pack_late",
    )(grid.place, shard, *late)


def join(pieces):
    height, cols = pieces[0].shape

    def body(*refs):
        for i, ref in enumerate(refs[:-1]):
            refs[-1][i * height : (i + 1) * height, :] = ref[...]

    vmem = pl.BlockSpec(memory_space=pltpu.VMEM)
    out = like((len(pieces) * height, cols), pieces[0].dtype)
    return pl.pallas_call(
        body,
        out_shape=out,
        in_specs=[vmem] * len(pieces),
        out_specs=vmem,
        cost_estimate=cost(0, out, out),
        name="join",
    )(*pieces)


def assemble(grid, cuts, base, own, side, came, across, along):
    full = own.shape[0]
    half = full // 2
    edges = [sum(cuts[:i]) for i in range(len(cuts) + 1)]

    def body(place, own_ref, side_ref, came_ref, across_ref, along_ref, *outs):
        outer, inner, row = place[0], place[1], place[2]

        def put(ref, start, length, step, swap_inner, swap_row, skip=0):
            at = (outer ^ step) * 2 + (inner ^ swap_inner)
            if length == half:
                at = at * 2 + (row ^ swap_row)
            here = pl.ds(pl.multiple_of(at * length, 16), length)
            for out, low, high in zip(outs, edges, edges[1:]):
                out[here, :] = ref[start : start + length, skip + low : skip + high]

        put(own_ref, 0, full, 0, 0, 0, base)
        put(side_ref, 0, full, 0, 1, 0, base)
        for step in (1, 2, 3):
            start = (step - 1) * half
            put(came_ref, start, half, step, 0, 0)
            put(across_ref, start, half, step, 1, 0)
            put(along_ref, start, half, step, 0, 1)
            for out in outs:
                at = (((outer ^ step) * 2 + (inner ^ 1)) * 2 + (row ^ 1)) * half
                out[pl.ds(pl.multiple_of(at, 16), half), :] = jnp.zeros((half, out.shape[1]), bf16)

    vmem = pl.BlockSpec(memory_space=pltpu.VMEM)
    outs = [like((8 * full, cols), own.dtype) for cols in cuts]
    return pl.pallas_call(
        body,
        out_shape=outs,
        in_specs=[pl.BlockSpec(memory_space=pltpu.SMEM)] + [vmem] * 5,
        out_specs=[vmem] * len(outs),
        compiler_params=pltpu.CompilerParams(vmem_limit_bytes=VMEM_LIMIT),
        cost_estimate=cost(0, *outs, *outs),
        name="assemble",
    )(grid.place, own, side, came, across, along)


def complete(grid, arrays, far_one, far_two):
    half = far_one.shape[0] // 3
    first = 0
    while sum(a.shape[1] for a in arrays[: first + 1]) <= far_one.shape[1]:
        first += 1
    count = len(arrays)
    copies = 3 * count

    def body(place, one_ref, two_ref, *refs):
        outs, sems = refs[count : 2 * count], refs[2 * count]
        outer, inner, row = place[0], place[1], place[2]
        started = []
        low = 0
        for i, out in enumerate(outs):
            ref = one_ref if i < first else two_ref
            if i == first:
                low = 0
            cols = out.shape[1]
            for step in (1, 2, 3):
                at = (((outer ^ step) * 2 + (inner ^ 1)) * 2 + (row ^ 1)) * half
                copy = pltpu.make_async_copy(
                    ref.at[(step - 1) * half : step * half, low : low + cols],
                    out.at[pl.ds(pl.multiple_of(at, 16), half), :],
                    sems.at[len(started)],
                )
                copy.start()
                started.append(copy)
            low += cols
        for copy in started:
            copy.wait()

    vmem = pl.BlockSpec(memory_space=pltpu.VMEM)
    anywhere = pl.BlockSpec(memory_space=pl.ANY)
    return pl.pallas_call(
        body,
        out_shape=[like(a.shape, a.dtype) for a in arrays],
        in_specs=[pl.BlockSpec(memory_space=pltpu.SMEM), vmem, vmem] + [anywhere] * count,
        out_specs=[anywhere] * count,
        scratch_shapes=[pltpu.SemaphoreType.DMA((copies,))],
        input_output_aliases={3 + i: i for i in range(count)},
        cost_estimate=cost(0, far_one, far_two, far_one, far_two),
        name="complete",
    )(grid.place, far_one, far_two, *arrays)


def lines_of(grid, mine):
    return [grid.over_outer(mine, step) for step in (1, 2, 3)]


def pairs_of(grid, came):
    return grid.over_inner(came), grid.over_ctx(came)


def corners_of(grid, across, along, cut):
    return grid.over_ctx(across[:, :cut]), grid.over_inner(along[:, cut:])


def pick(array, at, axis):
    return lax.dynamic_index_in_dim(array, at, axis, keepdims=False)


def add_low(left, right):
    return (left.astype(f32) + right.astype(f32)).astype(bf16)


VMEM_LIMIT = 60 * 1024 * 1024


def whole_block(array):
    rank = array.ndim
    return pl.BlockSpec(array.shape, lambda *_: (0,) * rank)


def cost(flops, *arrays, transcendentals=0):
    return pl.CostEstimate(flops=10**13, transcendentals=0, bytes_accessed=1)


def after(values, *earlier):
    return lax.optimization_barrier((values, earlier))[0]


def like(shape, dtype):
    return jax.ShapeDtypeStruct(shape, dtype)


def norm_rows(hidden_in):
    centre = jnp.mean(hidden_in, axis=-1, keepdims=True)
    shifted = hidden_in - centre
    spread = jnp.mean(shifted * shifted, axis=-1, keepdims=True)
    inverse = lax.rsqrt(spread + epsilon)
    return shifted * inverse, inverse


def norm_pull(upstream, normed, inverse, gain):
    scaled = upstream * gain
    mean_one = jnp.mean(scaled, axis=-1, keepdims=True)
    mean_two = jnp.mean(scaled * normed, axis=-1, keepdims=True)
    return inverse * (scaled - mean_one - normed * mean_two)


def column_sums(values):
    return jnp.sum(values, axis=0, keepdims=True)


def row_tile(rows):
    return 256 if rows % 256 == 0 else rows


def first_norm(prompt, conts, part, other, output_add, gain, shift):
    prompt_len, width = prompt.shape
    rows = prompt_len + conts.shape[0]
    tile = row_tile(prompt_len)
    ahead = prompt_len // tile

    def body(x, c, p, o, b, g, s, norm_out, inv_out, low_out, turned_out):
        rows_in = jnp.where(pl.program_id(0) < ahead, x[...].astype(f32), c[...].astype(f32))
        normed, inverse = norm_rows(rows_in + (p[...].astype(f32) + o[...].astype(f32)) + b[...])
        norm_out[...] = normed
        inv_out[...] = jnp.broadcast_to(inverse, inv_out.shape)
        value = normed * g[...] + s[...]
        low_out[...] = value.astype(bf16)
        turned_out[...] = value.T.astype(bf16)

    def tiled(array):
        return pl.BlockSpec((tile, array.shape[1]), lambda i: (i, 0))

    args = [prompt, conts, part, other, output_add, gain, shift]
    outs = [
        like((rows, width), f32),
        like((rows, LANES), f32),
        like((rows, width), bf16),
        like((width, rows), bf16),
    ]
    return pl.pallas_call(
        body,
        grid=(rows // tile,),
        out_shape=outs,
        in_specs=[
            pl.BlockSpec((tile, width), lambda i: (jnp.minimum(i, ahead - 1), 0)),
            pl.BlockSpec((tile, width), lambda i: (jnp.maximum(i - ahead, 0), 0)),
        ]
        + [tiled(a) for a in args[2:4]]
        + [whole_block(a) for a in args[4:]],
        out_specs=[tiled(a) for a in outs[:3]] + [pl.BlockSpec((width, tile), lambda i: (0, i))],
        compiler_params=pltpu.CompilerParams(vmem_limit_bytes=VMEM_LIMIT),
        cost_estimate=cost(0, *args, *outs),
        name="first_norm",
    )(*args)


def ffn_forward(low, up_mat, up_add, down_turned):
    rows, width = low.shape
    hidden = up_mat.shape[1]
    tile = row_tile(rows)

    def body(x, up, ub, dn, act_out, slope_out, part_out):
        inner = product(x[...], up[...]) + ub[...]
        normal_cdf = 0.5 * (1.0 + lax.erf(inner * math.sqrt(0.5)))
        act = (inner * normal_cdf).astype(bf16)
        act_out[...] = act
        density = jnp.exp(-0.5 * inner * inner) * (1.0 / math.sqrt(2.0 * math.pi))
        slope_out[...] = (normal_cdf + inner * density).astype(bf16)
        part_out[...] = contract_cols(act, dn[...]).astype(bf16)

    outs = [
        like((rows, hidden), bf16),
        like((rows, hidden), bf16),
        like((rows, width), bf16),
    ]

    def tiled(array):
        return pl.BlockSpec((tile, array.shape[1]), lambda i: (i, 0))

    args = [low, up_mat, up_add, down_turned]
    return pl.pallas_call(
        body,
        grid=(rows // tile,),
        out_shape=outs,
        in_specs=[tiled(low)] + [whole_block(a) for a in args[1:]],
        out_specs=[tiled(a) for a in outs],
        compiler_params=pltpu.CompilerParams(vmem_limit_bytes=VMEM_LIMIT),
        cost_estimate=cost(4 * rows * width * hidden, *args, *outs, transcendentals=2 * rows * hidden),
        name="ffn_forward",
    )(*args)


def split_out(grid, length, cols):
    if grid.staged:
        return [like((length // 2, cols), bf16), like((length // 2, cols), bf16)]
    return [like((length, cols), bf16)]


def store_split(grid, place, full_ref, outs, over_inner):
    if not grid.staged:
        outs[0][...] = full_ref[...]
        return
    half = full_ref.shape[0] // 16
    for out, flip in zip(outs, (0, 1)):
        if over_inner:
            for outer in range(4):
                at = pl.multiple_of((2 * outer + (place[1] ^ flip)) * (2 * half), 32)
                out[2 * half * outer : 2 * half * (outer + 1), :] = full_ref[pl.ds(at, 2 * half), :]
        else:
            for block in range(8):
                at = pl.multiple_of((2 * block + (place[2] ^ flip)) * half, 16)
                out[half * block : half * (block + 1), :] = full_ref[pl.ds(at, half), :]


def ffn_backward(grid, norm1, turned1, gain1, shift1, part, other, down_add, gain2, shift2, cots, act, slope, up_mat, down_turned):
    rows, width = norm1.shape
    hidden = up_mat.shape[1]
    tile = 256
    chunk = row_tile(rows)
    prompt_len = cots[0].shape[0]
    count = 2 if grid.staged else 1

    def body(place, n1, x1_t, g1, s1, p, o, db, g2, s2, cp, cc, u, sl, up, dn, *rest):
        outs, scratch = rest[:-5], rest[-5:]
        y_p, y_c, dh2, dx1, sums, up_sum = outs[:6]
        up_outs, down_outs = outs[6 : 6 + count], outs[6 + count :]
        df, df_t, acc, full_up, full_down = scratch
        step = pl.program_id(0)

        @pl.when(step == 0)
        def _():
            total = [jnp.zeros((1, width), f32) for _ in range(3)]
            for at in range(0, rows, chunk):
                here = slice(at, at + chunk)
                first = n1[here, :] * g1[...] + s1[...]
                second = first + (p[here, :].astype(f32) + o[here, :].astype(f32)) + db[...]
                normed, inverse = norm_rows(second)
                result = (normed * g2[...] + s2[...]).astype(bf16)
                if at < prompt_len:
                    y_p[here, :] = result
                    cot = cp[here, :].astype(f32)
                else:
                    there = slice(at - prompt_len, at - prompt_len + chunk)
                    y_c[there, :] = result
                    cot = cc[there, :].astype(f32)
                grad = norm_pull(cot, normed, inverse, g2[...])
                dh2[here, :] = grad
                low = grad.astype(bf16)
                df[here, :] = low
                wide = low.astype(f32)
                df_t[:, here] = wide.T.astype(bf16)
                total[0] += column_sums(cot * normed)
                total[1] += column_sums(cot)
                total[2] += column_sums(wide)
            sums[...] = jnp.zeros(sums.shape, f32)
            for i in range(3):
                sums[i : i + 1, :] = total[i]
            acc[...] = jnp.zeros_like(acc)

        inner = (product(df[...], dn[...]) * sl[...].astype(f32)).astype(bf16)
        up_sum[...] = jnp.broadcast_to(column_sums(inner.astype(f32)), up_sum.shape)
        full_up[...] = product(x1_t[...], inner).astype(bf16)
        full_down[...] = product(df_t[...], u[...]).astype(bf16)
        acc[...] += contract_cols(inner, up[...])
        store_split(grid, place, full_up, up_outs, True)
        store_split(grid, place, full_down, down_outs, False)

        @pl.when(step == hidden // tile - 1)
        def _():
            dx1[...] = acc[...].astype(bf16)

    def tiled(array):
        return pl.BlockSpec((array.shape[0], tile), lambda j: (0, j))

    fixed = [norm1, turned1, gain1, shift1, part, other, down_add, gain2, shift2, *cots]
    moving = [act, slope, up_mat, down_turned]
    outs = [
        like((prompt_len, width), bf16),
        like((rows - prompt_len, width), bf16),
        like((rows, width), f32),
        like((rows, width), bf16),
        like((8, width), f32),
        like((8, hidden), f32),
    ]
    grads = split_out(grid, width, hidden) * 2
    return pl.pallas_call(
        body,
        grid=(hidden // tile,),
        out_shape=outs + grads,
        in_specs=[pl.BlockSpec(memory_space=pltpu.SMEM)]
        + [whole_block(a) for a in fixed]
        + [tiled(a) for a in moving],
        out_specs=[whole_block(a) for a in outs[:5]] + [tiled(a) for a in outs[5:] + grads],
        scratch_shapes=[
            pltpu.VMEM((rows, width), bf16),
            pltpu.VMEM((width, rows), bf16),
            pltpu.VMEM((rows, width), f32),
            pltpu.VMEM((width, tile), bf16),
            pltpu.VMEM((width, tile), bf16),
        ],
        compiler_params=pltpu.CompilerParams(vmem_limit_bytes=VMEM_LIMIT),
        cost_estimate=cost(8 * rows * width * hidden, *fixed, *moving, *outs, *grads),
        name="ffn_backward",
    )(grid.place, *fixed, *moving)


def fold_pair(grid, firsts, seconds):
    half = firsts[0][0].shape[0] // 8
    outs = []
    for group in (firsts, seconds):
        outs += [like((4 * half, sum(kept.shape[1] for kept, _ in group)), bf16)] * 2

    def body(place, *refs):
        pairs, outs = refs[:-4], refs[-4:]
        at_pair = 0
        for group, mine, (keep, send) in (
            (firsts, place[2], outs[:2]),
            (seconds, place[1], outs[2:]),
        ):
            low = 0
            for _ in group:
                kept, came = pairs[at_pair : at_pair + 2]
                at_pair += 2
                high = low + kept.shape[1]
                for out, flip in ((send, 1), (keep, 0)):
                    for outer in range(4):
                        here = pl.ds(pl.multiple_of((2 * outer + (mine ^ flip)) * half, 16), half)
                        out[outer * half : (outer + 1) * half, low:high] = (
                            kept[here, :].astype(f32) + came[here, :].astype(f32)
                        ).astype(bf16)
                low = high

    vmem = pl.BlockSpec(memory_space=pltpu.VMEM)
    args = [a for group in (firsts, seconds) for pair in group for a in pair]
    return pl.pallas_call(
        body,
        out_shape=outs,
        in_specs=[pl.BlockSpec(memory_space=pltpu.SMEM)] + [vmem] * len(args),
        out_specs=[vmem] * 4,
        compiler_params=pltpu.CompilerParams(vmem_limit_bytes=VMEM_LIMIT),
        cost_estimate=cost(0, *args, *outs),
        name="fold_pair",
    )(grid.place, *args)


def fold_line(grid, first, second):
    half = first[0].shape[0] // 4
    left, right = first[0].shape[1], second[0].shape[1]
    outs = [like((half, left + right), f32)] + [like((half, left + right), bf16)] * 3

    def body(place, fk, fa, sk, sa, *out_refs):
        for step, out in enumerate(out_refs):
            here = pl.ds(pl.multiple_of((place[0] ^ step) * half, 16), half)
            out[:, :left] = (fk[here, :].astype(f32) + fa[here, :].astype(f32)).astype(out.dtype)
            out[:, left:] = (sk[here, :].astype(f32) + sa[here, :].astype(f32)).astype(out.dtype)

    vmem = pl.BlockSpec(memory_space=pltpu.VMEM)
    args = [*first, *second]
    return pl.pallas_call(
        body,
        out_shape=outs,
        in_specs=[pl.BlockSpec(memory_space=pltpu.SMEM)] + [vmem] * 4,
        out_specs=[vmem] * 4,
        cost_estimate=cost(0, *args, *outs),
        name="fold_line",
    )(grid.place, *args)


class Reduction:
    def __init__(self, grid, firsts, seconds):
        self.grid, self.firsts, self.seconds = grid, firsts, seconds
        if grid.staged:
            self.came = [
                [grid.over_inner(g[1]) for g in firsts],
                [grid.over_ctx(g[1]) for g in seconds],
            ]

    def fold(self, *earlier):
        if not self.grid.staged:
            return ()
        grid = self.grid
        came = after(self.came, *earlier)
        folded = fold_pair(
            grid,
            [(g[0], c) for g, c in zip(self.firsts, came[0])],
            [(g[0], c) for g, c in zip(self.seconds, came[1])],
        )
        f_keep, f_send, s_keep, s_send = folded
        self.kept = f_keep, s_keep
        self.came = grid.over_ctx(f_send), grid.over_inner(s_send)
        return folded

    def line(self, *earlier):
        if not self.grid.staged:
            return ()
        came = after(self.came, *earlier)
        self.total, *sent = fold_line(self.grid, (self.kept[0], came[0]), (self.kept[1], came[1]))
        self.came = [self.grid.over_outer(sent[step - 1], step) for step in (1, 2, 3)]
        return sent

    def shard(self, *earlier):
        grid = self.grid
        if not grid.staged:
            both = jnp.concatenate([g[0] for g in self.firsts + self.seconds], 1)
            both = lax.psum_scatter(both, "fsdp", scatter_dimension=0, tiled=True)
            return lax.psum(both, "ctx").astype(f32)
        came = after(self.came, *earlier)
        total = self.total
        for piece in came:
            total = total + piece.astype(f32)
        total = total.astype(bf16)
        other = grid.over_ctx(total)
        low = jnp.where(grid.row == 0, total, other)
        high = jnp.where(grid.row == 0, other, total)
        return jnp.concatenate([low, high], 0).astype(f32)


def columns_of(shard, widths):
    edges = [sum(widths[:i]) for i in range(len(widths) + 1)]
    return [shard[:, low:high] for low, high in zip(edges, edges[1:])]


def head_lanes(shape, index):
    lane = lax.broadcasted_iota(jnp.int32, shape, 1)
    return (lane < LANES // 2) if index == 0 else (lane >= LANES // 2)


def each_chunk(rows_at, prompt_len, rows, chunk):
    @pl.loop(0, prompt_len // chunk)
    def _(i):
        rows_at(pl.multiple_of(i * chunk, chunk), True)

    for at in range(prompt_len, rows, chunk):
        rows_at(at, False)


def attention_forward(queries, keys, values, prev_logits, cont_len, prompt_len, pairs, held=()):
    begin, end = pairs
    kept = len(held)
    rows, width = queries.shape
    total = keys.shape[0]
    cont_size = rows - prompt_len
    full_len = total - cont_size
    heads = prev_logits.shape[0]
    chunk = row_tile(prompt_len)

    def body(length, q, k, v, prev, *refs):
        logits, probs_p, probs_c, out = refs[kept:]

        def soft(scores):
            weights = jnp.exp(scores - jnp.max(scores, axis=-1, keepdims=True))
            return (weights * (1.0 / jnp.sum(weights, axis=-1, keepdims=True))).astype(bf16)

        column = lax.broadcasted_iota(jnp.int32, (1, total), 1)
        live = column < full_len + length[0, 0]
        def rows_at(at, in_prompt):
            here = pl.ds(at, chunk)
            halves = []
            for head in range(2):
                one = jnp.where(head_lanes((chunk, LANES), head), q[here, :], 0)
                if in_prompt:
                    probs = soft(contract_cols(one, k[:full_len, :]))
                    probs_p[head, here, :] = probs
                    halves.append(product(probs, v[:full_len, :]))
                else:
                    there = slice(at - prompt_len, at - prompt_len + chunk)
                    raw = prev[head, there, :].astype(f32) + contract_cols(one, k[...])
                    logits[head, there, :] = raw.astype(bf16)
                    probs = soft(jnp.where(live, raw, -1e30))
                    probs_c[head, there, :] = probs
                    halves.append(product(probs, v[...]))
            first = head_lanes((chunk, LANES), 0)
            out[here, :] = jnp.where(first, halves[0], halves[1]).astype(bf16)

        each_chunk(rows_at, prompt_len, rows, chunk)

    outs = [
        like((heads, cont_size, total), bf16),
        like((heads, prompt_len, full_len), bf16),
        like((heads, cont_size, total), bf16),
        like((rows, width), bf16),
    ]

    def columns(array):
        return pl.BlockSpec((array.shape[0], LANES), lambda i: (0, begin + i))

    def pair_of(array):
        return pl.BlockSpec((2,) + array.shape[1:], lambda i: (begin + i, 0, 0))

    args = [queries, keys, values, prev_logits]
    scores = heads * (prompt_len * full_len + cont_size * total)
    return pl.pallas_call(
        body,
        grid=(end - begin,),
        out_shape=outs,
        in_specs=[pl.BlockSpec(memory_space=pltpu.SMEM)]
        + [columns(a) for a in args[:3]]
        + [pair_of(prev_logits)]
        + [pl.BlockSpec(memory_space=pl.ANY)] * kept,
        out_specs=[pair_of(a) for a in outs[:3]] + [columns(outs[3])],
        compiler_params=pltpu.CompilerParams(vmem_limit_bytes=VMEM_LIMIT),
        input_output_aliases={5 + i: i for i in range(kept)},
        cost_estimate=cost((end - begin) * 256 * scores, *args, transcendentals=scores),
        name="attention_forward",
    )(cont_len, *args, *held)


def attention_backward(queries, keys, values, dout, attended, probs_p, probs_c, cots, scale):
    rows, width = queries.shape
    total = keys.shape[0]
    heads, prompt_len, full_len = probs_p.shape
    cont_size = rows - prompt_len
    chunk = row_tile(prompt_len)

    def body(q, k, v, do, o, pp, pc, cot, prev_out, dq, dk, dv, acc_k, acc_v):
        acc_k[...] = jnp.zeros_like(acc_k)
        acc_v[...] = jnp.zeros_like(acc_v)
        def rows_at(at, in_prompt):
            here = pl.ds(at, chunk)
            grads = []
            for head in range(2):
                mine = head_lanes((chunk, LANES), head)
                one_q = jnp.where(mine, q[here, :], 0)
                one_do = jnp.where(mine, do[here, :], 0)
                delta = jnp.sum(
                    one_do.astype(f32) * o[here, :].astype(f32), axis=-1, keepdims=True
                )
                if in_prompt:
                    span = full_len
                    probs = pp[head, here, :]
                    dprob = contract_cols(one_do, v[:span, :])
                    dscore = (probs.astype(f32) * (dprob - delta)).astype(bf16)
                else:
                    span = total
                    there = slice(at - prompt_len, at - prompt_len + chunk)
                    probs = pc[head, there, :]
                    dprob = contract_cols(one_do, v[...])
                    dscore = (
                        probs.astype(f32) * (dprob - delta) + cot[head, there, :].astype(f32)
                    ).astype(bf16)
                    prev_out[head, there, :] = dscore
                grads.append(product(dscore, k[:span, :]))
                acc_k[:span, :] += contract_rows(dscore, one_q)
                acc_v[:span, :] += contract_rows(probs, one_do)
            first = head_lanes((chunk, LANES), 0)
            dq[here, :] = (jnp.where(first, grads[0], grads[1]) * scale).astype(bf16)

        each_chunk(rows_at, prompt_len, rows, chunk)
        dk[...] = acc_k[...].astype(bf16)
        dv[...] = acc_v[...].astype(bf16)

    outs = [
        like((heads, cont_size, total), bf16),
        like((rows, width), bf16),
        like((total, width), bf16),
        like((total, width), bf16),
    ]

    def columns(array):
        return pl.BlockSpec((array.shape[0], LANES), lambda i: (0, i))

    def pairs(array):
        return pl.BlockSpec((2,) + array.shape[1:], lambda i: (i, 0, 0))

    args = [queries, keys, values, dout, attended, probs_p, probs_c, cots]
    scores = heads * (prompt_len * full_len + cont_size * total)
    return pl.pallas_call(
        body,
        grid=(heads // 2,),
        out_shape=outs,
        in_specs=[columns(a) for a in args[:5]] + [pairs(a) for a in args[5:]],
        out_specs=[pairs(outs[0])] + [columns(a) for a in outs[1:]],
        scratch_shapes=[pltpu.VMEM((total, LANES), f32), pltpu.VMEM((total, LANES), f32)],
        compiler_params=pltpu.CompilerParams(vmem_limit_bytes=VMEM_LIMIT),
        cost_estimate=cost(1024 * scores, *args, *outs),
        name="attention_backward",
    )(*args)


def first_norm_backward(grad_second, part, other, norm1, inv1, gain1, output_turned):
    rows, width = grad_second.shape
    tile = row_tile(rows)

    def body(d2, p, o, n1, r1, g1, ot, dh1, dout, sums):
        @pl.when(pl.program_id(0) == 0)
        def _():
            sums[...] = jnp.zeros_like(sums)

        upstream = d2[...] + (p[...].astype(f32) + o[...].astype(f32))
        normed = n1[...]
        grad = norm_pull(upstream, normed, r1[:, :1], g1[...])
        dh1[...] = grad
        low = grad.astype(bf16)
        dout[...] = product(low, ot[...]).astype(bf16)
        sums[0:1, :] += column_sums(upstream * normed)
        sums[1:2, :] += column_sums(upstream)
        sums[2:3, :] += column_sums(low.astype(f32))

    def tiled(array):
        return pl.BlockSpec((tile, array.shape[1]), lambda i: (i, 0))

    args = [grad_second, part, other, norm1, inv1, gain1, output_turned]
    outs = [
        like((rows, width), f32),
        like((rows, output_turned.shape[1]), bf16),
        like((8, width), f32),
    ]
    return pl.pallas_call(
        body,
        grid=(rows // tile,),
        out_shape=outs,
        in_specs=[tiled(a) for a in args[:5]] + [whole_block(a) for a in args[5:]],
        out_specs=[tiled(a) for a in outs[:2]] + [whole_block(outs[2])],
        compiler_params=pltpu.CompilerParams(vmem_limit_bytes=VMEM_LIMIT),
        cost_estimate=cost(2 * rows * width * output_turned.shape[1], *args, *outs),
        name="first_norm_backward",
    )(*args)


def input_pull(grid, dq, dk, dv, query_mat, key_mat, value_mat, prompt_len):
    rows, width = dq.shape[0], query_mat.shape[0]
    half = prompt_len // 2
    tile = half
    full_len = 2 * prompt_len

    def body(place, q, k, v, qm, km, vm, own, keep, low):
        def pull(at):
            here = pl.ds(pl.multiple_of(at, tile), tile)
            return contract_cols(k[here, :], km[...]) + contract_cols(v[here, :], vm[...])

        for at in range(0, rows, tile):
            source = place[2] * prompt_len + at if at < prompt_len else at - prompt_len + full_len
            value = contract_cols(q[at : at + tile, :], qm[...]) + pull(source)
            own[at : at + tile, :] = value
            low[at : at + tile, :] = value.astype(bf16)
        abroad = (1 - place[2]) * prompt_len
        keep[...] = pull(abroad + place[3] * half).astype(bf16)
        low[rows:, :] = pull(abroad + (1 - place[3]) * half).astype(bf16)

    args = [dq, dk, dv, query_mat, key_mat, value_mat]
    vmem = pl.BlockSpec(memory_space=pltpu.VMEM)
    return pl.pallas_call(
        body,
        out_shape=[like((rows, width), f32), like((half, width), bf16), like((rows + half, width), bf16)],
        in_specs=[pl.BlockSpec(memory_space=pltpu.SMEM)] + [vmem] * len(args),
        out_specs=[vmem] * 3,
        compiler_params=pltpu.CompilerParams(vmem_limit_bytes=VMEM_LIMIT),
        cost_estimate=cost(0, *args),
        name="input_pull",
    )(grid.place, *args)


def weight_grads(grid, shards, grad_first, attended, inputs_t, whole_t, dq, dk, dv, sums1, sums2, up_sum):
    width, part = inputs_t.shape[0], dq.shape[1]
    hidden = up_sum.shape[1]
    count = 2 if grid.staged else 1
    block = width // shards
    sides = pl.cdiv((6 * width + 2 * part + hidden) // LANES, block)
    extra = sides * LANES
    widths = [part, part, part, part, extra]

    def body(place, d1, o, xt, wt, q, k, v, s1, s2, us, *rest):
        firsts, seconds = rest[:count], rest[count : 2 * count]
        full_a, full_b = rest[2 * count :]
        turned = d1[...].T.astype(bf16)
        full_a[:, :part] = product(turned, o[...]).astype(bf16)
        full_a[:, part:] = product(xt[...], q[...]).astype(bf16)
        full_b[:, :part] = product(wt[...], k[...]).astype(bf16)
        wide = 2 * part
        full_b[:, part:wide] = product(wt[...], v[...]).astype(bf16)
        lines = [(s1, i) for i in range(3)] + [(s2, i) for i in range(3)]
        pieces = []
        for ref, i in lines:
            pieces += [ref[i : i + 1, at : at + LANES] for at in range(0, width, LANES)]
        for sums in (column_sums(q[...].astype(f32)), column_sums(v[...].astype(f32))):
            pieces += [sums[:, at : at + LANES] for at in range(0, part, LANES)]
        pieces += [us[0:1, at : at + LANES] for at in range(0, hidden, LANES)]
        pieces.append(jnp.zeros((sides * block - len(pieces), LANES), f32))
        table = jnp.concatenate(pieces, 0).astype(bf16)
        for shard in range(shards):
            for side in range(sides):
                low = wide + side * LANES
                full_b[shard * block : (shard + 1) * block, low : low + LANES] = table[
                    side * block : (side + 1) * block
                ]
        store_split(grid, place, full_a, firsts, True)
        store_split(grid, place, full_b, seconds, False)

    args = [grad_first, attended, inputs_t, whole_t, dq, dk, dv, sums1, sums2, up_sum]
    outs = split_out(grid, width, 2 * part) + split_out(grid, width, sum(widths[2:]))
    vmem = pl.BlockSpec(memory_space=pltpu.VMEM)
    outs = pl.pallas_call(
        body,
        out_shape=outs,
        in_specs=[pl.BlockSpec(memory_space=pltpu.SMEM)] + [vmem] * len(args),
        out_specs=[vmem] * len(outs),
        scratch_shapes=[
            pltpu.VMEM((width, 2 * part), bf16),
            pltpu.VMEM((width, sum(widths[2:])), bf16),
        ],
        compiler_params=pltpu.CompilerParams(vmem_limit_bytes=VMEM_LIMIT),
        cost_estimate=cost(0, *args, *outs),
        name="weight_grads",
    )(grid.place, *args)
    return outs[:count], outs[count:], widths


def unpack_small(grid, packed, heads, head_size, up_rows):
    width = packed.shape[0]
    shards = grid.fsdp
    block, per_head, per_up = width // shards, head_size // shards, LANES // shards

    def body(packed_ref, lines, query_out, value_out, up_out):
        source = lax.broadcasted_iota(jnp.int32, (LANES, width), 0)
        target = lax.broadcasted_iota(jnp.int32, (LANES, width), 1)
        whole = jnp.zeros((32, width), f32)
        by_head = jnp.zeros((32, LANES), f32)
        by_up = jnp.zeros((32, LANES), f32)
        near, far = source[:, :LANES], target[:, :LANES]
        for shard in range(shards):
            piece = packed_ref[shard * block : shard * block + 32, :]
            put = (target - source == shard * block) & (source < block)
            whole += product(piece, put.astype(bf16))
            place = shard * per_head
            shift = far - near
            put = ((shift == place) | (shift == place + head_size)) & (near < per_head)
            by_head += product(piece, put.astype(bf16))
            put = (shift == shard * per_up) & (near < per_up)
            by_up += product(piece, put.astype(bf16))
        lines[...] = whole[:8, :]
        low = lax.broadcasted_iota(jnp.int32, (1, LANES), 1) < head_size
        for pair in range(heads // 2):
            at = slice(pair * LANES, (pair + 1) * LANES)
            for out, base in ((query_out, 6), (value_out, 6 + heads)):
                row = base + 2 * pair
                out[:, at] = jnp.where(low, by_head[row : row + 1, :], by_head[row + 1 : row + 2, :])
        for i in range(up_rows):
            row = 6 + 2 * heads + i
            up_out[:, i * LANES : (i + 1) * LANES] = by_up[row : row + 1, :]

    outs = [
        like((8, width), f32),
        like((1, heads * head_size), f32),
        like((1, heads * head_size), f32),
        like((1, up_rows * LANES), f32),
    ]
    vmem = pl.BlockSpec(memory_space=pltpu.VMEM)
    return pl.pallas_call(
        body,
        out_shape=outs,
        in_specs=[vmem],
        out_specs=[vmem] * 4,
        cost_estimate=cost(0, packed, *outs),
        name="unpack_small",
    )(packed)


def per_device(
    sizes,
    prompt,
    continuations,
    prev_logits,
    cont_len,
    query_weight,
    query_bias,
    key_weight,
    value_weight,
    value_bias,
    output_weight,
    output_bias,
    first_gain,
    first_shift,
    up_weight,
    up_bias,
    down_weight,
    down_bias,
    second_gain,
    second_shift,
    cot_prompt,
    cot_conts,
    cot_logits,
):
    grid = Grid(sizes)
    rows = query_weight.shape[0]
    width = query_weight.shape[1]
    hidden = up_weight.shape[1]
    prompt_len = prompt.shape[1]
    cont_size = continuations.shape[2]
    head_count = query_bias.shape[0]
    head_size = width // head_count
    scale = 1.0 / math.sqrt(head_size)

    mine, conts = prompt[0], continuations[0, 0]
    lines = [v[None] for v in (output_bias, first_gain, first_shift, down_bias, second_gain, second_shift)]
    tables = [query_bias, value_bias, up_bias]
    early = [query_weight, key_weight, value_weight, output_weight.T]
    late = [up_weight, down_weight.T]
    shard, half_shard = pack_early(grid, early, lines, tables)
    cuts = [width, width, width, width, LANES]
    cut = 2 * width
    if grid.staged:
        came = lines_of(grid, half_shard)
        sent, shard = lax.optimization_barrier((mine, shard))
        theirs = grid.over_ctx(sent)
        shards, late_half = pack_late(grid, shard, late)
        side = grid.over_inner(shards)
        came, late_half, theirs = lax.optimization_barrier((came, late_half, theirs))
        came = join(came)
        across, along = pairs_of(grid, came)
        far = corners_of(grid, across, along, cut)
        late_came = lines_of(grid, late_half)
        far, late_came = lax.optimization_barrier((far, late_came))
        early = complete(
            grid, assemble(grid, cuts, 0, shards, side, came, across, along), *far
        )
        late_came = join(late_came)
        late_across, late_along = pairs_of(grid, late_came)
    else:
        shards = [shard] + late
        shards = [lax.all_gather(a, "fsdp", axis=0, tiled=True) for a in shards]
        edges = [sum(cuts[:i]) for i in range(len(cuts) + 1)]
        early = [shards[0][:, low:high] for low, high in zip(edges, edges[1:])]
        late = shards[1:]
    query_mat, key_mat, value_mat, output_turned, small = early
    vectors, query_add, value_add, up_line = unpack_small(
        grid, small, head_count, head_size, up_bias.shape[0]
    )
    output_line, gain1, shift1, down_line, gain2, shift2 = [vectors[i : i + 1] for i in range(6)]

    inputs = jnp.concatenate([mine, conts], 0)
    if sizes[1] == 2:
        if not grid.staged:
            theirs = grid.over_ctx(mine)
        whole = jnp.concatenate(
            [jnp.where(grid.row == 0, mine, theirs), jnp.where(grid.row == 0, theirs, mine), conts], 0
        )
    else:
        whole = jnp.concatenate([lax.all_gather(mine, "ctx", axis=0, tiled=True), conts], 0)
    full_len = whole.shape[0] - cont_size
    whole_t, inputs_t = whole.T, inputs.T

    queries = ((product(inputs, query_mat) + query_add) * scale).astype(bf16)
    keys = product(whole, key_mat).astype(bf16)
    values = (product(whole, value_mat) + value_add).astype(bf16)
    queries, whole_t, inputs_t = lax.optimization_barrier((queries, whole_t, inputs_t))
    attention = (queries, keys, values, prev_logits[0, 0], cont_len, prompt_len)
    pair_count = head_count // 2
    held = attention_forward(*attention, (0, pair_count - 1))
    if grid.staged:
        late_across, late_along, held = lax.optimization_barrier((late_across, late_along, held))
        far = corners_of(grid, late_across, late_along, hidden)
    new_logits, probs_p, probs_c, attended = attention_forward(
        *attention, (pair_count - 1, pair_count), held
    )
    if grid.staged:
        late = assemble(
            grid, [hidden, hidden], sum(cuts), shards, side, late_came, late_across, late_along
        )
    part = contract_cols(attended, output_turned).astype(bf16)
    norm1, inv1, low1, turned1 = first_norm(
        mine, conts, part, grid.over_tp(part), output_line, gain1, shift1
    )
    if grid.staged:
        late = complete(grid, late, *far)
    up_mat, down_turned = late
    activated, slope, part2 = ffn_forward(low1, up_mat, up_line, down_turned)
    results = ffn_backward(
        grid,
        norm1,
        turned1,
        gain1,
        shift1,
        part2,
        grid.over_tp(part2),
        down_line,
        gain2,
        shift2,
        (cot_prompt[0], cot_conts[0, 0]),
        activated,
        slope,
        up_mat,
        down_turned,
    )
    result_prompt, result_cont, grad_second, part3, sums2, up_sum = results[:6]
    splits = results[6:]
    half = len(splits) // 2
    sum_f = Reduction(grid, [splits[:half]], [splits[half:]])
    grad_first, dout, sums1 = first_norm_backward(
        grad_second, part3, grid.over_tp(part3), norm1, inv1, gain1, output_turned
    )
    grad_prev, dq, dk, dv = attention_backward(
        queries, keys, values, dout, attended, probs_p, probs_c, cot_logits[0, 0], scale
    )
    dq = after(dq, sum_f.fold(dq))
    *splits, widths = weight_grads(
        grid, sizes[0], grad_first, attended, inputs_t, whole_t, dq, dk, dv, sums1, sums2, up_sum
    )
    sum_c = Reduction(grid, [splits[0]], [splits[1]])

    if grid.staged:
        folded = sum_c.fold(sum_f.line(splits))
        grads = after((dq, dk, dv), folded)
        partial, keep, low = input_pull(grid, *grads, query_mat, key_mat, value_mat, prompt_len)
        sent = sum_c.line(partial)
        came = grid.over_tp(low)
        own_rows = partial.shape[0]
        input_grad = grad_first + partial.astype(bf16).astype(f32) + came[:own_rows].astype(f32)
        arrived = grid.over_ctx(add_low(keep, came[own_rows:]))
        shard_f = sum_f.shard(folded)
        other = grid.over_tp(arrived)
        first = jnp.where(grid.core == 0, arrived, other)
        second = jnp.where(grid.core == 0, other, arrived)
        grad_cont = input_grad[prompt_len:]
        shared = grad_cont, arrived
        grad_prompt = input_grad[:prompt_len] + jnp.concatenate([first, second], 0).astype(f32)
    else:
        from_query = contract_cols(dq, query_mat)
        from_keyvalue = contract_cols(dk, key_mat) + contract_cols(dv, value_mat)
        own = lax.psum_scatter(
            from_keyvalue[:full_len].astype(bf16), "ctx", scatter_dimension=0, tiled=True
        ).astype(f32)
        own = own + from_query[:prompt_len]
        partial = jnp.concatenate([own, from_keyvalue[full_len:] + from_query[prompt_len:]], 0)
        input_grad = grad_first + grid.tp_sum(partial)
        grad_prompt, grad_cont = input_grad[:prompt_len], input_grad[prompt_len:]
        shard_f = sum_f.shard()
        shared = ()
    up_grad, down_turned_grad = columns_of(shard_f, [hidden, hidden])
    down_grad = down_turned_grad.T
    shard_c = sum_c.shard(up_grad, down_grad, *shared)
    output_grads, query_grad, key_grad, value_grad, table = columns_of(shard_c, widths)
    model = whole.shape[1]
    table = jnp.concatenate([table[:, at : at + LANES] for at in range(0, table.shape[1], LANES)], 0)
    place = lax.axis_index("fsdp")
    at = 6 * (model // LANES)
    long_lines = table[:at].reshape(6, model)
    long_lines = lax.dynamic_slice_in_dim(long_lines, place * rows, rows, 1)
    shorts = []
    for bias in (query_bias, value_bias, up_bias):
        height, cols = bias.shape
        span = height * cols * sizes[0] // LANES
        block = table[at : at + span].reshape(height, -1)
        shorts.append(lax.dynamic_slice_in_dim(block, place * cols, cols, 1))
        at += span
    gain_one_grad, shift_one_grad, output_add_grad = long_lines[0], long_lines[1], long_lines[2]
    gain_two_grad, shift_two_grad, down_add_grad = long_lines[3], long_lines[4], long_lines[5]
    return (
        result_prompt[None],
        result_cont[None, None],
        new_logits[None, None],
        grad_prompt[None],
        grad_cont[None, None],
        grad_prev[None, None],
        query_grad,
        shorts[0],
        key_grad,
        value_grad,
        shorts[1],
        output_grads.T,
        output_add_grad,
        gain_one_grad,
        shift_one_grad,
        up_grad,
        shorts[2],
        down_grad,
        down_add_grad,
        gain_two_grad,
        shift_two_grad,
    )


def solution(mesh):
    sizes = tuple(mesh.shape[name] for name in ("fsdp", "ctx", "tp"))

    def step(*arrays):
        return per_device(sizes, *arrays)

    return jax.shard_map(
        step,
        mesh=mesh,
        in_specs=(
            P("fsdp", "ctx", None),
            P("fsdp", "ctx", None, None),
            P("fsdp", "ctx", "tp", None, None),
            P("fsdp", "ctx"),
            P("fsdp", "tp"),
            P("tp", "fsdp"),
            P("fsdp", "tp"),
            P("fsdp", "tp"),
            P("tp", "fsdp"),
            P("tp", "fsdp"),
            P("fsdp"),
            P("fsdp"),
            P("fsdp"),
            P("fsdp", "tp"),
            P("tp", "fsdp"),
            P("tp", "fsdp"),
            P("fsdp"),
            P("fsdp"),
            P("fsdp"),
            P("fsdp", "ctx", None),
            P("fsdp", "ctx", None, None),
            P("fsdp", "ctx", "tp", None, None),
        ),
        out_specs=(
            P("fsdp", "ctx", None),
            P("fsdp", "ctx", None, None),
            P("fsdp", "ctx", "tp", None, None),
            P("fsdp", "ctx", None),
            P("fsdp", "ctx", None, None),
            P("fsdp", "ctx", "tp", None, None),
            P("fsdp", "tp"),
            P("tp", "fsdp"),
            P("fsdp", "tp"),
            P("fsdp", "tp"),
            P("tp", "fsdp"),
            P("tp", "fsdp"),
            P("fsdp"),
            P("fsdp"),
            P("fsdp"),
            P("fsdp", "tp"),
            P("tp", "fsdp"),
            P("tp", "fsdp"),
            P("fsdp"),
            P("fsdp"),
            P("fsdp"),
        ),
        check_vma=False,
    )
```

```python
import math

import jax
import jax.numpy as jnp
from jax import lax
from jax.experimental import pallas as pl
from jax.experimental.pallas import tpu as pltpu
from jax.sharding import PartitionSpec as P

epsilon = 1e-06
f32 = jnp.float32
bf16 = jnp.bfloat16
LANES = 128


def product(left_mat, right_mat):
    return jnp.dot(left_mat, right_mat, preferred_element_type=f32)


def contract_rows(left_mat, right_mat):
    return lax.dot_general(
        left_mat, right_mat, (((0,), (0,)), ((), ())), preferred_element_type=f32
    )


def contract_cols(left_mat, right_mat):
    return lax.dot_general(
        left_mat, right_mat, (((1,), (1,)), ((), ())), preferred_element_type=f32
    )


class Grid:
    def __init__(self, sizes):
        self.fsdp, self.ctx, self.tp = sizes
        self.staged = sizes == (8, 2, 2)
        place = lax.axis_index("fsdp")
        self.outer, self.inner = place // 2, place % 2
        self.row = lax.axis_index("ctx")
        self.core = lax.axis_index("tp")
        self.place = jnp.stack([self.outer, self.inner, self.row, self.core]).astype(jnp.int32)

    def over_inner(self, array):
        return lax.ppermute(array, "fsdp", [(i, i ^ 1) for i in range(8)])

    def over_outer(self, array, step):
        return lax.ppermute(array, "fsdp", [(i, i ^ (2 * step)) for i in range(8)])

    def over_ctx(self, array):
        return lax.ppermute(array, "ctx", [(0, 1), (1, 0)])

    def over_tp(self, array):
        return lax.ppermute(array, "tp", [(0, 1), (1, 0)])

    def tp_sum(self, partial):
        low = partial.astype(bf16)
        return low.astype(f32) + self.over_tp(low).astype(f32)


def pack_early(grid, weights, vectors, tables):
    rows = weights[0].shape[0]
    edges = [sum(w.shape[1] for w in weights[:i]) for i in range(len(weights) + 1)]
    cols = edges[-1] + LANES
    count = len(weights)

    def body(place, *refs):
        out, half_out, lines = refs[-3:]
        for ref, low, high in zip(refs, edges, edges[1:]):
            out[:, low:high] = ref[...]
        lines[...] = jnp.zeros_like(lines)
        at = 0
        for ref in refs[count:-3]:
            height, width = ref.shape
            lines[at : at + height, :width] = ref[...].astype(f32)
            at += height
        out[:, edges[-1] :] = lines[...].astype(bf16)
        half_out[...] = out[pl.ds(pl.multiple_of(place[2] * (rows // 2), 16), rows // 2), :]

    vmem = pl.BlockSpec(memory_space=pltpu.VMEM)
    args = [*weights, *vectors, *tables]
    outs = [like((rows, cols), bf16), like((rows // 2, cols), bf16)]
    return pl.pallas_call(
        body,
        out_shape=outs,
        in_specs=[pl.BlockSpec(memory_space=pltpu.SMEM)] + [vmem] * len(args),
        out_specs=[vmem] * 2,
        scratch_shapes=[pltpu.VMEM((rows, LANES), f32)],
        cost_estimate=cost(0, *args, *outs),
        name="pack_early",
    )(grid.place, *args)


def pack_late(grid, shard, late):
    rows, head = shard.shape
    cols = sum(w.shape[1] for w in late)

    def body(place, early_ref, *refs):
        out, half_out = refs[-2:]
        out[:, :head] = early_ref[...]
        here = pl.ds(pl.multiple_of(place[2] * (rows // 2), 16), rows // 2)
        low = 0
        for ref in refs[:-2]:
            high = low + ref.shape[1]
            out[:, head + low : head + high] = ref[...]
            half_out[:, low:high] = ref[here, :]
            low = high

    vmem = pl.BlockSpec(memory_space=pltpu.VMEM)
    outs = [like((rows, head + cols), bf16), like((rows // 2, cols), bf16)]
    return pl.pallas_call(
        body,
        out_shape=outs,
        in_specs=[pl.BlockSpec(memory_space=pltpu.SMEM)] + [vmem] * (1 + len(late)),
        out_specs=[vmem] * 2,
        cost_estimate=cost(0, shard, *late, *outs),
        name="pack_late",
    )(grid.place, shard, *late)


def join(pieces):
    height, cols = pieces[0].shape

    def body(*refs):
        for i, ref in enumerate(refs[:-1]):
            refs[-1][i * height : (i + 1) * height, :] = ref[...]

    vmem = pl.BlockSpec(memory_space=pltpu.VMEM)
    out = like((len(pieces) * height, cols), pieces[0].dtype)
    return pl.pallas_call(
        body,
        out_shape=out,
        in_specs=[vmem] * len(pieces),
        out_specs=vmem,
        cost_estimate=cost(0, out, out),
        name="join",
    )(*pieces)


def assemble(grid, cuts, base, own, side, came, across, along):
    full = own.shape[0]
    half = full // 2
    edges = [sum(cuts[:i]) for i in range(len(cuts) + 1)]

    def body(place, own_ref, side_ref, came_ref, across_ref, along_ref, *outs):
        outer, inner, row = place[0], place[1], place[2]

        def put(ref, start, length, step, swap_inner, swap_row, skip=0):
            at = (outer ^ step) * 2 + (inner ^ swap_inner)
            if length == half:
                at = at * 2 + (row ^ swap_row)
            here = pl.ds(pl.multiple_of(at * length, 16), length)
            for out, low, high in zip(outs, edges, edges[1:]):
                out[here, :] = ref[start : start + length, skip + low : skip + high]

        put(own_ref, 0, full, 0, 0, 0, base)
        put(side_ref, 0, full, 0, 1, 0, base)
        for step in (1, 2, 3):
            start = (step - 1) * half
            put(came_ref, start, half, step, 0, 0)
            put(across_ref, start, half, step, 1, 0)
            put(along_ref, start, half, step, 0, 1)
            for out in outs:
                at = (((outer ^ step) * 2 + (inner ^ 1)) * 2 + (row ^ 1)) * half
                out[pl.ds(pl.multiple_of(at, 16), half), :] = jnp.zeros((half, out.shape[1]), bf16)

    vmem = pl.BlockSpec(memory_space=pltpu.VMEM)
    outs = [like((8 * full, cols), own.dtype) for cols in cuts]
    return pl.pallas_call(
        body,
        out_shape=outs,
        in_specs=[pl.BlockSpec(memory_space=pltpu.SMEM)] + [vmem] * 5,
        out_specs=[vmem] * len(outs),
        compiler_params=pltpu.CompilerParams(vmem_limit_bytes=VMEM_LIMIT),
        cost_estimate=cost(0, *outs, *outs),
        name="assemble",
    )(grid.place, own, side, came, across, along)


def complete(grid, arrays, far_one, far_two):
    half = far_one.shape[0] // 3
    first = 0
    while sum(a.shape[1] for a in arrays[: first + 1]) <= far_one.shape[1]:
        first += 1
    count = len(arrays)
    copies = 3 * count

    def body(place, one_ref, two_ref, *refs):
        outs, sems = refs[count : 2 * count], refs[2 * count]
        outer, inner, row = place[0], place[1], place[2]
        started = []
        low = 0
        for i, out in enumerate(outs):
            ref = one_ref if i < first else two_ref
            if i == first:
                low = 0
            cols = out.shape[1]
            for step in (1, 2, 3):
                at = (((outer ^ step) * 2 + (inner ^ 1)) * 2 + (row ^ 1)) * half
                copy = pltpu.make_async_copy(
                    ref.at[(step - 1) * half : step * half, low : low + cols],
                    out.at[pl.ds(pl.multiple_of(at, 16), half), :],
                    sems.at[len(started)],
                )
                copy.start()
                started.append(copy)
            low += cols
        for copy in started:
            copy.wait()

    vmem = pl.BlockSpec(memory_space=pltpu.VMEM)
    anywhere = pl.BlockSpec(memory_space=pl.ANY)
    return pl.pallas_call(
        body,
        out_shape=[like(a.shape, a.dtype) for a in arrays],
        in_specs=[pl.BlockSpec(memory_space=pltpu.SMEM), vmem, vmem] + [anywhere] * count,
        out_specs=[anywhere] * count,
        scratch_shapes=[pltpu.SemaphoreType.DMA((copies,))],
        input_output_aliases={3 + i: i for i in range(count)},
        cost_estimate=cost(0, far_one, far_two, far_one, far_two),
        name="complete",
    )(grid.place, far_one, far_two, *arrays)


def lines_of(grid, mine):
    return [grid.over_outer(mine, step) for step in (1, 2, 3)]


def pairs_of(grid, came):
    return grid.over_inner(came), grid.over_ctx(came)


def corners_of(grid, across, along, cut):
    return grid.over_ctx(across[:, :cut]), grid.over_inner(along[:, cut:])


def halves_of(across, along):
    rows, cols = across.shape[0], across.shape[1] // 2

    def body(first, second, first_out, second_out):
        first_out[...] = first[...]
        second_out[...] = second[...]

    return pl.pallas_call(
        body,
        grid=(1,),
        out_shape=[like((rows, cols), across.dtype)] * 2,
        in_specs=[pl.BlockSpec((rows, cols), lambda i: (0, 0)), pl.BlockSpec((rows, cols), lambda i: (0, 1))],
        out_specs=[pl.BlockSpec((rows, cols), lambda i: (0, 0))] * 2,
        cost_estimate=cost(0, across, along),
        name="halves_of",
    )(across, along)


def pick(array, at, axis):
    return lax.dynamic_index_in_dim(array, at, axis, keepdims=False)


def add_low(left, right):
    return (left.astype(f32) + right.astype(f32)).astype(bf16)


VMEM_LIMIT = 60 * 1024 * 1024


def whole_block(array):
    rank = array.ndim
    return pl.BlockSpec(array.shape, lambda *_: (0,) * rank)


def cost(flops, *arrays, transcendentals=0):
    return pl.CostEstimate(flops=10**13, transcendentals=0, bytes_accessed=1)


def after(values, *earlier):
    return lax.optimization_barrier((values, earlier))[0]


def like(shape, dtype):
    return jax.ShapeDtypeStruct(shape, dtype)


def norm_rows(hidden_in):
    centre = jnp.mean(hidden_in, axis=-1, keepdims=True)
    shifted = hidden_in - centre
    spread = jnp.mean(shifted * shifted, axis=-1, keepdims=True)
    inverse = lax.rsqrt(spread + epsilon)
    return shifted * inverse, inverse


def norm_pull(upstream, normed, inverse, gain):
    scaled = upstream * gain
    mean_one = jnp.mean(scaled, axis=-1, keepdims=True)
    mean_two = jnp.mean(scaled * normed, axis=-1, keepdims=True)
    return inverse * (scaled - mean_one - normed * mean_two)


def column_sums(values):
    return jnp.sum(values, axis=0, keepdims=True)


def row_tile(rows):
    return 256 if rows % 256 == 0 else rows


def first_norm(prompt, conts, part, other, output_add, gain, shift):
    prompt_len, width = prompt.shape
    rows = prompt_len + conts.shape[0]
    tile = row_tile(prompt_len)
    ahead = prompt_len // tile

    def body(x, c, p, o, b, g, s, norm_out, inv_out, low_out):
        rows_in = jnp.where(pl.program_id(0) < ahead, x[...].astype(f32), c[...].astype(f32))
        normed, inverse = norm_rows(rows_in + (p[...].astype(f32) + o[...].astype(f32)) + b[...])
        norm_out[...] = normed
        inv_out[...] = jnp.broadcast_to(inverse, inv_out.shape)
        low_out[...] = (normed * g[...] + s[...]).astype(bf16)

    def tiled(array):
        return pl.BlockSpec((tile, array.shape[1]), lambda i: (i, 0))

    args = [prompt, conts, part, other, output_add, gain, shift]
    outs = [
        like((rows, width), f32),
        like((rows, LANES), f32),
        like((rows, width), bf16),
    ]
    return pl.pallas_call(
        body,
        grid=(rows // tile,),
        out_shape=outs,
        in_specs=[
            pl.BlockSpec((tile, width), lambda i: (jnp.minimum(i, ahead - 1), 0)),
            pl.BlockSpec((tile, width), lambda i: (jnp.maximum(i - ahead, 0), 0)),
        ]
        + [tiled(a) for a in args[2:4]]
        + [whole_block(a) for a in args[4:]],
        out_specs=[tiled(a) for a in outs],
        compiler_params=pltpu.CompilerParams(vmem_limit_bytes=VMEM_LIMIT),
        cost_estimate=cost(0, *args, *outs),
        name="first_norm",
    )(*args)


def turn(array):
    rows, cols = array.shape
    tile = row_tile(rows)

    def body(x, out):
        out[...] = x[...].astype(f32).T.astype(bf16)

    return pl.pallas_call(
        body,
        grid=(rows // tile,),
        out_shape=like((cols, rows), bf16),
        in_specs=[pl.BlockSpec((tile, cols), lambda i: (i, 0))],
        out_specs=pl.BlockSpec((cols, tile), lambda i: (0, i)),
        cost_estimate=cost(0, array),
        name="turn",
    )(array)


def ffn_forward(low, up_mat, up_add, down_turned):
    rows, width = low.shape
    hidden = up_mat.shape[1]
    tile = row_tile(rows)

    def body(x, up, ub, dn, act_out, slope_out, part_out):
        inner = product(x[...], up[...]) + ub[...]
        normal_cdf = 0.5 * (1.0 + lax.erf(inner * math.sqrt(0.5)))
        act = (inner * normal_cdf).astype(bf16)
        act_out[...] = act
        density = jnp.exp(-0.5 * inner * inner) * (1.0 / math.sqrt(2.0 * math.pi))
        slope_out[...] = (normal_cdf + inner * density).astype(bf16)
        part_out[...] = contract_cols(act, dn[...]).astype(bf16)

    outs = [
        like((rows, hidden), bf16),
        like((rows, hidden), bf16),
        like((rows, width), bf16),
    ]

    def tiled(array):
        return pl.BlockSpec((tile, array.shape[1]), lambda i: (i, 0))

    args = [low, up_mat, up_add, down_turned]
    return pl.pallas_call(
        body,
        grid=(rows // tile,),
        out_shape=outs,
        in_specs=[tiled(low)] + [whole_block(a) for a in args[1:]],
        out_specs=[tiled(a) for a in outs],
        compiler_params=pltpu.CompilerParams(vmem_limit_bytes=VMEM_LIMIT),
        cost_estimate=cost(4 * rows * width * hidden, *args, *outs, transcendentals=2 * rows * hidden),
        name="ffn_forward",
    )(*args)


def split_out(grid, length, cols):
    if grid.staged:
        return [like((length // 2, cols), bf16), like((length // 2, cols), bf16)]
    return [like((length, cols), bf16)]


def store_split(grid, place, full_ref, outs, over_inner):
    if not grid.staged:
        outs[0][...] = full_ref[...]
        return
    half = full_ref.shape[0] // 16
    for out, flip in zip(outs, (0, 1)):
        if over_inner:
            for outer in range(4):
                at = pl.multiple_of((2 * outer + (place[1] ^ flip)) * (2 * half), 32)
                out[2 * half * outer : 2 * half * (outer + 1), :] = full_ref[pl.ds(at, 2 * half), :]
        else:
            for block in range(8):
                at = pl.multiple_of((2 * block + (place[2] ^ flip)) * half, 16)
                out[half * block : half * (block + 1), :] = full_ref[pl.ds(at, half), :]


def ffn_backward(grid, norm1, turned1, gain1, shift1, part, other, down_add, gain2, shift2, cots, act, slope, up_mat, down_turned):
    rows, width = norm1.shape
    hidden = up_mat.shape[1]
    tile = 256
    chunk = row_tile(rows)
    prompt_len = cots[0].shape[0]
    count = 2 if grid.staged else 1

    def body(place, n1, x1_t, g1, s1, p, o, db, g2, s2, cp, cc, u, sl, up, dn, *rest):
        outs, scratch = rest[:-5], rest[-5:]
        y_p, y_c, dh2, dx1, sums, up_sum = outs[:6]
        up_outs, down_outs = outs[6 : 6 + count], outs[6 + count :]
        df, df_t, acc, full_up, full_down = scratch
        step = pl.program_id(0)

        @pl.when(step == 0)
        def _():
            total = [jnp.zeros((1, width), f32) for _ in range(3)]
            for at in range(0, rows, chunk):
                here = slice(at, at + chunk)
                first = n1[here, :] * g1[...] + s1[...]
                second = first + (p[here, :].astype(f32) + o[here, :].astype(f32)) + db[...]
                normed, inverse = norm_rows(second)
                result = (normed * g2[...] + s2[...]).astype(bf16)
                if at < prompt_len:
                    y_p[here, :] = result
                    cot = cp[here, :].astype(f32)
                else:
                    there = slice(at - prompt_len, at - prompt_len + chunk)
                    y_c[there, :] = result
                    cot = cc[there, :].astype(f32)
                grad = norm_pull(cot, normed, inverse, g2[...])
                dh2[here, :] = grad
                low = grad.astype(bf16)
                df[here, :] = low
                wide = low.astype(f32)
                df_t[:, here] = wide.T.astype(bf16)
                total[0] += column_sums(cot * normed)
                total[1] += column_sums(cot)
                total[2] += column_sums(wide)
            sums[...] = jnp.zeros(sums.shape, f32)
            for i in range(3):
                sums[i : i + 1, :] = total[i]
            acc[...] = jnp.zeros_like(acc)

        inner = (product(df[...], dn[...]) * sl[...].astype(f32)).astype(bf16)
        up_sum[...] = jnp.broadcast_to(column_sums(inner.astype(f32)), up_sum.shape)
        full_up[...] = product(x1_t[...], inner).astype(bf16)
        full_down[...] = product(df_t[...], u[...]).astype(bf16)
        acc[...] += contract_cols(inner, up[...])
        store_split(grid, place, full_up, up_outs, True)
        store_split(grid, place, full_down, down_outs, False)

        @pl.when(step == hidden // tile - 1)
        def _():
            dx1[...] = acc[...].astype(bf16)

    def tiled(array):
        return pl.BlockSpec((array.shape[0], tile), lambda j: (0, j))

    fixed = [norm1, turned1, gain1, shift1, part, other, down_add, gain2, shift2, *cots]
    moving = [act, slope, up_mat, down_turned]
    outs = [
        like((prompt_len, width), bf16),
        like((rows - prompt_len, width), bf16),
        like((rows, width), f32),
        like((rows, width), bf16),
        like((8, width), f32),
        like((8, hidden), f32),
    ]
    grads = split_out(grid, width, hidden) * 2
    return pl.pallas_call(
        body,
        grid=(hidden // tile,),
        out_shape=outs + grads,
        in_specs=[pl.BlockSpec(memory_space=pltpu.SMEM)]
        + [whole_block(a) for a in fixed]
        + [tiled(a) for a in moving],
        out_specs=[whole_block(a) for a in outs[:5]] + [tiled(a) for a in outs[5:] + grads],
        scratch_shapes=[
            pltpu.VMEM((rows, width), bf16),
            pltpu.VMEM((width, rows), bf16),
            pltpu.VMEM((rows, width), f32),
            pltpu.VMEM((width, tile), bf16),
            pltpu.VMEM((width, tile), bf16),
        ],
        compiler_params=pltpu.CompilerParams(vmem_limit_bytes=VMEM_LIMIT),
        cost_estimate=cost(8 * rows * width * hidden, *fixed, *moving, *outs, *grads),
        name="ffn_backward",
    )(grid.place, *fixed, *moving)


def fold_pair(grid, firsts, seconds):
    half = firsts[0][0].shape[0] // 8
    outs = []
    for group in (firsts, seconds):
        outs += [like((4 * half, sum(kept.shape[1] for kept, _ in group)), bf16)] * 2

    vmem = pl.BlockSpec(memory_space=pltpu.VMEM)

    def body(place, *refs):
        pairs, outs = refs[:-4], refs[-4:]
        at_pair = 0
        for group, mine, (keep, send) in (
            (firsts, place[2], outs[:2]),
            (seconds, place[1], outs[2:]),
        ):
            low = 0
            for _ in group:
                kept, came = pairs[at_pair : at_pair + 2]
                at_pair += 2
                high = low + kept.shape[1]
                for out, flip in ((send, 1), (keep, 0)):
                    for outer in range(4):
                        here = pl.ds(pl.multiple_of((2 * outer + (mine ^ flip)) * half, 16), half)
                        out[outer * half : (outer + 1) * half, low:high] = (
                            kept[here, :].astype(f32) + came[here, :].astype(f32)
                        ).astype(bf16)
                low = high

    args = [a for group in (firsts, seconds) for pair in group for a in pair]
    return pl.pallas_call(
        body,
        out_shape=outs,
        in_specs=[pl.BlockSpec(memory_space=pltpu.SMEM)] + [vmem] * len(args),
        out_specs=[vmem] * 4,
        compiler_params=pltpu.CompilerParams(vmem_limit_bytes=VMEM_LIMIT),
        cost_estimate=cost(0, *args, *outs),
        name="fold_pair",
    )(grid.place, *args)


def fold_line(grid, first, second):
    half = first[0].shape[0] // 4
    left, right = first[0].shape[1], second[0].shape[1]
    outs = [like((half, left + right), f32)] + [like((half, left + right), bf16)] * 3

    def body(place, fk, fa, sk, sa, *out_refs):
        for step, out in enumerate(out_refs):
            here = pl.ds(pl.multiple_of((place[0] ^ step) * half, 16), half)
            out[:, :left] = (fk[here, :].astype(f32) + fa[here, :].astype(f32)).astype(out.dtype)
            out[:, left:] = (sk[here, :].astype(f32) + sa[here, :].astype(f32)).astype(out.dtype)

    vmem = pl.BlockSpec(memory_space=pltpu.VMEM)
    args = [*first, *second]
    return pl.pallas_call(
        body,
        out_shape=outs,
        in_specs=[pl.BlockSpec(memory_space=pltpu.SMEM)] + [vmem] * 4,
        out_specs=[vmem] * 4,
        cost_estimate=cost(0, *args, *outs),
        name="fold_line",
    )(grid.place, *args)


class Reduction:
    def __init__(self, grid, firsts, seconds):
        self.grid, self.firsts, self.seconds = grid, firsts, seconds
        if grid.staged:
            self.came = [
                [grid.over_inner(g[1]) for g in firsts],
                [grid.over_ctx(g[1]) for g in seconds],
            ]

    def fold(self, *earlier):
        if not self.grid.staged:
            return ()
        grid = self.grid
        came = after(self.came, *earlier)
        folded = fold_pair(
            grid,
            [(g[0], c) for g, c in zip(self.firsts, came[0])],
            [(g[0], c) for g, c in zip(self.seconds, came[1])],
        )
        f_keep, f_send, s_keep, s_send = folded
        self.kept = f_keep, s_keep
        self.came = grid.over_ctx(f_send), grid.over_inner(s_send)
        return folded

    def line(self, *earlier):
        if not self.grid.staged:
            return ()
        came = after(self.came, *earlier)
        self.total, *sent = fold_line(self.grid, (self.kept[0], came[0]), (self.kept[1], came[1]))
        self.came = [self.grid.over_outer(sent[step - 1], step) for step in (1, 2, 3)]
        return sent

    def shard(self, *earlier, beside=()):
        grid = self.grid
        if not grid.staged:
            both = jnp.concatenate([g[0] for g in self.firsts + self.seconds], 1)
            both = lax.psum_scatter(both, "fsdp", scatter_dimension=0, tiled=True)
            return lax.psum(both, "ctx").astype(f32)
        came = after(self.came, *earlier)
        total = self.total
        for piece in came:
            total = total + piece.astype(f32)
        total = total.astype(bf16)
        other = after(grid.over_ctx(total), *beside)
        low = jnp.where(grid.row == 0, total, other)
        high = jnp.where(grid.row == 0, other, total)
        return jnp.concatenate([low, high], 0).astype(f32)


def columns_of(shard, widths):
    edges = [sum(widths[:i]) for i in range(len(widths) + 1)]
    return [shard[:, low:high] for low, high in zip(edges, edges[1:])]


def head_lanes(shape, index):
    lane = lax.broadcasted_iota(jnp.int32, shape, 1)
    return (lane < LANES // 2) if index == 0 else (lane >= LANES // 2)


def each_chunk(rows_at, prompt_len, rows, chunk):
    @pl.loop(0, prompt_len // chunk)
    def _(i):
        rows_at(pl.multiple_of(i * chunk, chunk), True)

    for at in range(prompt_len, rows, chunk):
        rows_at(at, False)


def attention_forward(queries, keys, values, prev_logits, cont_len, prompt_len, pairs, held=()):
    begin, end = pairs
    kept = len(held)
    rows, width = queries.shape
    total = keys.shape[0]
    cont_size = rows - prompt_len
    full_len = total - cont_size
    heads = prev_logits.shape[0]
    chunk = row_tile(prompt_len)

    def body(length, q, k, v, prev, *refs):
        logits, probs_p, probs_c, out = refs[kept:]

        def soft(scores):
            weights = jnp.exp(scores - jnp.max(scores, axis=-1, keepdims=True))
            return (weights * (1.0 / jnp.sum(weights, axis=-1, keepdims=True))).astype(bf16)

        column = lax.broadcasted_iota(jnp.int32, (1, total), 1)
        live = column < full_len + length[0, 0]
        def rows_at(at, in_prompt):
            here = pl.ds(at, chunk)
            halves = []
            for head in range(2):
                one = jnp.where(head_lanes((chunk, LANES), head), q[here, :], 0)
                if in_prompt:
                    probs = soft(contract_cols(one, k[:full_len, :]))
                    probs_p[head, here, :] = probs
                    halves.append(product(probs, v[:full_len, :]))
                else:
                    there = slice(at - prompt_len, at - prompt_len + chunk)
                    raw = prev[head, there, :].astype(f32) + contract_cols(one, k[...])
                    logits[head, there, :] = raw.astype(bf16)
                    probs = soft(jnp.where(live, raw, -1e30))
                    probs_c[head, there, :] = probs
                    halves.append(product(probs, v[...]))
            first = head_lanes((chunk, LANES), 0)
            out[here, :] = jnp.where(first, halves[0], halves[1]).astype(bf16)

        each_chunk(rows_at, prompt_len, rows, chunk)

    outs = [
        like((heads, cont_size, total), bf16),
        like((heads, prompt_len, full_len), bf16),
        like((heads, cont_size, total), bf16),
        like((rows, width), bf16),
    ]

    def columns(array):
        return pl.BlockSpec((array.shape[0], LANES), lambda i: (0, begin + i))

    def pair_of(array):
        return pl.BlockSpec((2,) + array.shape[1:], lambda i: (begin + i, 0, 0))

    args = [queries, keys, values, prev_logits]
    scores = heads * (prompt_len * full_len + cont_size * total)
    return pl.pallas_call(
        body,
        grid=(end - begin,),
        out_shape=outs,
        in_specs=[pl.BlockSpec(memory_space=pltpu.SMEM)]
        + [columns(a) for a in args[:3]]
        + [pair_of(prev_logits)]
        + [pl.BlockSpec(memory_space=pl.ANY)] * kept,
        out_specs=[pair_of(a) for a in outs[:3]] + [columns(outs[3])],
        compiler_params=pltpu.CompilerParams(vmem_limit_bytes=VMEM_LIMIT),
        input_output_aliases={5 + i: i for i in range(kept)},
        cost_estimate=cost((end - begin) * 256 * scores, *args, transcendentals=scores),
        name="attention_forward",
    )(cont_len, *args, *held)


def attention_backward(queries, keys, values, dout, attended, probs_p, probs_c, cots, scale):
    rows, width = queries.shape
    total = keys.shape[0]
    heads, prompt_len, full_len = probs_p.shape
    cont_size = rows - prompt_len
    chunk = row_tile(prompt_len)

    def body(q, k, v, do, o, pp, pc, cot, prev_out, dq, dk, dv, acc_k, acc_v):
        acc_k[...] = jnp.zeros_like(acc_k)
        acc_v[...] = jnp.zeros_like(acc_v)
        def rows_at(at, in_prompt):
            here = pl.ds(at, chunk)
            grads = []
            for head in range(2):
                mine = head_lanes((chunk, LANES), head)
                one_q = jnp.where(mine, q[here, :], 0)
                one_do = jnp.where(mine, do[here, :], 0)
                delta = jnp.sum(
                    one_do.astype(f32) * o[here, :].astype(f32), axis=-1, keepdims=True
                )
                if in_prompt:
                    span = full_len
                    probs = pp[head, here, :]
                    dprob = contract_cols(one_do, v[:span, :])
                    dscore = (probs.astype(f32) * (dprob - delta)).astype(bf16)
                else:
                    span = total
                    there = slice(at - prompt_len, at - prompt_len + chunk)
                    probs = pc[head, there, :]
                    dprob = contract_cols(one_do, v[...])
                    dscore = (
                        probs.astype(f32) * (dprob - delta) + cot[head, there, :].astype(f32)
                    ).astype(bf16)
                    prev_out[head, there, :] = dscore
                grads.append(product(dscore, k[:span, :]))
                acc_k[:span, :] += contract_rows(dscore, one_q)
                acc_v[:span, :] += contract_rows(probs, one_do)
            first = head_lanes((chunk, LANES), 0)
            dq[here, :] = (jnp.where(first, grads[0], grads[1]) * scale).astype(bf16)

        each_chunk(rows_at, prompt_len, rows, chunk)
        dk[...] = acc_k[...].astype(bf16)
        dv[...] = acc_v[...].astype(bf16)

    outs = [
        like((heads, cont_size, total), bf16),
        like((rows, width), bf16),
        like((total, width), bf16),
        like((total, width), bf16),
    ]

    def columns(array):
        return pl.BlockSpec((array.shape[0], LANES), lambda i: (0, i))

    def pairs(array):
        return pl.BlockSpec((2,) + array.shape[1:], lambda i: (i, 0, 0))

    args = [queries, keys, values, dout, attended, probs_p, probs_c, cots]
    scores = heads * (prompt_len * full_len + cont_size * total)
    return pl.pallas_call(
        body,
        grid=(heads // 2,),
        out_shape=outs,
        in_specs=[columns(a) for a in args[:5]] + [pairs(a) for a in args[5:]],
        out_specs=[pairs(outs[0])] + [columns(a) for a in outs[1:]],
        scratch_shapes=[pltpu.VMEM((total, LANES), f32), pltpu.VMEM((total, LANES), f32)],
        compiler_params=pltpu.CompilerParams(vmem_limit_bytes=VMEM_LIMIT),
        cost_estimate=cost(1024 * scores, *args, *outs),
        name="attention_backward",
    )(*args)


def first_norm_backward(grad_second, part, other, norm1, inv1, gain1, output_turned):
    rows, width = grad_second.shape
    tile = row_tile(rows)

    def body(d2, p, o, n1, r1, g1, ot, dh1, dout, sums):
        @pl.when(pl.program_id(0) == 0)
        def _():
            sums[...] = jnp.zeros_like(sums)

        upstream = d2[...] + (p[...].astype(f32) + o[...].astype(f32))
        normed = n1[...]
        grad = norm_pull(upstream, normed, r1[:, :1], g1[...])
        dh1[...] = grad
        low = grad.astype(bf16)
        dout[...] = product(low, ot[...]).astype(bf16)
        sums[0:1, :] += column_sums(upstream * normed)
        sums[1:2, :] += column_sums(upstream)
        sums[2:3, :] += column_sums(low.astype(f32))

    def tiled(array):
        return pl.BlockSpec((tile, array.shape[1]), lambda i: (i, 0))

    args = [grad_second, part, other, norm1, inv1, gain1, output_turned]
    outs = [
        like((rows, width), f32),
        like((rows, output_turned.shape[1]), bf16),
        like((8, width), f32),
    ]
    return pl.pallas_call(
        body,
        grid=(rows // tile,),
        out_shape=outs,
        in_specs=[tiled(a) for a in args[:5]] + [whole_block(a) for a in args[5:]],
        out_specs=[tiled(a) for a in outs[:2]] + [whole_block(outs[2])],
        compiler_params=pltpu.CompilerParams(vmem_limit_bytes=VMEM_LIMIT),
        cost_estimate=cost(2 * rows * width * output_turned.shape[1], *args, *outs),
        name="first_norm_backward",
    )(*args)


def input_pull(grid, dq, dk, dv, query_mat, key_mat, value_mat, prompt_len):
    rows, width = dq.shape[0], query_mat.shape[0]
    half = prompt_len // 2
    tile = half
    full_len = 2 * prompt_len

    def body(place, q, k, v, qm, km, vm, own, keep, low):
        def pull(at):
            here = pl.ds(pl.multiple_of(at, tile), tile)
            return contract_cols(k[here, :], km[...]) + contract_cols(v[here, :], vm[...])

        for at in range(0, rows, tile):
            source = place[2] * prompt_len + at if at < prompt_len else at - prompt_len + full_len
            value = contract_cols(q[at : at + tile, :], qm[...]) + pull(source)
            own[at : at + tile, :] = value
            low[at : at + tile, :] = value.astype(bf16)
        abroad = (1 - place[2]) * prompt_len
        keep[...] = pull(abroad + place[3] * half).astype(bf16)
        low[rows:, :] = pull(abroad + (1 - place[3]) * half).astype(bf16)

    args = [dq, dk, dv, query_mat, key_mat, value_mat]
    vmem = pl.BlockSpec(memory_space=pltpu.VMEM)
    return pl.pallas_call(
        body,
        out_shape=[like((rows, width), f32), like((half, width), bf16), like((rows + half, width), bf16)],
        in_specs=[pl.BlockSpec(memory_space=pltpu.SMEM)] + [vmem] * len(args),
        out_specs=[vmem] * 3,
        compiler_params=pltpu.CompilerParams(vmem_limit_bytes=VMEM_LIMIT),
        cost_estimate=cost(0, *args),
        name="input_pull",
    )(grid.place, *args)


def weight_grads(grid, shards, grad_first, attended, inputs_t, whole_t, dq, dk, dv, sums1, sums2, up_sum):
    width, part = inputs_t.shape[0], dq.shape[1]
    hidden = up_sum.shape[1]
    count = 2 if grid.staged else 1
    block = width // shards
    sides = pl.cdiv((6 * width + 2 * part + hidden) // LANES, block)
    extra = sides * LANES
    widths = [part, part, part, part, extra]

    def body(place, d1, o, xt, wt, q, k, v, s1, s2, us, *rest):
        firsts, seconds = rest[:count], rest[count : 2 * count]
        full_a, full_b = rest[2 * count :]
        turned = d1[...].T.astype(bf16)
        full_a[:, :part] = product(turned, o[...]).astype(bf16)
        full_a[:, part:] = product(xt[...], q[...]).astype(bf16)
        full_b[:, :part] = product(wt[...], k[...]).astype(bf16)
        wide = 2 * part
        full_b[:, part:wide] = product(wt[...], v[...]).astype(bf16)
        lines = [(s1, i) for i in range(3)] + [(s2, i) for i in range(3)]
        pieces = []
        for ref, i in lines:
            pieces += [ref[i : i + 1, at : at + LANES] for at in range(0, width, LANES)]
        for sums in (column_sums(q[...].astype(f32)), column_sums(v[...].astype(f32))):
            pieces += [sums[:, at : at + LANES] for at in range(0, part, LANES)]
        pieces += [us[0:1, at : at + LANES] for at in range(0, hidden, LANES)]
        pieces.append(jnp.zeros((sides * block - len(pieces), LANES), f32))
        table = jnp.concatenate(pieces, 0).astype(bf16)
        for shard in range(shards):
            for side in range(sides):
                low = wide + side * LANES
                full_b[shard * block : (shard + 1) * block, low : low + LANES] = table[
                    side * block : (side + 1) * block
                ]
        store_split(grid, place, full_a, firsts, True)
        store_split(grid, place, full_b, seconds, False)

    args = [grad_first, attended, inputs_t, whole_t, dq, dk, dv, sums1, sums2, up_sum]
    outs = split_out(grid, width, 2 * part) + split_out(grid, width, sum(widths[2:]))
    vmem = pl.BlockSpec(memory_space=pltpu.VMEM)
    outs = pl.pallas_call(
        body,
        out_shape=outs,
        in_specs=[pl.BlockSpec(memory_space=pltpu.SMEM)] + [vmem] * len(args),
        out_specs=[vmem] * len(outs),
        scratch_shapes=[
            pltpu.VMEM((width, 2 * part), bf16),
            pltpu.VMEM((width, sum(widths[2:])), bf16),
        ],
        compiler_params=pltpu.CompilerParams(vmem_limit_bytes=VMEM_LIMIT),
        cost_estimate=cost(0, *args, *outs),
        name="weight_grads",
    )(grid.place, *args)
    return outs[:count], outs[count:], widths


def unpack_small(grid, packed, heads, head_size, up_rows):
    width = packed.shape[0]
    shards = grid.fsdp
    block, per_head, per_up = width // shards, head_size // shards, LANES // shards

    def body(packed_ref, lines, query_out, value_out, up_out):
        source = lax.broadcasted_iota(jnp.int32, (LANES, width), 0)
        target = lax.broadcasted_iota(jnp.int32, (LANES, width), 1)
        whole = jnp.zeros((32, width), f32)
        by_head = jnp.zeros((32, LANES), f32)
        by_up = jnp.zeros((32, LANES), f32)
        near, far = source[:, :LANES], target[:, :LANES]
        for shard in range(shards):
            piece = packed_ref[shard * block : shard * block + 32, :]
            put = (target - source == shard * block) & (source < block)
            whole += product(piece, put.astype(bf16))
            place = shard * per_head
            shift = far - near
            put = ((shift == place) | (shift == place + head_size)) & (near < per_head)
            by_head += product(piece, put.astype(bf16))
            put = (shift == shard * per_up) & (near < per_up)
            by_up += product(piece, put.astype(bf16))
        lines[...] = whole[:8, :]
        low = lax.broadcasted_iota(jnp.int32, (1, LANES), 1) < head_size
        for pair in range(heads // 2):
            at = slice(pair * LANES, (pair + 1) * LANES)
            for out, base in ((query_out, 6), (value_out, 6 + heads)):
                row = base + 2 * pair
                out[:, at] = jnp.where(low, by_head[row : row + 1, :], by_head[row + 1 : row + 2, :])
        for i in range(up_rows):
            row = 6 + 2 * heads + i
            up_out[:, i * LANES : (i + 1) * LANES] = by_up[row : row + 1, :]

    outs = [
        like((8, width), f32),
        like((1, heads * head_size), f32),
        like((1, heads * head_size), f32),
        like((1, up_rows * LANES), f32),
    ]
    vmem = pl.BlockSpec(memory_space=pltpu.VMEM)
    return pl.pallas_call(
        body,
        out_shape=outs,
        in_specs=[vmem],
        out_specs=[vmem] * 4,
        cost_estimate=cost(0, packed, *outs),
        name="unpack_small",
    )(packed)


def per_device(
    sizes,
    prompt,
    continuations,
    prev_logits,
    cont_len,
    query_weight,
    query_bias,
    key_weight,
    value_weight,
    value_bias,
    output_weight,
    output_bias,
    first_gain,
    first_shift,
    up_weight,
    up_bias,
    down_weight,
    down_bias,
    second_gain,
    second_shift,
    cot_prompt,
    cot_conts,
    cot_logits,
):
    grid = Grid(sizes)
    rows = query_weight.shape[0]
    width = query_weight.shape[1]
    hidden = up_weight.shape[1]
    prompt_len = prompt.shape[1]
    cont_size = continuations.shape[2]
    head_count = query_bias.shape[0]
    head_size = width // head_count
    scale = 1.0 / math.sqrt(head_size)

    mine, conts = prompt[0], continuations[0, 0]
    lines = [v[None] for v in (output_bias, first_gain, first_shift, down_bias, second_gain, second_shift)]
    tables = [query_bias, value_bias, up_bias]
    early = [query_weight, key_weight, value_weight, output_weight.T]
    late = [up_weight, down_weight.T]
    shard, half_shard = pack_early(grid, early, lines, tables)
    cuts = [width, width, width, width, LANES]
    cut = 2 * width
    if grid.staged:
        came = lines_of(grid, half_shard)
        sent, shard = lax.optimization_barrier((mine, shard))
        theirs = grid.over_ctx(sent)
        shards, late_half = pack_late(grid, shard, late)
        side = grid.over_inner(shards)
        came, late_half, theirs = lax.optimization_barrier((came, late_half, theirs))
        came = join(came)
        across, along = pairs_of(grid, came)
        far = corners_of(grid, across, along, cut)
        late_came = lines_of(grid, late_half)
        early = complete(
            grid, assemble(grid, cuts, 0, shards, side, came, across, along), *far
        )
    else:
        shards = [shard] + late
        shards = [lax.all_gather(a, "fsdp", axis=0, tiled=True) for a in shards]
        edges = [sum(cuts[:i]) for i in range(len(cuts) + 1)]
        early = [shards[0][:, low:high] for low, high in zip(edges, edges[1:])]
        late = shards[1:]
    query_mat, key_mat, value_mat, output_turned, small = early
    vectors, query_add, value_add, up_line = unpack_small(
        grid, small, head_count, head_size, up_bias.shape[0]
    )
    if grid.staged:
        late_came = join(after(late_came, vectors))
        late_across, late_along = pairs_of(grid, late_came)
        query_mat, key_mat, value_mat = after((query_mat, key_mat, value_mat), late_came)
    output_line, gain1, shift1, down_line, gain2, shift2 = [vectors[i : i + 1] for i in range(6)]

    inputs = jnp.concatenate([mine, conts], 0)
    if sizes[1] == 2:
        if not grid.staged:
            theirs = grid.over_ctx(mine)
        whole = jnp.concatenate(
            [jnp.where(grid.row == 0, mine, theirs), jnp.where(grid.row == 0, theirs, mine), conts], 0
        )
    else:
        whole = jnp.concatenate([lax.all_gather(mine, "ctx", axis=0, tiled=True), conts], 0)
    full_len = whole.shape[0] - cont_size
    whole_t, inputs_t = whole.T, inputs.T

    queries = ((product(inputs, query_mat) + query_add) * scale).astype(bf16)
    keys = product(whole, key_mat).astype(bf16)
    values = (product(whole, value_mat) + value_add).astype(bf16)
    queries, whole_t, inputs_t = lax.optimization_barrier((queries, whole_t, inputs_t))
    attention = (queries, keys, values, prev_logits[0, 0], cont_len, prompt_len)
    pair_count = head_count // 2
    held = attention_forward(*attention, (0, pair_count - 1))
    if grid.staged:
        late_across, late_along, held = lax.optimization_barrier((late_across, late_along, held))
        first, second = halves_of(late_across, late_along)
        held = after(held, first)
        far = grid.over_ctx(first), grid.over_inner(second)
    new_logits, probs_p, probs_c, attended = attention_forward(
        *attention, (pair_count - 1, pair_count), held
    )
    if grid.staged:
        late = assemble(
            grid, [hidden, hidden], sum(cuts), shards, side, late_came, late_across, late_along
        )
    part = contract_cols(attended, output_turned).astype(bf16)
    norm1, inv1, low1 = first_norm(
        mine, conts, part, grid.over_tp(part), output_line, gain1, shift1
    )
    if grid.staged:
        late = complete(grid, late, *far)
    up_mat, down_turned = late
    activated, slope, part2 = ffn_forward(low1, up_mat, up_line, down_turned)
    turned1 = turn(after(low1, part2))
    results = ffn_backward(
        grid,
        norm1,
        turned1,
        gain1,
        shift1,
        part2,
        grid.over_tp(part2),
        down_line,
        gain2,
        shift2,
        (cot_prompt[0], cot_conts[0, 0]),
        activated,
        slope,
        up_mat,
        down_turned,
    )
    result_prompt, result_cont, grad_second, part3, sums2, up_sum = results[:6]
    splits = results[6:]
    half = len(splits) // 2
    sum_f = Reduction(grid, [splits[:half]], [splits[half:]])
    grad_first, dout, sums1 = first_norm_backward(
        grad_second, part3, grid.over_tp(part3), norm1, inv1, gain1, output_turned
    )
    grad_prev, dq, dk, dv = attention_backward(
        queries, keys, values, dout, attended, probs_p, probs_c, cot_logits[0, 0], scale
    )
    dq = after(dq, sum_f.fold(dq))
    *splits, widths = weight_grads(
        grid, sizes[0], grad_first, attended, inputs_t, whole_t, dq, dk, dv, sums1, sums2, up_sum
    )
    sum_c = Reduction(grid, [splits[0]], [splits[1]])

    if grid.staged:
        folded = sum_c.fold(sum_f.line(splits))
        grads = after((dq, dk, dv), folded)
        partial, keep, low = input_pull(grid, *grads, query_mat, key_mat, value_mat, prompt_len)
        sent = sum_c.line(partial)
        came = grid.over_tp(low)
        own_rows = partial.shape[0]
        input_grad = grad_first + partial.astype(bf16).astype(f32) + came[:own_rows].astype(f32)
        arrived = grid.over_ctx(add_low(keep, came[own_rows:]))
        shard_f = sum_f.shard(folded)
        other = grid.over_tp(arrived)
        first = jnp.where(grid.core == 0, arrived, other)
        second = jnp.where(grid.core == 0, other, arrived)
        grad_cont = input_grad[prompt_len:]
        shared = grad_cont, arrived
        grad_prompt = input_grad[:prompt_len] + jnp.concatenate([first, second], 0).astype(f32)
    else:
        from_query = contract_cols(dq, query_mat)
        from_keyvalue = contract_cols(dk, key_mat) + contract_cols(dv, value_mat)
        own = lax.psum_scatter(
            from_keyvalue[:full_len].astype(bf16), "ctx", scatter_dimension=0, tiled=True
        ).astype(f32)
        own = own + from_query[:prompt_len]
        partial = jnp.concatenate([own, from_keyvalue[full_len:] + from_query[prompt_len:]], 0)
        input_grad = grad_first + grid.tp_sum(partial)
        grad_prompt, grad_cont = input_grad[:prompt_len], input_grad[prompt_len:]
        shard_f = sum_f.shard()
        shared = ()
    up_grad, down_turned_grad = columns_of(shard_f, [hidden, hidden])
    down_grad = down_turned_grad.T
    shard_c = sum_c.shard(up_grad, down_grad, *shared, beside=[grad_prompt])
    output_grads, query_grad, key_grad, value_grad, table = columns_of(shard_c, widths)
    model = whole.shape[1]
    table = jnp.concatenate([table[:, at : at + LANES] for at in range(0, table.shape[1], LANES)], 0)
    place = lax.axis_index("fsdp")
    at = 6 * (model // LANES)
    long_lines = table[:at].reshape(6, model)
    long_lines = lax.dynamic_slice_in_dim(long_lines, place * rows, rows, 1)
    shorts = []
    for bias in (query_bias, value_bias, up_bias):
        height, cols = bias.shape
        span = height * cols * sizes[0] // LANES
        block = table[at : at + span].reshape(height, -1)
        shorts.append(lax.dynamic_slice_in_dim(block, place * cols, cols, 1))
        at += span
    gain_one_grad, shift_one_grad, output_add_grad = long_lines[0], long_lines[1], long_lines[2]
    gain_two_grad, shift_two_grad, down_add_grad = long_lines[3], long_lines[4], long_lines[5]
    return (
        result_prompt[None],
        result_cont[None, None],
        new_logits[None, None],
        grad_prompt[None],
        grad_cont[None, None],
        grad_prev[None, None],
        query_grad,
        shorts[0],
        key_grad,
        value_grad,
        shorts[1],
        output_grads.T,
        output_add_grad,
        gain_one_grad,
        shift_one_grad,
        up_grad,
        shorts[2],
        down_grad,
        down_add_grad,
        gain_two_grad,
        shift_two_grad,
    )


def solution(mesh):
    sizes = tuple(mesh.shape[name] for name in ("fsdp", "ctx", "tp"))

    def step(*arrays):
        return per_device(sizes, *arrays)

    return jax.shard_map(
        step,
        mesh=mesh,
        in_specs=(
            P("fsdp", "ctx", None),
            P("fsdp", "ctx", None, None),
            P("fsdp", "ctx", "tp", None, None),
            P("fsdp", "ctx"),
            P("fsdp", "tp"),
            P("tp", "fsdp"),
            P("fsdp", "tp"),
            P("fsdp", "tp"),
            P("tp", "fsdp"),
            P("tp", "fsdp"),
            P("fsdp"),
            P("fsdp"),
            P("fsdp"),
            P("fsdp", "tp"),
            P("tp", "fsdp"),
            P("tp", "fsdp"),
            P("fsdp"),
            P("fsdp"),
            P("fsdp"),
            P("fsdp", "ctx", None),
            P("fsdp", "ctx", None, None),
            P("fsdp", "ctx", "tp", None, None),
        ),
        out_specs=(
            P("fsdp", "ctx", None),
            P("fsdp", "ctx", None, None),
            P("fsdp", "ctx", "tp", None, None),
            P("fsdp", "ctx", None),
            P("fsdp", "ctx", None, None),
            P("fsdp", "ctx", "tp", None, None),
            P("fsdp", "tp"),
            P("tp", "fsdp"),
            P("fsdp", "tp"),
            P("fsdp", "tp"),
            P("tp", "fsdp"),
            P("tp", "fsdp"),
            P("fsdp"),
            P("fsdp"),
            P("fsdp"),
            P("fsdp", "tp"),
            P("tp", "fsdp"),
            P("tp", "fsdp"),
            P("fsdp"),
            P("fsdp"),
            P("fsdp"),
        ),
        check_vma=False,
    )
```

```python
import math

import jax
import jax.numpy as jnp
from jax import lax
from jax.experimental import pallas as pl
from jax.experimental.pallas import tpu as pltpu
from jax.sharding import PartitionSpec as P

epsilon = 1e-06
f32 = jnp.float32
bf16 = jnp.bfloat16
LANES = 128


def product(left_mat, right_mat):
    return jnp.dot(left_mat, right_mat, preferred_element_type=f32)


def contract_rows(left_mat, right_mat):
    return lax.dot_general(
        left_mat, right_mat, (((0,), (0,)), ((), ())), preferred_element_type=f32
    )


def contract_cols(left_mat, right_mat):
    return lax.dot_general(
        left_mat, right_mat, (((1,), (1,)), ((), ())), preferred_element_type=f32
    )


class Grid:
    def __init__(self, sizes):
        self.fsdp, self.ctx, self.tp = sizes
        self.staged = sizes == (8, 2, 2)
        place = lax.axis_index("fsdp")
        self.outer, self.inner = place // 2, place % 2
        self.row = lax.axis_index("ctx")
        self.core = lax.axis_index("tp")
        self.place = jnp.stack([self.outer, self.inner, self.row, self.core]).astype(jnp.int32)

    def over_inner(self, array):
        return lax.ppermute(array, "fsdp", [(i, i ^ 1) for i in range(8)])

    def over_outer(self, array, step):
        return lax.ppermute(array, "fsdp", [(i, i ^ (2 * step)) for i in range(8)])

    def over_ctx(self, array):
        return lax.ppermute(array, "ctx", [(0, 1), (1, 0)])

    def over_tp(self, array):
        return lax.ppermute(array, "tp", [(0, 1), (1, 0)])

    def tp_sum(self, partial):
        low = partial.astype(bf16)
        return low.astype(f32) + self.over_tp(low).astype(f32)


def pack_early(grid, weights, vectors, tables):
    rows = weights[0].shape[0]
    edges = [sum(w.shape[1] for w in weights[:i]) for i in range(len(weights) + 1)]
    cols = edges[-1] + LANES
    count = len(weights)

    def body(place, *refs):
        out, half_out, lines = refs[-3:]
        for ref, low, high in zip(refs, edges, edges[1:]):
            out[:, low:high] = ref[...]
        lines[...] = jnp.zeros_like(lines)
        at = 0
        for ref in refs[count:-3]:
            height, width = ref.shape
            lines[at : at + height, :width] = ref[...].astype(f32)
            at += height
        out[:, edges[-1] :] = lines[...].astype(bf16)
        half_out[...] = out[pl.ds(pl.multiple_of(place[2] * (rows // 2), 16), rows // 2), :]

    vmem = pl.BlockSpec(memory_space=pltpu.VMEM)
    args = [*weights, *vectors, *tables]
    outs = [like((rows, cols), bf16), like((rows // 2, cols), bf16)]
    return pl.pallas_call(
        body,
        out_shape=outs,
        in_specs=[pl.BlockSpec(memory_space=pltpu.SMEM)] + [vmem] * len(args),
        out_specs=[vmem] * 2,
        scratch_shapes=[pltpu.VMEM((rows, LANES), f32)],
        cost_estimate=cost(0, *args, *outs),
        name="pack_early",
    )(grid.place, *args)


def pack_late(grid, shard, late):
    rows, head = shard.shape
    cols = sum(w.shape[1] for w in late)

    def body(place, early_ref, *refs):
        out, half_out = refs[-2:]
        out[:, :head] = early_ref[...]
        here = pl.ds(pl.multiple_of(place[2] * (rows // 2), 16), rows // 2)
        low = 0
        for ref in refs[:-2]:
            high = low + ref.shape[1]
            out[:, head + low : head + high] = ref[...]
            half_out[:, low:high] = ref[here, :]
            low = high

    vmem = pl.BlockSpec(memory_space=pltpu.VMEM)
    outs = [like((rows, head + cols), bf16), like((rows // 2, cols), bf16)]
    return pl.pallas_call(
        body,
        out_shape=outs,
        in_specs=[pl.BlockSpec(memory_space=pltpu.SMEM)] + [vmem] * (1 + len(late)),
        out_specs=[vmem] * 2,
        cost_estimate=cost(0, shard, *late, *outs),
        name="pack_late",
    )(grid.place, shard, *late)


def join(pieces):
    height, cols = pieces[0].shape

    def body(*refs):
        for i, ref in enumerate(refs[:-1]):
            refs[-1][i * height : (i + 1) * height, :] = ref[...]

    vmem = pl.BlockSpec(memory_space=pltpu.VMEM)
    out = like((len(pieces) * height, cols), pieces[0].dtype)
    return pl.pallas_call(
        body,
        out_shape=out,
        in_specs=[vmem] * len(pieces),
        out_specs=vmem,
        cost_estimate=cost(0, out, out),
        name="join",
    )(*pieces)


def assemble(grid, cuts, base, own, side, came, across, along):
    full = own.shape[0]
    half = full // 2
    edges = [sum(cuts[:i]) for i in range(len(cuts) + 1)]

    def body(place, own_ref, side_ref, came_ref, across_ref, along_ref, *outs):
        outer, inner, row = place[0], place[1], place[2]

        def put(ref, start, length, step, swap_inner, swap_row, skip=0):
            at = (outer ^ step) * 2 + (inner ^ swap_inner)
            if length == half:
                at = at * 2 + (row ^ swap_row)
            here = pl.ds(pl.multiple_of(at * length, 16), length)
            for out, low, high in zip(outs, edges, edges[1:]):
                out[here, :] = ref[start : start + length, skip + low : skip + high]

        put(own_ref, 0, full, 0, 0, 0, base)
        put(side_ref, 0, full, 0, 1, 0, base)
        for step in (1, 2, 3):
            start = (step - 1) * half
            put(came_ref, start, half, step, 0, 0)
            put(across_ref, start, half, step, 1, 0)
            put(along_ref, start, half, step, 0, 1)
            for out in outs:
                at = (((outer ^ step) * 2 + (inner ^ 1)) * 2 + (row ^ 1)) * half
                out[pl.ds(pl.multiple_of(at, 16), half), :] = jnp.zeros((half, out.shape[1]), bf16)

    vmem = pl.BlockSpec(memory_space=pltpu.VMEM)
    outs = [like((8 * full, cols), own.dtype) for cols in cuts]
    return pl.pallas_call(
        body,
        out_shape=outs,
        in_specs=[pl.BlockSpec(memory_space=pltpu.SMEM)] + [vmem] * 5,
        out_specs=[vmem] * len(outs),
        compiler_params=pltpu.CompilerParams(vmem_limit_bytes=VMEM_LIMIT),
        cost_estimate=cost(0, *outs, *outs),
        name="assemble",
    )(grid.place, own, side, came, across, along)


def complete(grid, arrays, far_one, far_two):
    half = far_one.shape[0] // 3
    first = 0
    while sum(a.shape[1] for a in arrays[: first + 1]) <= far_one.shape[1]:
        first += 1
    count = len(arrays)
    copies = 3 * count

    def body(place, one_ref, two_ref, *refs):
        outs, sems = refs[count : 2 * count], refs[2 * count]
        outer, inner, row = place[0], place[1], place[2]
        started = []
        low = 0
        for i, out in enumerate(outs):
            ref = one_ref if i < first else two_ref
            if i == first:
                low = 0
            cols = out.shape[1]
            for step in (1, 2, 3):
                at = (((outer ^ step) * 2 + (inner ^ 1)) * 2 + (row ^ 1)) * half
                copy = pltpu.make_async_copy(
                    ref.at[(step - 1) * half : step * half, low : low + cols],
                    out.at[pl.ds(pl.multiple_of(at, 16), half), :],
                    sems.at[len(started)],
                )
                copy.start()
                started.append(copy)
            low += cols
        for copy in started:
            copy.wait()

    vmem = pl.BlockSpec(memory_space=pltpu.VMEM)
    anywhere = pl.BlockSpec(memory_space=pl.ANY)
    return pl.pallas_call(
        body,
        out_shape=[like(a.shape, a.dtype) for a in arrays],
        in_specs=[pl.BlockSpec(memory_space=pltpu.SMEM), vmem, vmem] + [anywhere] * count,
        out_specs=[anywhere] * count,
        scratch_shapes=[pltpu.SemaphoreType.DMA((copies,))],
        input_output_aliases={3 + i: i for i in range(count)},
        cost_estimate=cost(0, far_one, far_two, far_one, far_two),
        name="complete",
    )(grid.place, far_one, far_two, *arrays)


def lines_of(grid, mine):
    return [grid.over_outer(mine, step) for step in (1, 2, 3)]


def pairs_of(grid, came):
    return grid.over_inner(came), grid.over_ctx(came)


def corners_of(grid, across, along, cut):
    return grid.over_ctx(across[:, :cut]), grid.over_inner(along[:, cut:])


def halves_of(across, along):
    rows, cols = across.shape[0], across.shape[1] // 2

    def body(first, second, first_out, second_out):
        first_out[...] = first[...]
        second_out[...] = second[...]

    return pl.pallas_call(
        body,
        grid=(1,),
        out_shape=[like((rows, cols), across.dtype)] * 2,
        in_specs=[pl.BlockSpec((rows, cols), lambda i: (0, 0)), pl.BlockSpec((rows, cols), lambda i: (0, 1))],
        out_specs=[pl.BlockSpec((rows, cols), lambda i: (0, 0))] * 2,
        cost_estimate=cost(0, across, along),
        name="halves_of",
    )(across, along)


def pick(array, at, axis):
    return lax.dynamic_index_in_dim(array, at, axis, keepdims=False)


def add_low(left, right):
    return (left.astype(f32) + right.astype(f32)).astype(bf16)


VMEM_LIMIT = 60 * 1024 * 1024
SMALL_VMEM_LIMIT = 30 * 1024 * 1024


def whole_block(array):
    rank = array.ndim
    return pl.BlockSpec(array.shape, lambda *_: (0,) * rank)


def cost(flops, *arrays, transcendentals=0):
    return pl.CostEstimate(flops=10**13, transcendentals=0, bytes_accessed=1)


def after(values, *earlier):
    return lax.optimization_barrier((values, earlier))[0]


def like(shape, dtype):
    return jax.ShapeDtypeStruct(shape, dtype)


def norm_rows(hidden_in):
    centre = jnp.mean(hidden_in, axis=-1, keepdims=True)
    shifted = hidden_in - centre
    spread = jnp.mean(shifted * shifted, axis=-1, keepdims=True)
    inverse = lax.rsqrt(spread + epsilon)
    return shifted * inverse, inverse


def norm_pull(upstream, normed, inverse, gain):
    scaled = upstream * gain
    mean_one = jnp.mean(scaled, axis=-1, keepdims=True)
    mean_two = jnp.mean(scaled * normed, axis=-1, keepdims=True)
    return inverse * (scaled - mean_one - normed * mean_two)


def column_sums(values):
    return jnp.sum(values, axis=0, keepdims=True)


def row_tile(rows):
    return 256 if rows % 256 == 0 else rows


def first_norm(prompt, conts, part, other, output_add, gain, shift):
    prompt_len, width = prompt.shape
    rows = prompt_len + conts.shape[0]
    tile = row_tile(prompt_len)
    ahead = prompt_len // tile

    def body(x, c, p, o, b, g, s, norm_out, inv_out, low_out):
        rows_in = jnp.where(pl.program_id(0) < ahead, x[...].astype(f32), c[...].astype(f32))
        normed, inverse = norm_rows(rows_in + (p[...].astype(f32) + o[...].astype(f32)) + b[...])
        norm_out[...] = normed
        inv_out[...] = jnp.broadcast_to(inverse, inv_out.shape)
        low_out[...] = (normed * g[...] + s[...]).astype(bf16)

    def tiled(array):
        return pl.BlockSpec((tile, array.shape[1]), lambda i: (i, 0))

    args = [prompt, conts, part, other, output_add, gain, shift]
    outs = [
        like((rows, width), f32),
        like((rows, LANES), f32),
        like((rows, width), bf16),
    ]
    return pl.pallas_call(
        body,
        grid=(rows // tile,),
        out_shape=outs,
        in_specs=[
            pl.BlockSpec((tile, width), lambda i: (jnp.minimum(i, ahead - 1), 0)),
            pl.BlockSpec((tile, width), lambda i: (jnp.maximum(i - ahead, 0), 0)),
        ]
        + [tiled(a) for a in args[2:4]]
        + [whole_block(a) for a in args[4:]],
        out_specs=[tiled(a) for a in outs],
        compiler_params=pltpu.CompilerParams(vmem_limit_bytes=SMALL_VMEM_LIMIT),
        cost_estimate=cost(0, *args, *outs),
        name="first_norm",
    )(*args)


def turn(array):
    rows, cols = array.shape
    tile = row_tile(rows)

    def body(x, out):
        out[...] = x[...].astype(f32).T.astype(bf16)

    return pl.pallas_call(
        body,
        grid=(rows // tile,),
        out_shape=like((cols, rows), bf16),
        in_specs=[pl.BlockSpec((tile, cols), lambda i: (i, 0))],
        out_specs=pl.BlockSpec((cols, tile), lambda i: (0, i)),
        compiler_params=pltpu.CompilerParams(vmem_limit_bytes=SMALL_VMEM_LIMIT),
        cost_estimate=cost(0, array),
        name="turn",
    )(array)


def ffn_forward(low, up_mat, up_add, down_turned):
    rows, width = low.shape
    hidden = up_mat.shape[1]
    tile = row_tile(rows)

    def body(x, up, ub, dn, act_out, slope_out, part_out):
        inner = product(x[...], up[...]) + ub[...]
        normal_cdf = 0.5 * (1.0 + lax.erf(inner * math.sqrt(0.5)))
        act = (inner * normal_cdf).astype(bf16)
        act_out[...] = act
        density = jnp.exp(-0.5 * inner * inner) * (1.0 / math.sqrt(2.0 * math.pi))
        slope_out[...] = (normal_cdf + inner * density).astype(bf16)
        part_out[...] = contract_cols(act, dn[...]).astype(bf16)

    outs = [
        like((rows, hidden), bf16),
        like((rows, hidden), bf16),
        like((rows, width), bf16),
    ]

    def tiled(array):
        return pl.BlockSpec((tile, array.shape[1]), lambda i: (i, 0))

    args = [low, up_mat, up_add, down_turned]
    return pl.pallas_call(
        body,
        grid=(rows // tile,),
        out_shape=outs,
        in_specs=[tiled(low)] + [whole_block(a) for a in args[1:]],
        out_specs=[tiled(a) for a in outs],
        compiler_params=pltpu.CompilerParams(vmem_limit_bytes=SMALL_VMEM_LIMIT),
        cost_estimate=cost(4 * rows * width * hidden, *args, *outs, transcendentals=2 * rows * hidden),
        name="ffn_forward",
    )(*args)


def split_out(grid, length, cols):
    if grid.staged:
        return [like((length // 2, cols), bf16), like((length // 2, cols), bf16)]
    return [like((length, cols), bf16)]


def store_split(grid, place, full_ref, outs, over_inner):
    if not grid.staged:
        outs[0][...] = full_ref[...]
        return
    half = full_ref.shape[0] // 16
    for out, flip in zip(outs, (0, 1)):
        if over_inner:
            for outer in range(4):
                at = pl.multiple_of((2 * outer + (place[1] ^ flip)) * (2 * half), 32)
                out[2 * half * outer : 2 * half * (outer + 1), :] = full_ref[pl.ds(at, 2 * half), :]
        else:
            for block in range(8):
                at = pl.multiple_of((2 * block + (place[2] ^ flip)) * half, 16)
                out[half * block : half * (block + 1), :] = full_ref[pl.ds(at, half), :]


def ffn_backward(grid, norm1, turned1, gain1, shift1, part, other, down_add, gain2, shift2, cots, act, slope, up_mat, down_turned):
    rows, width = norm1.shape
    hidden = up_mat.shape[1]
    tile = 256
    chunk = row_tile(rows)
    prompt_len = cots[0].shape[0]
    count = 2 if grid.staged else 1

    def body(place, n1, x1_t, g1, s1, p, o, db, g2, s2, cp, cc, u, sl, up, dn, *rest):
        outs, scratch = rest[:-5], rest[-5:]
        y_p, y_c, dh2, dx1, sums, up_sum = outs[:6]
        up_outs, down_outs = outs[6 : 6 + count], outs[6 + count :]
        df, df_t, acc, full_up, full_down = scratch
        step = pl.program_id(0)

        @pl.when(step == 0)
        def _():
            total = [jnp.zeros((1, width), f32) for _ in range(3)]
            for at in range(0, rows, chunk):
                here = slice(at, at + chunk)
                first = n1[here, :] * g1[...] + s1[...]
                second = first + (p[here, :].astype(f32) + o[here, :].astype(f32)) + db[...]
                normed, inverse = norm_rows(second)
                result = (normed * g2[...] + s2[...]).astype(bf16)
                if at < prompt_len:
                    y_p[here, :] = result
                    cot = cp[here, :].astype(f32)
                else:
                    there = slice(at - prompt_len, at - prompt_len + chunk)
                    y_c[there, :] = result
                    cot = cc[there, :].astype(f32)
                grad = norm_pull(cot, normed, inverse, g2[...])
                dh2[here, :] = grad
                low = grad.astype(bf16)
                df[here, :] = low
                wide = low.astype(f32)
                df_t[:, here] = wide.T.astype(bf16)
                total[0] += column_sums(cot * normed)
                total[1] += column_sums(cot)
                total[2] += column_sums(wide)
            sums[...] = jnp.zeros(sums.shape, f32)
            for i in range(3):
                sums[i : i + 1, :] = total[i]
            acc[...] = jnp.zeros_like(acc)

        inner = (product(df[...], dn[...]) * sl[...].astype(f32)).astype(bf16)
        up_sum[...] = jnp.broadcast_to(column_sums(inner.astype(f32)), up_sum.shape)
        full_up[...] = product(x1_t[...], inner).astype(bf16)
        full_down[...] = product(df_t[...], u[...]).astype(bf16)
        acc[...] += contract_cols(inner, up[...])
        store_split(grid, place, full_up, up_outs, True)
        store_split(grid, place, full_down, down_outs, False)

        @pl.when(step == hidden // tile - 1)
        def _():
            dx1[...] = acc[...].astype(bf16)

    def tiled(array):
        return pl.BlockSpec((array.shape[0], tile), lambda j: (0, j))

    fixed = [norm1, turned1, gain1, shift1, part, other, down_add, gain2, shift2, *cots]
    moving = [act, slope, up_mat, down_turned]
    outs = [
        like((prompt_len, width), bf16),
        like((rows - prompt_len, width), bf16),
        like((rows, width), f32),
        like((rows, width), bf16),
        like((8, width), f32),
        like((8, hidden), f32),
    ]
    grads = split_out(grid, width, hidden) * 2
    return pl.pallas_call(
        body,
        grid=(hidden // tile,),
        out_shape=outs + grads,
        in_specs=[pl.BlockSpec(memory_space=pltpu.SMEM)]
        + [whole_block(a) for a in fixed]
        + [tiled(a) for a in moving],
        out_specs=[whole_block(a) for a in outs[:5]] + [tiled(a) for a in outs[5:] + grads],
        scratch_shapes=[
            pltpu.VMEM((rows, width), bf16),
            pltpu.VMEM((width, rows), bf16),
            pltpu.VMEM((rows, width), f32),
            pltpu.VMEM((width, tile), bf16),
            pltpu.VMEM((width, tile), bf16),
        ],
        compiler_params=pltpu.CompilerParams(vmem_limit_bytes=VMEM_LIMIT),
        cost_estimate=cost(8 * rows * width * hidden, *fixed, *moving, *outs, *grads),
        name="ffn_backward",
    )(grid.place, *fixed, *moving)


def fold_pair(grid, firsts, seconds):
    half = firsts[0][0].shape[0] // 8
    outs = []
    for group in (firsts, seconds):
        outs += [like((4 * half, sum(kept.shape[1] for kept, _ in group)), bf16)] * 2

    vmem = pl.BlockSpec(memory_space=pltpu.VMEM)

    def body(place, *refs):
        pairs, outs = refs[:-4], refs[-4:]
        at_pair = 0
        for group, mine, (keep, send) in (
            (firsts, place[2], outs[:2]),
            (seconds, place[1], outs[2:]),
        ):
            low = 0
            for _ in group:
                kept, came = pairs[at_pair : at_pair + 2]
                at_pair += 2
                high = low + kept.shape[1]
                for out, flip in ((send, 1), (keep, 0)):
                    for outer in range(4):
                        here = pl.ds(pl.multiple_of((2 * outer + (mine ^ flip)) * half, 16), half)
                        out[outer * half : (outer + 1) * half, low:high] = (
                            kept[here, :].astype(f32) + came[here, :].astype(f32)
                        ).astype(bf16)
                low = high

    args = [a for group in (firsts, seconds) for pair in group for a in pair]
    return pl.pallas_call(
        body,
        out_shape=outs,
        in_specs=[pl.BlockSpec(memory_space=pltpu.SMEM)] + [vmem] * len(args),
        out_specs=[vmem] * 4,
        compiler_params=pltpu.CompilerParams(vmem_limit_bytes=VMEM_LIMIT),
        cost_estimate=cost(0, *args, *outs),
        name="fold_pair",
    )(grid.place, *args)


def fold_line(grid, first, second):
    half = first[0].shape[0] // 4
    left, right = first[0].shape[1], second[0].shape[1]
    outs = [like((half, left + right), f32)] + [like((half, left + right), bf16)] * 3

    def body(place, fk, fa, sk, sa, *out_refs):
        for step, out in enumerate(out_refs):
            here = pl.ds(pl.multiple_of((place[0] ^ step) * half, 16), half)
            out[:, :left] = (fk[here, :].astype(f32) + fa[here, :].astype(f32)).astype(out.dtype)
            out[:, left:] = (sk[here, :].astype(f32) + sa[here, :].astype(f32)).astype(out.dtype)

    vmem = pl.BlockSpec(memory_space=pltpu.VMEM)
    args = [*first, *second]
    return pl.pallas_call(
        body,
        out_shape=outs,
        in_specs=[pl.BlockSpec(memory_space=pltpu.SMEM)] + [vmem] * 4,
        out_specs=[vmem] * 4,
        cost_estimate=cost(0, *args, *outs),
        name="fold_line",
    )(grid.place, *args)


class Reduction:
    def __init__(self, grid, firsts, seconds):
        self.grid, self.firsts, self.seconds = grid, firsts, seconds
        if grid.staged:
            self.came = [
                [grid.over_inner(g[1]) for g in firsts],
                [grid.over_ctx(g[1]) for g in seconds],
            ]

    def fold(self, *earlier):
        if not self.grid.staged:
            return ()
        grid = self.grid
        came = after(self.came, *earlier)
        folded = fold_pair(
            grid,
            [(g[0], c) for g, c in zip(self.firsts, came[0])],
            [(g[0], c) for g, c in zip(self.seconds, came[1])],
        )
        f_keep, f_send, s_keep, s_send = folded
        self.kept = f_keep, s_keep
        self.came = grid.over_ctx(f_send), grid.over_inner(s_send)
        return folded

    def line(self, *earlier):
        if not self.grid.staged:
            return ()
        came = after(self.came, *earlier)
        self.total, *sent = fold_line(self.grid, (self.kept[0], came[0]), (self.kept[1], came[1]))
        self.came = [self.grid.over_outer(sent[step - 1], step) for step in (1, 2, 3)]
        return sent

    def shard(self, *earlier, beside=()):
        grid = self.grid
        if not grid.staged:
            both = jnp.concatenate([g[0] for g in self.firsts + self.seconds], 1)
            both = lax.psum_scatter(both, "fsdp", scatter_dimension=0, tiled=True)
            return lax.psum(both, "ctx").astype(f32)
        came = after(self.came, *earlier)
        total = self.total
        for piece in came:
            total = total + piece.astype(f32)
        total = total.astype(bf16)
        other = after(grid.over_ctx(total), *beside)
        low = jnp.where(grid.row == 0, total, other)
        high = jnp.where(grid.row == 0, other, total)
        return jnp.concatenate([low, high], 0).astype(f32)


def columns_of(shard, widths):
    edges = [sum(widths[:i]) for i in range(len(widths) + 1)]
    return [shard[:, low:high] for low, high in zip(edges, edges[1:])]


def head_lanes(shape, index):
    lane = lax.broadcasted_iota(jnp.int32, shape, 1)
    return (lane < LANES // 2) if index == 0 else (lane >= LANES // 2)


def each_chunk(rows_at, prompt_len, rows, chunk):
    @pl.loop(0, prompt_len // chunk)
    def _(i):
        rows_at(pl.multiple_of(i * chunk, chunk), True)

    for at in range(prompt_len, rows, chunk):
        rows_at(at, False)


def attention_forward(queries, keys, values, prev_logits, cont_len, prompt_len, pairs, held=()):
    begin, end = pairs
    kept = len(held)
    rows, width = queries.shape
    total = keys.shape[0]
    cont_size = rows - prompt_len
    full_len = total - cont_size
    heads = prev_logits.shape[0]
    chunk = row_tile(prompt_len)

    def body(length, q, k, v, prev, *refs):
        logits, probs_p, probs_c, out = refs[kept:]

        def soft(scores):
            weights = jnp.exp(scores - jnp.max(scores, axis=-1, keepdims=True))
            return (weights * (1.0 / jnp.sum(weights, axis=-1, keepdims=True))).astype(bf16)

        column = lax.broadcasted_iota(jnp.int32, (1, total), 1)
        live = column < full_len + length[0, 0]
        def rows_at(at, in_prompt):
            here = pl.ds(at, chunk)
            halves = []
            for head in range(2):
                one = jnp.where(head_lanes((chunk, LANES), head), q[here, :], 0)
                if in_prompt:
                    probs = soft(contract_cols(one, k[:full_len, :]))
                    probs_p[head, here, :] = probs
                    halves.append(product(probs, v[:full_len, :]))
                else:
                    there = slice(at - prompt_len, at - prompt_len + chunk)
                    raw = prev[head, there, :].astype(f32) + contract_cols(one, k[...])
                    logits[head, there, :] = raw.astype(bf16)
                    probs = soft(jnp.where(live, raw, -1e30))
                    probs_c[head, there, :] = probs
                    halves.append(product(probs, v[...]))
            first = head_lanes((chunk, LANES), 0)
            out[here, :] = jnp.where(first, halves[0], halves[1]).astype(bf16)

        each_chunk(rows_at, prompt_len, rows, chunk)

    outs = [
        like((heads, cont_size, total), bf16),
        like((heads, prompt_len, full_len), bf16),
        like((heads, cont_size, total), bf16),
        like((rows, width), bf16),
    ]

    def columns(array):
        return pl.BlockSpec((array.shape[0], LANES), lambda i: (0, begin + i))

    def pair_of(array):
        return pl.BlockSpec((2,) + array.shape[1:], lambda i: (begin + i, 0, 0))

    args = [queries, keys, values, prev_logits]
    scores = heads * (prompt_len * full_len + cont_size * total)
    return pl.pallas_call(
        body,
        grid=(end - begin,),
        out_shape=outs,
        in_specs=[pl.BlockSpec(memory_space=pltpu.SMEM)]
        + [columns(a) for a in args[:3]]
        + [pair_of(prev_logits)]
        + [pl.BlockSpec(memory_space=pl.ANY)] * kept,
        out_specs=[pair_of(a) for a in outs[:3]] + [columns(outs[3])],
        compiler_params=pltpu.CompilerParams(vmem_limit_bytes=VMEM_LIMIT),
        input_output_aliases={5 + i: i for i in range(kept)},
        cost_estimate=cost((end - begin) * 256 * scores, *args, transcendentals=scores),
        name="attention_forward",
    )(cont_len, *args, *held)


def attention_backward(queries, keys, values, dout, attended, probs_p, probs_c, cots, scale):
    rows, width = queries.shape
    total = keys.shape[0]
    heads, prompt_len, full_len = probs_p.shape
    cont_size = rows - prompt_len
    chunk = row_tile(prompt_len)

    def body(q, k, v, do, o, pp, pc, cot, prev_out, dq, dk, dv, acc_k, acc_v):
        acc_k[...] = jnp.zeros_like(acc_k)
        acc_v[...] = jnp.zeros_like(acc_v)
        def rows_at(at, in_prompt):
            here = pl.ds(at, chunk)
            grads = []
            for head in range(2):
                mine = head_lanes((chunk, LANES), head)
                one_q = jnp.where(mine, q[here, :], 0)
                one_do = jnp.where(mine, do[here, :], 0)
                delta = jnp.sum(
                    one_do.astype(f32) * o[here, :].astype(f32), axis=-1, keepdims=True
                )
                if in_prompt:
                    span = full_len
                    probs = pp[head, here, :]
                    dprob = contract_cols(one_do, v[:span, :])
                    dscore = (probs.astype(f32) * (dprob - delta)).astype(bf16)
                else:
                    span = total
                    there = slice(at - prompt_len, at - prompt_len + chunk)
                    probs = pc[head, there, :]
                    dprob = contract_cols(one_do, v[...])
                    dscore = (
                        probs.astype(f32) * (dprob - delta) + cot[head, there, :].astype(f32)
                    ).astype(bf16)
                    prev_out[head, there, :] = dscore
                grads.append(product(dscore, k[:span, :]))
                acc_k[:span, :] += contract_rows(dscore, one_q)
                acc_v[:span, :] += contract_rows(probs, one_do)
            first = head_lanes((chunk, LANES), 0)
            dq[here, :] = (jnp.where(first, grads[0], grads[1]) * scale).astype(bf16)

        each_chunk(rows_at, prompt_len, rows, chunk)
        dk[...] = acc_k[...].astype(bf16)
        dv[...] = acc_v[...].astype(bf16)

    outs = [
        like((heads, cont_size, total), bf16),
        like((rows, width), bf16),
        like((total, width), bf16),
        like((total, width), bf16),
    ]

    def columns(array):
        return pl.BlockSpec((array.shape[0], LANES), lambda i: (0, i))

    def pairs(array):
        return pl.BlockSpec((2,) + array.shape[1:], lambda i: (i, 0, 0))

    args = [queries, keys, values, dout, attended, probs_p, probs_c, cots]
    scores = heads * (prompt_len * full_len + cont_size * total)
    return pl.pallas_call(
        body,
        grid=(heads // 2,),
        out_shape=outs,
        in_specs=[columns(a) for a in args[:5]] + [pairs(a) for a in args[5:]],
        out_specs=[pairs(outs[0])] + [columns(a) for a in outs[1:]],
        scratch_shapes=[pltpu.VMEM((total, LANES), f32), pltpu.VMEM((total, LANES), f32)],
        compiler_params=pltpu.CompilerParams(vmem_limit_bytes=VMEM_LIMIT),
        cost_estimate=cost(1024 * scores, *args, *outs),
        name="attention_backward",
    )(*args)


def first_norm_backward(grad_second, part, other, norm1, inv1, gain1, output_turned):
    rows, width = grad_second.shape
    tile = row_tile(rows)

    def body(d2, p, o, n1, r1, g1, ot, dh1, dout, sums):
        @pl.when(pl.program_id(0) == 0)
        def _():
            sums[...] = jnp.zeros_like(sums)

        upstream = d2[...] + (p[...].astype(f32) + o[...].astype(f32))
        normed = n1[...]
        grad = norm_pull(upstream, normed, r1[:, :1], g1[...])
        dh1[...] = grad
        low = grad.astype(bf16)
        dout[...] = product(low, ot[...]).astype(bf16)
        sums[0:1, :] += column_sums(upstream * normed)
        sums[1:2, :] += column_sums(upstream)
        sums[2:3, :] += column_sums(low.astype(f32))

    def tiled(array):
        return pl.BlockSpec((tile, array.shape[1]), lambda i: (i, 0))

    args = [grad_second, part, other, norm1, inv1, gain1, output_turned]
    outs = [
        like((rows, width), f32),
        like((rows, output_turned.shape[1]), bf16),
        like((8, width), f32),
    ]
    return pl.pallas_call(
        body,
        grid=(rows // tile,),
        out_shape=outs,
        in_specs=[tiled(a) for a in args[:5]] + [whole_block(a) for a in args[5:]],
        out_specs=[tiled(a) for a in outs[:2]] + [whole_block(outs[2])],
        compiler_params=pltpu.CompilerParams(vmem_limit_bytes=VMEM_LIMIT),
        cost_estimate=cost(2 * rows * width * output_turned.shape[1], *args, *outs),
        name="first_norm_backward",
    )(*args)


def input_pull(grid, dq, dk, dv, query_mat, key_mat, value_mat, prompt_len):
    rows, width = dq.shape[0], query_mat.shape[0]
    half = prompt_len // 2
    tile = half
    full_len = 2 * prompt_len

    def body(place, q, k, v, qm, km, vm, own, keep, low):
        def pull(at):
            here = pl.ds(pl.multiple_of(at, tile), tile)
            return contract_cols(k[here, :], km[...]) + contract_cols(v[here, :], vm[...])

        for at in range(0, rows, tile):
            source = place[2] * prompt_len + at if at < prompt_len else at - prompt_len + full_len
            value = contract_cols(q[at : at + tile, :], qm[...]) + pull(source)
            own[at : at + tile, :] = value
            low[at : at + tile, :] = value.astype(bf16)
        abroad = (1 - place[2]) * prompt_len
        keep[...] = pull(abroad + place[3] * half).astype(bf16)
        low[rows:, :] = pull(abroad + (1 - place[3]) * half).astype(bf16)

    args = [dq, dk, dv, query_mat, key_mat, value_mat]
    vmem = pl.BlockSpec(memory_space=pltpu.VMEM)
    return pl.pallas_call(
        body,
        out_shape=[like((rows, width), f32), like((half, width), bf16), like((rows + half, width), bf16)],
        in_specs=[pl.BlockSpec(memory_space=pltpu.SMEM)] + [vmem] * len(args),
        out_specs=[vmem] * 3,
        compiler_params=pltpu.CompilerParams(vmem_limit_bytes=VMEM_LIMIT),
        cost_estimate=cost(0, *args),
        name="input_pull",
    )(grid.place, *args)


def weight_grads(grid, shards, grad_first, attended, inputs_t, whole_t, dq, dk, dv, sums1, sums2, up_sum):
    width, part = inputs_t.shape[0], dq.shape[1]
    hidden = up_sum.shape[1]
    count = 2 if grid.staged else 1
    block = width // shards
    sides = pl.cdiv((6 * width + 2 * part + hidden) // LANES, block)
    extra = sides * LANES
    widths = [part, part, part, part, extra]

    def body(place, d1, o, xt, wt, q, k, v, s1, s2, us, *rest):
        firsts, seconds = rest[:count], rest[count : 2 * count]
        full_a, full_b = rest[2 * count :]
        turned = d1[...].T.astype(bf16)
        full_a[:, :part] = product(turned, o[...]).astype(bf16)
        full_a[:, part:] = product(xt[...], q[...]).astype(bf16)
        full_b[:, :part] = product(wt[...], k[...]).astype(bf16)
        wide = 2 * part
        full_b[:, part:wide] = product(wt[...], v[...]).astype(bf16)
        lines = [(s1, i) for i in range(3)] + [(s2, i) for i in range(3)]
        pieces = []
        for ref, i in lines:
            pieces += [ref[i : i + 1, at : at + LANES] for at in range(0, width, LANES)]
        for sums in (column_sums(q[...].astype(f32)), column_sums(v[...].astype(f32))):
            pieces += [sums[:, at : at + LANES] for at in range(0, part, LANES)]
        pieces += [us[0:1, at : at + LANES] for at in range(0, hidden, LANES)]
        pieces.append(jnp.zeros((sides * block - len(pieces), LANES), f32))
        table = jnp.concatenate(pieces, 0).astype(bf16)
        for shard in range(shards):
            for side in range(sides):
                low = wide + side * LANES
                full_b[shard * block : (shard + 1) * block, low : low + LANES] = table[
                    side * block : (side + 1) * block
                ]
        store_split(grid, place, full_a, firsts, True)
        store_split(grid, place, full_b, seconds, False)

    args = [grad_first, attended, inputs_t, whole_t, dq, dk, dv, sums1, sums2, up_sum]
    outs = split_out(grid, width, 2 * part) + split_out(grid, width, sum(widths[2:]))
    vmem = pl.BlockSpec(memory_space=pltpu.VMEM)
    outs = pl.pallas_call(
        body,
        out_shape=outs,
        in_specs=[pl.BlockSpec(memory_space=pltpu.SMEM)] + [vmem] * len(args),
        out_specs=[vmem] * len(outs),
        scratch_shapes=[
            pltpu.VMEM((width, 2 * part), bf16),
            pltpu.VMEM((width, sum(widths[2:])), bf16),
        ],
        compiler_params=pltpu.CompilerParams(vmem_limit_bytes=VMEM_LIMIT),
        cost_estimate=cost(0, *args, *outs),
        name="weight_grads",
    )(grid.place, *args)
    return outs[:count], outs[count:], widths


def unpack_small(grid, packed, heads, head_size, up_rows):
    width = packed.shape[0]
    shards = grid.fsdp
    block, per_head, per_up = width // shards, head_size // shards, LANES // shards

    def body(packed_ref, *refs):
        lines, (query_out, value_out, up_out) = refs[:6], refs[6:]
        source = lax.broadcasted_iota(jnp.int32, (LANES, width), 0)
        target = lax.broadcasted_iota(jnp.int32, (LANES, width), 1)
        whole = jnp.zeros((32, width), f32)
        by_head = jnp.zeros((32, LANES), f32)
        by_up = jnp.zeros((32, LANES), f32)
        near, far = source[:, :LANES], target[:, :LANES]
        for shard in range(shards):
            piece = packed_ref[shard * block : shard * block + 32, :]
            put = (target - source == shard * block) & (source < block)
            whole += product(piece, put.astype(bf16))
            place = shard * per_head
            shift = far - near
            put = ((shift == place) | (shift == place + head_size)) & (near < per_head)
            by_head += product(piece, put.astype(bf16))
            put = (shift == shard * per_up) & (near < per_up)
            by_up += product(piece, put.astype(bf16))
        for i, out in enumerate(lines):
            out[...] = whole[i : i + 1, :]
        low = lax.broadcasted_iota(jnp.int32, (1, LANES), 1) < head_size
        for pair in range(heads // 2):
            at = slice(pair * LANES, (pair + 1) * LANES)
            for out, base in ((query_out, 6), (value_out, 6 + heads)):
                row = base + 2 * pair
                out[:, at] = jnp.where(low, by_head[row : row + 1, :], by_head[row + 1 : row + 2, :])
        for i in range(up_rows):
            row = 6 + 2 * heads + i
            up_out[:, i * LANES : (i + 1) * LANES] = by_up[row : row + 1, :]

    outs = [like((1, width), f32)] * 6 + [
        like((1, heads * head_size), f32),
        like((1, heads * head_size), f32),
        like((1, up_rows * LANES), f32),
    ]
    vmem = pl.BlockSpec(memory_space=pltpu.VMEM)
    return pl.pallas_call(
        body,
        out_shape=outs,
        in_specs=[vmem],
        out_specs=[vmem] * 9,
        cost_estimate=cost(0, packed, *outs),
        name="unpack_small",
    )(packed)


def per_device(
    sizes,
    prompt,
    continuations,
    prev_logits,
    cont_len,
    query_weight,
    query_bias,
    key_weight,
    value_weight,
    value_bias,
    output_weight,
    output_bias,
    first_gain,
    first_shift,
    up_weight,
    up_bias,
    down_weight,
    down_bias,
    second_gain,
    second_shift,
    cot_prompt,
    cot_conts,
    cot_logits,
):
    grid = Grid(sizes)
    rows = query_weight.shape[0]
    width = query_weight.shape[1]
    hidden = up_weight.shape[1]
    prompt_len = prompt.shape[1]
    cont_size = continuations.shape[2]
    head_count = query_bias.shape[0]
    head_size = width // head_count
    scale = 1.0 / math.sqrt(head_size)

    mine, conts = prompt[0], continuations[0, 0]
    lines = [v[None] for v in (output_bias, first_gain, first_shift, down_bias, second_gain, second_shift)]
    tables = [query_bias, value_bias, up_bias]
    early = [query_weight, key_weight, value_weight, output_weight.T]
    late = [up_weight, down_weight.T]
    shard, half_shard = pack_early(grid, early, lines, tables)
    cuts = [width, width, width, width, LANES]
    cut = 2 * width
    if grid.staged:
        came = lines_of(grid, half_shard)
        sent, shard = lax.optimization_barrier((mine, shard))
        theirs = grid.over_ctx(sent)
        shards, late_half = pack_late(grid, shard, late)
        side = grid.over_inner(shards)
        came, late_half, theirs = lax.optimization_barrier((came, late_half, theirs))
        came = join(came)
        across, along = pairs_of(grid, came)
        far = corners_of(grid, across, along, cut)
        late_came = lines_of(grid, late_half)
        early = complete(
            grid, assemble(grid, cuts, 0, shards, side, came, across, along), *far
        )
    else:
        shards = [shard] + late
        shards = [lax.all_gather(a, "fsdp", axis=0, tiled=True) for a in shards]
        edges = [sum(cuts[:i]) for i in range(len(cuts) + 1)]
        early = [shards[0][:, low:high] for low, high in zip(edges, edges[1:])]
        late = shards[1:]
    query_mat, key_mat, value_mat, output_turned, small = early
    *vectors, query_add, value_add, up_line = unpack_small(
        grid, small, head_count, head_size, up_bias.shape[0]
    )
    if grid.staged:
        late_came = join(after(late_came, vectors))
        late_across, late_along = pairs_of(grid, late_came)
        query_mat, key_mat, value_mat = after((query_mat, key_mat, value_mat), late_came)
    output_line, gain1, shift1, down_line, gain2, shift2 = vectors

    inputs = jnp.concatenate([mine, conts], 0)
    if sizes[1] == 2:
        if not grid.staged:
            theirs = grid.over_ctx(mine)
        whole = jnp.concatenate(
            [jnp.where(grid.row == 0, mine, theirs), jnp.where(grid.row == 0, theirs, mine), conts], 0
        )
    else:
        whole = jnp.concatenate([lax.all_gather(mine, "ctx", axis=0, tiled=True), conts], 0)
    full_len = whole.shape[0] - cont_size
    whole_t, inputs_t = whole.T, inputs.T

    queries = ((product(inputs, query_mat) + query_add) * scale).astype(bf16)
    keys = product(whole, key_mat).astype(bf16)
    values = (product(whole, value_mat) + value_add).astype(bf16)
    queries, whole_t, inputs_t = lax.optimization_barrier((queries, whole_t, inputs_t))
    attention = (queries, keys, values, prev_logits[0, 0], cont_len, prompt_len)
    pair_count = head_count // 2
    held = attention_forward(*attention, (0, pair_count - 1))
    if grid.staged:
        late_across, late_along, held = lax.optimization_barrier((late_across, late_along, held))
        first, second = halves_of(late_across, late_along)
        held = after(held, first)
        far = grid.over_ctx(first), grid.over_inner(second)
    new_logits, probs_p, probs_c, attended = attention_forward(
        *attention, (pair_count - 1, pair_count), held
    )
    if grid.staged:
        late = assemble(
            grid, [hidden, hidden], sum(cuts), shards, side, late_came, late_across, late_along
        )
    part = contract_cols(attended, output_turned).astype(bf16)
    norm1, inv1, low1 = first_norm(
        mine, conts, part, grid.over_tp(part), output_line, gain1, shift1
    )
    if grid.staged:
        late = complete(grid, late, *far)
    up_mat, down_turned = late
    activated, slope, part2 = ffn_forward(low1, up_mat, up_line, down_turned)
    turned1 = turn(after(low1, part2))
    results = ffn_backward(
        grid,
        norm1,
        turned1,
        gain1,
        shift1,
        part2,
        grid.over_tp(part2),
        down_line,
        gain2,
        shift2,
        (cot_prompt[0], cot_conts[0, 0]),
        activated,
        slope,
        up_mat,
        down_turned,
    )
    result_prompt, result_cont, grad_second, part3, sums2, up_sum = results[:6]
    splits = results[6:]
    half = len(splits) // 2
    sum_f = Reduction(grid, [splits[:half]], [splits[half:]])
    grad_first, dout, sums1 = first_norm_backward(
        grad_second, part3, grid.over_tp(part3), norm1, inv1, gain1, output_turned
    )
    grad_prev, dq, dk, dv = attention_backward(
        queries, keys, values, dout, attended, probs_p, probs_c, cot_logits[0, 0], scale
    )
    dq = after(dq, sum_f.fold(dq))
    *splits, widths = weight_grads(
        grid, sizes[0], grad_first, attended, inputs_t, whole_t, dq, dk, dv, sums1, sums2, up_sum
    )
    sum_c = Reduction(grid, [splits[0]], [splits[1]])

    if grid.staged:
        folded = sum_c.fold(sum_f.line(splits))
        grads = after((dq, dk, dv), folded)
        partial, keep, low = input_pull(grid, *grads, query_mat, key_mat, value_mat, prompt_len)
        sent = sum_c.line(partial)
        came = grid.over_tp(low)
        own_rows = partial.shape[0]
        input_grad = grad_first + partial.astype(bf16).astype(f32) + came[:own_rows].astype(f32)
        arrived = grid.over_ctx(add_low(keep, came[own_rows:]))
        shard_f = sum_f.shard(folded)
        other = grid.over_tp(arrived)
        first = jnp.where(grid.core == 0, arrived, other)
        second = jnp.where(grid.core == 0, other, arrived)
        grad_cont = input_grad[prompt_len:]
        shared = grad_cont, arrived
        grad_prompt = input_grad[:prompt_len] + jnp.concatenate([first, second], 0).astype(f32)
    else:
        from_query = contract_cols(dq, query_mat)
        from_keyvalue = contract_cols(dk, key_mat) + contract_cols(dv, value_mat)
        own = lax.psum_scatter(
            from_keyvalue[:full_len].astype(bf16), "ctx", scatter_dimension=0, tiled=True
        ).astype(f32)
        own = own + from_query[:prompt_len]
        partial = jnp.concatenate([own, from_keyvalue[full_len:] + from_query[prompt_len:]], 0)
        input_grad = grad_first + grid.tp_sum(partial)
        grad_prompt, grad_cont = input_grad[:prompt_len], input_grad[prompt_len:]
        shard_f = sum_f.shard()
        shared = ()
    up_grad, down_turned_grad = columns_of(shard_f, [hidden, hidden])
    down_grad = down_turned_grad.T
    shard_c = sum_c.shard(up_grad, down_grad, *shared, beside=[grad_prompt])
    output_grads, query_grad, key_grad, value_grad, table = columns_of(shard_c, widths)
    model = whole.shape[1]
    table = jnp.concatenate([table[:, at : at + LANES] for at in range(0, table.shape[1], LANES)], 0)
    place = lax.axis_index("fsdp")
    at = 6 * (model // LANES)
    long_lines = table[:at].reshape(6, model)
    long_lines = lax.dynamic_slice_in_dim(long_lines, place * rows, rows, 1)
    shorts = []
    for bias in (query_bias, value_bias, up_bias):
        height, cols = bias.shape
        span = height * cols * sizes[0] // LANES
        block = table[at : at + span].reshape(height, -1)
        shorts.append(lax.dynamic_slice_in_dim(block, place * cols, cols, 1))
        at += span
    gain_one_grad, shift_one_grad, output_add_grad = long_lines[0], long_lines[1], long_lines[2]
    gain_two_grad, shift_two_grad, down_add_grad = long_lines[3], long_lines[4], long_lines[5]
    return (
        result_prompt[None],
        result_cont[None, None],
        new_logits[None, None],
        grad_prompt[None],
        grad_cont[None, None],
        grad_prev[None, None],
        query_grad,
        shorts[0],
        key_grad,
        value_grad,
        shorts[1],
        output_grads.T,
        output_add_grad,
        gain_one_grad,
        shift_one_grad,
        up_grad,
        shorts[2],
        down_grad,
        down_add_grad,
        gain_two_grad,
        shift_two_grad,
    )


def solution(mesh):
    sizes = tuple(mesh.shape[name] for name in ("fsdp", "ctx", "tp"))

    def step(*arrays):
        return per_device(sizes, *arrays)

    return jax.shard_map(
        step,
        mesh=mesh,
        in_specs=(
            P("fsdp", "ctx", None),
            P("fsdp", "ctx", None, None),
            P("fsdp", "ctx", "tp", None, None),
            P("fsdp", "ctx"),
            P("fsdp", "tp"),
            P("tp", "fsdp"),
            P("fsdp", "tp"),
            P("fsdp", "tp"),
            P("tp", "fsdp"),
            P("tp", "fsdp"),
            P("fsdp"),
            P("fsdp"),
            P("fsdp"),
            P("fsdp", "tp"),
            P("tp", "fsdp"),
            P("tp", "fsdp"),
            P("fsdp"),
            P("fsdp"),
            P("fsdp"),
            P("fsdp", "ctx", None),
            P("fsdp", "ctx", None, None),
            P("fsdp", "ctx", "tp", None, None),
        ),
        out_specs=(
            P("fsdp", "ctx", None),
            P("fsdp", "ctx", None, None),
            P("fsdp", "ctx", "tp", None, None),
            P("fsdp", "ctx", None),
            P("fsdp", "ctx", None, None),
            P("fsdp", "ctx", "tp", None, None),
            P("fsdp", "tp"),
            P("tp", "fsdp"),
            P("fsdp", "tp"),
            P("fsdp", "tp"),
            P("tp", "fsdp"),
            P("tp", "fsdp"),
            P("fsdp"),
            P("fsdp"),
            P("fsdp"),
            P("fsdp", "tp"),
            P("tp", "fsdp"),
            P("tp", "fsdp"),
            P("fsdp"),
            P("fsdp"),
            P("fsdp"),
        ),
        check_vma=False,
    )
```
